768 devices in a mesh: depth: 32 (over y, z_hi), chan: 24 (over x, z_lo, core).
Axes of the slice: x: 4, y: 8, z: 12 (z_hi: 4, z_lo: 3; z = z_hi * 3 + z_lo), core: 2. Of those that a mesh axis runs over, the one named last changes fastest.
Arguments:
- volume: bfloat16 [1, 32, 384, 1024], P(None, 'depth', 'chan'), may hold values from -6 to 6
- kernel: bfloat16 [384, 3, 3, 3, 384], P('chan'), may hold values from -0.09375 to 0.09375
- cotangent: bfloat16 [1, 32, 384, 1024], P(None, 'depth', 'chan'), may hold values from -6 to 6
Outputs:
- activated: bfloat16 [1, 32, 384, 1024], P(None, 'depth', 'chan')
- grad_volume: bfloat16 [1, 32, 384, 1024], P(None, 'depth', 'chan')
- grad_kernel: float32 [384, 3, 3, 3, 384], P('chan')
The draws below stay inside these ranges and needn't reach their ends.
All inputs are finite; a program needn't handle non-finite values.
Results may differ from the reference program's by a relative error of at most 0.0049.
Values may be sent and summed in bfloat16 or wider, within the bound.
No kernel may reach another device: no remote copies, remote signals or barrier semaphores. Data moves between devices by JAX's collectives and lax.ppermute only.
A program may use at most 32 MiB of HBM per device.

```python
import math
import jax
import jax.numpy as jnp
from jax import lax

DEPTH = 32
SIDE = 32
CH = 384
UNIV = 1
CELLS = 1024


def spiked(result, key, source, target, parts, factor):
    def block_of(axis_at):
        return (jnp.arange(result.shape[axis_at]) // (result.shape[axis_at] // parts)).reshape((-1,) + (1,) * (result.ndim - 1 - axis_at))

    one_side = jax.random.permutation(key, parts)[block_of(target)]
    other_side = (block_of(target) + parts // 2) % parts
    return jnp.where((block_of(source) == one_side) | (block_of(source) == other_side), factor * result, result)


def shard_levels(stream_key, shape, shards, low, largest):
    loudness, own = 1.0, jax.random.fold_in(stream_key, 6)
    for axis_at, blocks in shards:
        draws = jnp.exp(jax.random.uniform(jax.random.fold_in(own, axis_at), (blocks,), jnp.float32, low / len(shards), largest / len(shards)))
        loudness = loudness * jnp.repeat(draws, shape[axis_at] // blocks).reshape([-1 if axis == axis_at else 1 for axis in range(len(shape))])
    return loudness


def bell_draw(stream_key, shape, deviation, bound, split=(), dtype=jnp.bfloat16):
    drawn = deviation * jax.random.normal(stream_key, shape, jnp.float32)
    if split:
        drawn = drawn * shard_levels(stream_key, shape, split, -0.22, 0.18)
    return jnp.clip(drawn, -bound, bound).astype(dtype)


def bell_draw_with(key, dims, width, limit, split, heavy, kind=jnp.bfloat16):
    values = width * jax.random.normal(key, dims, jnp.float32)
    if split:
        values = values * shard_levels(key, dims, split, -0.22, 0.18)
    return jnp.clip(spiked(values, jax.random.fold_in(key, 3), *heavy), -limit, limit).astype(kind)


def setup_inputs(seed: int = 0) -> dict:
    keys = jax.random.split(jax.random.key(seed), 4)
    return {
        "volume": bell_draw(keys[0], (UNIV, DEPTH, CH, CELLS), 1.0, 6.0, ((1, 32), (2, 24))),
        "kernel": bell_draw_with(keys[1], (CH, 3, 3, 3, CH), (27 * CH) ** -0.5, 0.09375, ((0, 24),), (0, 4, 24, 2.25)),
        "cotangent": bell_draw(keys[2], (UNIV, DEPTH, CH, CELLS), 1.0, 6.0, ((1, 32), (2, 24))),
    }


def to_boxes(flat):
    return jnp.transpose(flat.reshape(UNIV, DEPTH, CH, SIDE, SIDE), (0, 1, 3, 4, 2))

def from_boxes(boxes):
    return jnp.transpose(boxes, (0, 1, 4, 2, 3)).reshape(UNIV, DEPTH, CH, SIDE * SIDE)

def reference(volume, kernel, cotangent):
    source = to_boxes(volume).astype(jnp.float32)
    cot_boxes = to_boxes(cotangent).astype(jnp.float32)
    weights = kernel.astype(jnp.float32)
    shape_full = source.shape
    preact = jnp.zeros(shape_full, jnp.float32)
    for depth_tap in range(3):
        for row_tap in range(3):
            for col_tap in range(3):
                shifted = jnp.roll(source, (1 - depth_tap, 1 - row_tap, 1 - col_tap), axis=(1, 2, 3))
                tap_weight = weights[:, depth_tap, row_tap, col_tap, :].T
                product = jnp.dot(shifted.reshape(-1, CH), tap_weight, precision=lax.Precision.HIGHEST)
                preact = preact + product.reshape(shape_full)
    activated = jax.nn.silu(preact).astype(jnp.bfloat16)
    sigmoid_pre = jax.nn.sigmoid(preact)
    grad_pre = (cot_boxes * sigmoid_pre * (1.0 + preact * (1.0 - sigmoid_pre))).astype(jnp.bfloat16)
    grad_pre = lax.optimization_barrier(grad_pre).astype(jnp.float32)
    grad_flat = grad_pre.reshape(-1, CH)
    grad_volume = jnp.zeros(shape_full, jnp.float32)
    kernel_terms = []
    for depth_tap in range(3):
        for row_tap in range(3):
            for col_tap in range(3):
                tap_weight = weights[:, depth_tap, row_tap, col_tap, :].T
                moved_grad = jnp.roll(grad_pre, (depth_tap - 1, row_tap - 1, col_tap - 1), axis=(1, 2, 3))
                grad_volume = grad_volume + jnp.dot(moved_grad.reshape(-1, CH), tap_weight.T, precision=lax.Precision.HIGHEST).reshape(shape_full)
                shifted = jnp.roll(source, (1 - depth_tap, 1 - row_tap, 1 - col_tap), axis=(1, 2, 3))
                kernel_terms.append(jnp.dot(shifted.reshape(-1, CH).T, grad_flat, precision=lax.Precision.HIGHEST))
    grad_scale = 1.0 / math.sqrt(UNIV * DEPTH * SIDE * SIDE)
    stacked_terms = jnp.stack(kernel_terms).reshape(3, 3, 3, CH, CH)
    grad_kernel = jnp.transpose(stacked_terms, (4, 0, 1, 2, 3)) * grad_scale
    return (from_boxes(activated), from_boxes(grad_volume.astype(jnp.bfloat16)), grad_kernel)
```

```python
import math

import jax
import jax.numpy as jnp
from jax import lax
from jax.sharding import PartitionSpec as P

DEPTH = 32
SIDE = 32
UNIV = 1
TAPS = 27


def roll_plane(plane_data, row_step, col_step):
    if col_step != 0:
        columns = lax.broadcasted_iota(jnp.int32, plane_data.shape, plane_data.ndim - 1) % SIDE
        edge_col = 0 if col_step > 0 else SIDE - 1
        wrapped = jnp.roll(plane_data, col_step - col_step * SIDE, axis=-1)
        plain = jnp.roll(plane_data, col_step, axis=-1)
        plane_data = jnp.where(columns == edge_col, wrapped, plain)
    if row_step != 0:
        plane_data = jnp.roll(plane_data, row_step * SIDE, axis=-1)
    return plane_data


def spread(block, axis):
    count = lax.axis_size(axis)
    return lax.all_to_all(jnp.broadcast_to(block[None], (count,) + block.shape), axis, 0, 0)


def rolled_sum(product, sign):
    product = product.reshape(3, 3, 3, -1, product.shape[-1])
    sums = []
    for depth_tap in range(3):
        total = None
        for row_tap in range(3):
            for col_tap in range(3):
                term = roll_plane(
                    product[depth_tap, row_tap, col_tap], sign * (1 - row_tap), sign * (1 - col_tap)
                )
                total = term if total is None else total + term
        sums.append(total)
    return sums


def body(volume, kernel, cotangent):
    ch_local = volume.shape[2]
    cells = volume.shape[3]
    chans = lax.axis_size("chan")
    depths = lax.axis_size("depth")
    ring = [(i, (i + 1) % depths) for i in range(depths)]
    back = [(b, a) for a, b in ring]

    gathered = spread(volume.reshape(ch_local, cells), "chan").reshape(-1, cells)
    k4 = kernel.reshape(ch_local, TAPS, chans, ch_local)
    k_in = lax.all_to_all(
        jnp.transpose(k4, (2, 0, 1, 3)).reshape(chans, ch_local, TAPS * ch_local), "chan", 0, 0
    ).reshape(chans * ch_local, TAPS * ch_local)
    k_rows = jnp.transpose(kernel.reshape(ch_local, TAPS, -1), (1, 0, 2)).reshape(TAPS * ch_local, -1)

    product = jnp.dot(k_rows, gathered, preferred_element_type=jnp.float32)
    up, mid, down = rolled_sum(product, 1)
    preact = mid + lax.ppermute(up, "depth", ring) + lax.ppermute(down, "depth", back)
    sig = jax.nn.sigmoid(preact)
    activated = (preact * sig).astype(jnp.bfloat16)
    cot = cotangent.reshape(ch_local, cells).astype(jnp.float32)
    grad_pre = (cot * sig * (1.0 + preact * (1.0 - sig))).astype(jnp.bfloat16)

    grad_above = lax.ppermute(grad_pre, "depth", back)
    grad_below = lax.ppermute(grad_pre, "depth", ring)
    stacked = jnp.concatenate(
        [
            roll_plane(plane, row_tap - 1, col_tap - 1)
            for plane in (grad_above, grad_pre, grad_below)
            for row_tap in range(3)
            for col_tap in range(3)
        ],
        axis=0,
    )
    local = lax.dot_general(
        stacked, gathered, (((1,), (1,)), ((), ())), preferred_element_type=jnp.float32
    )
    pieces = local.astype(jnp.bfloat16).reshape(TAPS, ch_local, -1)
    pieces = jnp.concatenate(
        [pieces, jnp.zeros((depths - TAPS,) + pieces.shape[1:], pieces.dtype)], axis=0
    )
    terms = lax.all_to_all(pieces, "depth", 0, 0)
    grad_scale = 1.0 / math.sqrt(UNIV * DEPTH * SIDE * SIDE)
    tap_total = jnp.sum(terms.astype(jnp.float32), axis=0) * grad_scale
    all_taps = spread(tap_total.astype(jnp.bfloat16), "depth")[:TAPS]
    grad_kernel = jnp.transpose(all_taps.astype(jnp.float32), (1, 0, 2)).reshape(kernel.shape)

    grad_all = spread(grad_pre, "chan").reshape(-1, cells)
    back_product = lax.dot_general(
        k_in, grad_all, (((0,), (0,)), ((), ())), preferred_element_type=jnp.float32
    )
    low, same, high = rolled_sum(back_product, -1)
    grad_volume = (
        same + lax.ppermute(low, "depth", back) + lax.ppermute(high, "depth", ring)
    ).astype(jnp.bfloat16)
    return (activated.reshape(volume.shape), grad_volume.reshape(volume.shape), grad_kernel)


def solution(mesh):
    placed = (
        P(None, "depth", "chan", None),
        P("chan", None, None, None, None),
        P(None, "depth", "chan", None),
    )
    return jax.shard_map(
        body,
        mesh=mesh,
        in_specs=placed,
        out_specs=(
            P(None, "depth", "chan", None),
            P(None, "depth", "chan", None),
            P("chan", None, None, None, None),
        ),
        check_vma=False,
    )
```

```python
import functools
import math

import jax
import jax.numpy as jnp
from jax import lax
from jax.experimental import pallas as pl
from jax.experimental.pallas import tpu as pltpu
from jax.sharding import Mesh
from jax.sharding import PartitionSpec as P

DEPTH = 32
SIDE = 32
UNIV = 1
TAPS = 27
VMEM_LIMIT = 48 * 1024 * 1024
DEP = ("y", "zh")
CHIPS = ("x", "zl")
CHAN = ("x", "zl", "core")


def shift_cells(plane, row_step, col_step):
    cells = plane.shape[-1]
    if col_step:
        columns = lax.broadcasted_iota(jnp.int32, plane.shape, 1) % SIDE
        edge = 0 if col_step > 0 else SIDE - 1
        plain = pltpu.roll(plane, col_step % cells, 1)
        wrapped = pltpu.roll(plane, (col_step - col_step * SIDE) % cells, 1)
        plane = jnp.where(columns == edge, wrapped, plain)
    if row_step:
        plane = pltpu.roll(plane, (row_step * SIDE) % cells, 1)
    return plane


def merge_cores(core_ref, mine_ref, other_ref, x_ref):
    first = core_ref[0] == 0
    mine, other = mine_ref[...], other_ref[...]
    x_ref[:, 0] = jnp.where(first, mine, other)
    x_ref[:, 1] = jnp.where(first, other, mine)
    return x_ref[...].reshape(-1, x_ref.shape[-1])


def conv_kernel(core_ref, w_ref, mine_ref, other_ref, *refs, sign):
    outs, x_ref = refs[:3], refs[3]
    rows = outs[0].shape[0]
    x = merge_cores(core_ref, mine_ref, other_ref, x_ref)
    for depth_tap in range(3):
        w = w_ref[depth_tap * 9 * rows : (depth_tap + 1) * 9 * rows, :]
        product = jnp.dot(w, x, preferred_element_type=jnp.float32)
        total = None
        for col_tap in range(3):
            part = None
            for row_tap in range(3):
                at = (row_tap * 3 + col_tap) * rows
                term = shift_cells(product[at : at + rows], sign * (1 - row_tap), 0)
                part = term if part is None else part + term
            part = shift_cells(part, 0, sign * (1 - col_tap))
            total = part if total is None else total + part
        outs[depth_tap][...] = total


def merged_specs(count):
    smem = pl.BlockSpec(memory_space=pltpu.SMEM)
    return [smem] + [pl.BlockSpec(memory_space=pltpu.VMEM)] * count


def merged_scratch(mine):
    return [pltpu.VMEM((mine.shape[0], 2) + mine.shape[1:], mine.dtype)]


def conv(core, weights, mine, other, sign):
    rows = weights.shape[0] // TAPS
    cells = mine.shape[-1]
    return pl.pallas_call(
        functools.partial(conv_kernel, sign=sign),
        out_shape=[jax.ShapeDtypeStruct((rows, cells), jnp.float32)] * 3,
        in_specs=merged_specs(3),
        scratch_shapes=merged_scratch(mine),
        compiler_params=pltpu.CompilerParams(vmem_limit_bytes=VMEM_LIMIT),
        name="conv",
    )(core, weights, mine, other)


def wgrad_kernel(core_ref, above_ref, own_ref, below_ref, mine_ref, other_ref, out_ref, x_ref):
    rows = own_ref.shape[0]
    x = merge_cores(core_ref, mine_ref, other_ref, x_ref)
    for depth_tap, ref in enumerate((above_ref, own_ref, below_ref)):
        plane = ref[...].astype(jnp.float32)
        moved = [shift_cells(plane, 0, col_tap - 1) for col_tap in range(3)]
        stack = jnp.concatenate(
            [
                shift_cells(moved[col_tap], row_tap - 1, 0).astype(jnp.bfloat16)
                for row_tap in range(3)
                for col_tap in range(3)
            ],
            axis=0,
        )
        grad = lax.dot_general(
            stack, x, (((1,), (1,)), ((), ())), preferred_element_type=jnp.float32
        )
        out_ref[depth_tap * 9 : depth_tap * 9 + 9] = grad.astype(jnp.bfloat16).reshape(9, rows, -1)
    out_ref[TAPS:] = jnp.zeros((out_ref.shape[0] - TAPS,) + out_ref.shape[1:], out_ref.dtype)


def wgrad(core, above, own, below, mine, other, slots):
    rows = own.shape[0]
    chans = 2 * mine.shape[0] * mine.shape[1]
    return pl.pallas_call(
        wgrad_kernel,
        out_shape=jax.ShapeDtypeStruct((slots, rows, chans), jnp.bfloat16),
        in_specs=merged_specs(5),
        scratch_shapes=merged_scratch(mine),
        compiler_params=pltpu.CompilerParams(vmem_limit_bytes=VMEM_LIMIT),
        name="wgrad",
    )(core, above, own, below, mine, other)


def act_kernel(mid_ref, low_ref, high_ref, cot_ref, act_ref, grad_ref):
    preact = mid_ref[...] + low_ref[...] + high_ref[...]
    sig = jax.nn.sigmoid(preact)
    act_ref[...] = (preact * sig).astype(jnp.bfloat16)
    cot = cot_ref[...].astype(jnp.float32)
    grad_ref[...] = (cot * sig * (1.0 + preact * (1.0 - sig))).astype(jnp.bfloat16)


def activate(mid, low, high, cot):
    shape = jax.ShapeDtypeStruct(mid.shape, jnp.bfloat16)
    return pl.pallas_call(
        act_kernel,
        out_shape=[shape, shape],
        compiler_params=pltpu.CompilerParams(vmem_limit_bytes=VMEM_LIMIT),
        name="activate",
    )(mid, low, high, cot)


def total_kernel(terms_ref, out_ref, *, scale):
    total = jnp.sum(terms_ref[...].astype(jnp.float32), axis=0) * scale
    out_ref[...] = jnp.broadcast_to(total.astype(jnp.bfloat16)[None], out_ref.shape)


def total_spread(terms, scale, copies):
    return pl.pallas_call(
        functools.partial(total_kernel, scale=scale),
        out_shape=jax.ShapeDtypeStruct((copies,) + terms.shape[1:], jnp.bfloat16),
        compiler_params=pltpu.CompilerParams(vmem_limit_bytes=VMEM_LIMIT),
        name="total",
    )(terms)


def swap_cores(blocks):
    return lax.ppermute(blocks, "core", [(0, 1), (1, 0)])


def body(volume, kernel, cotangent):
    rows = volume.shape[2]
    cells = volume.shape[3]
    chips = lax.axis_size(CHIPS)
    chans = lax.axis_size(CHAN)
    depths = lax.axis_size(DEP)
    ring = [(i, (i + 1) % depths) for i in range(depths)]
    back = [(b, a) for a, b in ring]
    core = lax.axis_index("core").astype(jnp.int32).reshape(1)
    own = volume.reshape(rows, cells)
    cot = cotangent.reshape(rows, cells)

    def copies(block):
        return jnp.broadcast_to(block[None], (chips, rows, cells))

    mine = lax.all_to_all(copies(own), CHIPS, 0, 0)
    k_rows = jnp.transpose(kernel.reshape(rows, TAPS, -1), (1, 0, 2)).reshape(TAPS * rows, -1)
    pieces = jnp.transpose(k_rows).reshape(chans, rows, TAPS * rows)
    mine, pieces, k_rows, cot = lax.optimization_barrier((mine, pieces, k_rows, cot))
    other = swap_cores(mine)
    k_in = lax.all_to_all(pieces, CHAN, 0, 0)

    up, mid, down = conv(core, k_rows, mine, other, 1)
    low = lax.ppermute(up, DEP, ring)
    high = lax.ppermute(down, DEP, back)
    activated, grad_pre = activate(mid, low, high, cot)
    grad_pre, k_in = lax.optimization_barrier((grad_pre, k_in))

    grad_above = lax.ppermute(grad_pre, DEP, back)
    grad_below = lax.ppermute(grad_pre, DEP, ring)
    grad_mine = lax.all_to_all(copies(grad_pre), CHIPS, 0, 0)
    wide = wgrad(core, grad_above, grad_pre, grad_below, mine, other, depths)
    wide, grad_mine = lax.optimization_barrier((wide, grad_mine))
    terms = lax.all_to_all(wide, DEP, 0, 0)

    k_cols = jnp.transpose(k_in.reshape(chans, rows, TAPS, rows), (2, 1, 0, 3))
    k_cols = k_cols.reshape(TAPS * rows, chans * rows)
    grad_other = swap_cores(grad_mine)
    to_low, same, to_high = conv(core, k_cols, grad_mine, grad_other, -1)
    terms, same = lax.optimization_barrier((terms, same))
    from_high = lax.ppermute(to_low, DEP, back)
    from_low = lax.ppermute(to_high, DEP, ring)
    grad_volume = (same + from_high + from_low).astype(jnp.bfloat16)

    scale = 1.0 / math.sqrt(UNIV * DEPTH * SIDE * SIDE)
    all_taps = lax.all_to_all(total_spread(terms, scale, depths), DEP, 0, 0)[:TAPS]
    grad_kernel = jnp.transpose(all_taps.astype(jnp.float32), (1, 0, 2)).reshape(kernel.shape)
    return (activated.reshape(volume.shape), grad_volume.reshape(volume.shape), grad_kernel)


def solution(mesh):
    fine = Mesh(mesh.devices.reshape(8, 4, 4, 3, 2), ("y", "zh", "x", "zl", "core"))
    field = P(None, DEP, CHAN, None)
    weight = P(CHAN, None, None, None, None)
    return jax.shard_map(
        body,
        mesh=fine,
        in_specs=(field, weight, field),
        out_specs=(field, field, weight),
        check_vma=False,
    )
```

```python
import functools
import math

import jax
import jax.numpy as jnp
from jax import lax
from jax.experimental import pallas as pl
from jax.experimental.pallas import tpu as pltpu
from jax.sharding import Mesh
from jax.sharding import PartitionSpec as P

DEPTH = 32
SIDE = 32
UNIV = 1
TAPS = 27
VMEM_LIMIT = 48 * 1024 * 1024
DEP = ("y", "zh")
CHIPS = ("x", "zl")
CHAN = ("x", "zl", "core")


def shift_cells(plane, row_step, col_step):
    cells = plane.shape[-1]
    if col_step:
        columns = lax.broadcasted_iota(jnp.int32, plane.shape, 1) % SIDE
        edge = 0 if col_step > 0 else SIDE - 1
        plain = pltpu.roll(plane, col_step % cells, 1)
        wrapped = pltpu.roll(plane, (col_step - col_step * SIDE) % cells, 1)
        plane = jnp.where(columns == edge, wrapped, plain)
    if row_step:
        plane = pltpu.roll(plane, (row_step * SIDE) % cells, 1)
    return plane


def merge_cores(core_ref, mine_ref, other_ref, x_ref):
    first = core_ref[0] == 0
    mine, other = mine_ref[...], other_ref[...]
    x_ref[:, 0] = jnp.where(first, mine, other)
    x_ref[:, 1] = jnp.where(first, other, mine)
    return x_ref[...].reshape(-1, x_ref.shape[-1])


def conv_kernel(core_ref, w_ref, mine_ref, other_ref, *refs, sign):
    outs, x_ref = refs[:3], refs[3]
    rows = outs[0].shape[0]
    x = merge_cores(core_ref, mine_ref, other_ref, x_ref)
    for depth_tap in range(3):
        w = w_ref[depth_tap * 9 * rows : (depth_tap + 1) * 9 * rows, :]
        product = jnp.dot(w, x, preferred_element_type=jnp.float32)
        total = None
        for col_tap in range(3):
            part = None
            for row_tap in range(3):
                at = (row_tap * 3 + col_tap) * rows
                term = shift_cells(product[at : at + rows], sign * (1 - row_tap), 0)
                part = term if part is None else part + term
            part = shift_cells(part, 0, sign * (1 - col_tap))
            total = part if total is None else total + part
        outs[depth_tap][...] = total


def merged_specs(count):
    smem = pl.BlockSpec(memory_space=pltpu.SMEM)
    return [smem] + [pl.BlockSpec(memory_space=pltpu.VMEM)] * count


def merged_scratch(mine):
    return [pltpu.VMEM((mine.shape[0], 2) + mine.shape[1:], mine.dtype)]


def conv(core, weights, mine, other, sign):
    rows = weights.shape[0] // TAPS
    cells = mine.shape[-1]
    return pl.pallas_call(
        functools.partial(conv_kernel, sign=sign),
        out_shape=[jax.ShapeDtypeStruct((rows, cells), jnp.float32)] * 3,
        in_specs=merged_specs(3),
        scratch_shapes=merged_scratch(mine),
        compiler_params=pltpu.CompilerParams(vmem_limit_bytes=VMEM_LIMIT),
        name="conv",
    )(core, weights, mine, other)


def grads_kernel(
    place_ref, k_ref, above_ref, own_ref, below_ref, mine_ref, other_ref,
    wide_ref, keep_ref, send_ref, x_ref, stack_ref,
):
    rows = own_ref.shape[0]
    x = merge_cores(place_ref, mine_ref, other_ref, x_ref)
    for depth_tap, ref in enumerate((above_ref, own_ref, below_ref)):
        plane = ref[...].astype(jnp.float32)
        moved = [shift_cells(plane, 0, col_tap - 1) for col_tap in range(3)]
        for row_tap in range(3):
            for col_tap in range(3):
                at = ((depth_tap * 3 + row_tap) * 3 + col_tap) * rows
                stack_ref[at : at + rows, :] = shift_cells(moved[col_tap], row_tap - 1, 0).astype(
                    jnp.bfloat16
                )
        at = depth_tap * 9 * rows
        grad = lax.dot_general(
            stack_ref[at : at + 9 * rows, :],
            x,
            (((1,), (1,)), ((), ())),
            preferred_element_type=jnp.float32,
        )
        wide_ref[depth_tap * 9 : depth_tap * 9 + 9] = grad.astype(jnp.bfloat16).reshape(9, rows, -1)
    wide_ref[TAPS:] = jnp.zeros((wide_ref.shape[0] - TAPS,) + wide_ref.shape[1:], wide_ref.dtype)

    partial = lax.dot_general(
        k_ref[...], stack_ref[...], (((0,), (0,)), ((), ())), preferred_element_type=jnp.float32
    ).astype(jnp.bfloat16)
    first = place_ref[0] == 0
    for x_at in range(4):
        for z_at in range(3):
            x_slot = x_at ^ place_ref[1]
            z_slot = lax.rem(z_at - place_ref[2] + 3, 3)
            at = (x_at * 3 + z_at) * 2 * rows
            even, odd = partial[at : at + rows], partial[at + rows : at + 2 * rows]
            keep_ref[x_slot, z_slot] = jnp.where(first, even, odd)
            send_ref[x_slot, z_slot] = jnp.where(first, odd, even)


def grads(place, k_rows, above, own, below, mine, other, slots):
    rows, cells = own.shape
    chans = 2 * mine.shape[0] * mine.shape[1]
    half = jax.ShapeDtypeStruct((4, 3, rows, cells), jnp.bfloat16)
    return pl.pallas_call(
        grads_kernel,
        out_shape=[jax.ShapeDtypeStruct((slots, rows, chans), jnp.bfloat16), half, half],
        in_specs=merged_specs(6),
        scratch_shapes=merged_scratch(mine) + [pltpu.VMEM((TAPS * rows, cells), jnp.bfloat16)],
        compiler_params=pltpu.CompilerParams(vmem_limit_bytes=VMEM_LIMIT),
        name="grads",
    )(place, k_rows, above, own, below, mine, other)


def act_kernel(mid_ref, low_ref, high_ref, cot_ref, act_ref, grad_ref):
    preact = mid_ref[...] + low_ref[...] + high_ref[...]
    sig = jax.nn.sigmoid(preact)
    act_ref[...] = (preact * sig).astype(jnp.bfloat16)
    cot = cot_ref[...].astype(jnp.float32)
    grad_ref[...] = (cot * sig * (1.0 + preact * (1.0 - sig))).astype(jnp.bfloat16)


def activate(mid, low, high, cot):
    shape = jax.ShapeDtypeStruct(mid.shape, jnp.bfloat16)
    return pl.pallas_call(
        act_kernel,
        out_shape=[shape, shape],
        compiler_params=pltpu.CompilerParams(vmem_limit_bytes=VMEM_LIMIT),
        name="activate",
    )(mid, low, high, cot)


def total_kernel(terms_ref, out_ref, *, scale):
    total = jnp.sum(terms_ref[...].astype(jnp.float32), axis=0) * scale
    out_ref[...] = jnp.broadcast_to(total.astype(jnp.bfloat16)[None], out_ref.shape)


def total_spread(terms, scale, copies):
    return pl.pallas_call(
        functools.partial(total_kernel, scale=scale),
        out_shape=jax.ShapeDtypeStruct((copies,) + terms.shape[1:], jnp.bfloat16),
        compiler_params=pltpu.CompilerParams(vmem_limit_bytes=VMEM_LIMIT),
        name="total",
    )(terms)


def swap_cores(blocks):
    return lax.ppermute(blocks, "core", [(0, 1), (1, 0)])


def body(volume, kernel, cotangent):
    rows = volume.shape[2]
    cells = volume.shape[3]
    chips = lax.axis_size(CHIPS)
    depths = lax.axis_size(DEP)
    ring = [(i, (i + 1) % depths) for i in range(depths)]
    back = [(b, a) for a, b in ring]
    place = jnp.stack([lax.axis_index(name) for name in ("core", "x", "zl")]).astype(jnp.int32)
    own = volume.reshape(rows, cells)
    cot = cotangent.reshape(rows, cells)

    def copies(block):
        return jnp.broadcast_to(block[None], (chips, rows, cells))

    mine = lax.all_to_all(copies(own), CHIPS, 0, 0)
    k_rows = jnp.transpose(kernel.reshape(rows, TAPS, -1), (1, 0, 2)).reshape(TAPS * rows, -1)
    mine, k_rows, cot, place = lax.optimization_barrier((mine, k_rows, cot, place))
    other = swap_cores(mine)

    up, mid, down = conv(place, k_rows, mine, other, 1)
    low = lax.ppermute(up, DEP, ring)
    high = lax.ppermute(down, DEP, back)
    activated, grad_pre = activate(mid, low, high, cot)

    grad_above = lax.ppermute(grad_pre, DEP, back)
    grad_below = lax.ppermute(grad_pre, DEP, ring)
    wide, keep, send = grads(place, k_rows, grad_above, grad_pre, grad_below, mine, other, depths)
    terms = lax.all_to_all(wide, DEP, 0, 0)

    total = keep.astype(jnp.float32) + swap_cores(send).astype(jnp.float32)
    total = total.reshape(2, 2, 3, rows, cells)
    step = lax.ppermute(total[:, 1].astype(jnp.bfloat16), "x", [(i, i ^ 1) for i in range(4)])
    total = total[:, 0] + step.astype(jnp.float32)
    terms, total = lax.optimization_barrier((terms, total))
    step = lax.ppermute(total[1].astype(jnp.bfloat16), "x", [(i, i ^ 2) for i in range(4)])
    total = total[0] + step.astype(jnp.float32)
    after = lax.ppermute(total[1], "zl", [(i, (i + 1) % 3) for i in range(3)])
    before = lax.ppermute(total[2], "zl", [(i, (i + 2) % 3) for i in range(3)])
    grad_volume = (total[0] + after + before).astype(jnp.bfloat16)

    scale = 1.0 / math.sqrt(UNIV * DEPTH * SIDE * SIDE)
    all_taps = lax.all_to_all(total_spread(terms, scale, depths), DEP, 0, 0)[:TAPS]
    grad_kernel = jnp.transpose(all_taps.astype(jnp.float32), (1, 0, 2)).reshape(kernel.shape)
    return (activated.reshape(volume.shape), grad_volume.reshape(volume.shape), grad_kernel)


def solution(mesh):
    fine = Mesh(mesh.devices.reshape(8, 4, 4, 3, 2), ("y", "zh", "x", "zl", "core"))
    field = P(None, DEP, CHAN, None)
    weight = P(CHAN, None, None, None, None)
    return jax.shard_map(
        body,
        mesh=fine,
        in_specs=(field, weight, field),
        out_specs=(field, field, weight),
        check_vma=False,
    )
```

```python
import functools
import math

import jax
import jax.numpy as jnp
from jax import lax
from jax.experimental import pallas as pl
from jax.experimental.pallas import tpu as pltpu
from jax.sharding import Mesh
from jax.sharding import PartitionSpec as P

DEPTH = 32
SIDE = 32
UNIV = 1
TAPS = 27
LANES = 128
VMEM_LIMIT = 48 * 1024 * 1024
DEP = ("y", "zh")
CHIPS = ("x", "zl")
CHAN = ("x", "zl", "core")


def shift_cells(plane, row_step, col_step):
    cells = plane.shape[-1]
    if col_step:
        columns = lax.broadcasted_iota(jnp.int32, plane.shape, 1) % SIDE
        edge = 0 if col_step > 0 else SIDE - 1
        plain = pltpu.roll(plane, col_step % cells, 1)
        wrapped = pltpu.roll(plane, (col_step - col_step * SIDE) % cells, 1)
        plane = jnp.where(columns == edge, wrapped, plain)
    if row_step:
        plane = pltpu.roll(plane, (row_step * SIDE) % cells, 1)
    return plane


def merge_cores(core_ref, mine_ref, other_ref, x_ref):
    first = core_ref[0] == 0
    mine, other = mine_ref[...], other_ref[...]
    x_ref[:, 0] = jnp.where(first, mine, other)
    x_ref[:, 1] = jnp.where(first, other, mine)
    return x_ref[...].reshape(-1, x_ref.shape[-1])


def conv_kernel(core_ref, w_ref, mine_ref, other_ref, *refs, sign):
    outs, x_ref = refs[:3], refs[3]
    rows = outs[0].shape[0]
    x = merge_cores(core_ref, mine_ref, other_ref, x_ref)
    for depth_tap in range(3):
        w = w_ref[depth_tap * 9 * rows : (depth_tap + 1) * 9 * rows, :]
        product = jnp.dot(w, x, preferred_element_type=jnp.float32)
        total = None
        for col_tap in range(3):
            part = None
            for row_tap in range(3):
                at = (row_tap * 3 + col_tap) * rows
                term = shift_cells(product[at : at + rows], sign * (1 - row_tap), 0)
                part = term if part is None else part + term
            part = shift_cells(part, 0, sign * (1 - col_tap))
            total = part if total is None else total + part
        outs[depth_tap][...] = total


def merged_specs(count):
    smem = pl.BlockSpec(memory_space=pltpu.SMEM)
    return [smem] + [pl.BlockSpec(memory_space=pltpu.VMEM)] * count


def merged_scratch(mine):
    return [pltpu.VMEM((mine.shape[0], 2) + mine.shape[1:], mine.dtype)]


def conv(core, weights, mine, other, sign):
    rows = weights.shape[0] // TAPS
    cells = mine.shape[-1]
    return pl.pallas_call(
        functools.partial(conv_kernel, sign=sign),
        out_shape=[jax.ShapeDtypeStruct((rows, cells), jnp.float32)] * 3,
        in_specs=merged_specs(3),
        scratch_shapes=merged_scratch(mine),
        compiler_params=pltpu.CompilerParams(vmem_limit_bytes=VMEM_LIMIT),
        name="conv",
    )(core, weights, mine, other)


def grads_kernel(
    place_ref, k_ref, above_ref, own_ref, below_ref, mine_ref, other_ref,
    wide_ref, keep_ref, send_ref, x_ref, stack_ref,
):
    rows = own_ref.shape[0]
    slots, per = wide_ref.shape[:2]
    columns = x_ref.shape[0] * x_ref.shape[1] * x_ref.shape[2] // LANES
    x = merge_cores(place_ref, mine_ref, other_ref, x_ref)
    for depth_tap, ref in enumerate((above_ref, own_ref, below_ref)):
        plane = ref[...].astype(jnp.float32)
        moved = [shift_cells(plane, 0, col_tap - 1) for col_tap in range(3)]
        for row_tap in range(3):
            for col_tap in range(3):
                at = ((depth_tap * 3 + row_tap) * 3 + col_tap) * rows
                stack_ref[at : at + rows, :] = shift_cells(moved[col_tap], row_tap - 1, 0).astype(
                    jnp.bfloat16
                )
        at = depth_tap * 9 * rows
        grad = lax.dot_general(
            stack_ref[at : at + 9 * rows, :],
            x,
            (((1,), (1,)), ((), ())),
            preferred_element_type=jnp.float32,
        )
        grad = grad.astype(jnp.bfloat16)
        for tap in range(9):
            for column in range(columns):
                unit = (depth_tap * 9 + tap) * columns + column
                wide_ref[unit // per, unit % per] = grad[
                    tap * rows : (tap + 1) * rows, column * LANES : (column + 1) * LANES
                ]
    for unit in range(TAPS * columns, slots * per):
        wide_ref[unit // per, unit % per] = jnp.zeros((rows, LANES), jnp.bfloat16)

    partial = lax.dot_general(
        k_ref[...], stack_ref[...], (((0,), (0,)), ((), ())), preferred_element_type=jnp.float32
    ).astype(jnp.bfloat16)
    first = place_ref[0] == 0
    for x_at in range(4):
        for z_at in range(3):
            x_slot = x_at ^ place_ref[1]
            z_slot = lax.rem(z_at - place_ref[2] + 3, 3)
            at = (x_at * 3 + z_at) * 2 * rows
            even, odd = partial[at : at + rows], partial[at + rows : at + 2 * rows]
            keep_ref[x_slot, z_slot] = jnp.where(first, even, odd)
            send_ref[x_slot, z_slot] = jnp.where(first, odd, even)


def grads(place, k_rows, above, own, below, mine, other, slots):
    rows, cells = own.shape
    chans = 2 * mine.shape[0] * mine.shape[1]
    per = -(-TAPS * chans // (LANES * slots))
    half = jax.ShapeDtypeStruct((4, 3, rows, cells), jnp.bfloat16)
    return pl.pallas_call(
        grads_kernel,
        out_shape=[jax.ShapeDtypeStruct((slots, per, rows, LANES), jnp.bfloat16), half, half],
        in_specs=merged_specs(6),
        scratch_shapes=merged_scratch(mine) + [pltpu.VMEM((TAPS * rows, cells), jnp.bfloat16)],
        compiler_params=pltpu.CompilerParams(vmem_limit_bytes=VMEM_LIMIT),
        name="grads",
    )(place, k_rows, above, own, below, mine, other)


def act_kernel(mid_ref, low_ref, high_ref, cot_ref, act_ref, grad_ref):
    preact = mid_ref[...] + low_ref[...] + high_ref[...]
    sig = jax.nn.sigmoid(preact)
    act_ref[...] = (preact * sig).astype(jnp.bfloat16)
    cot = cot_ref[...].astype(jnp.float32)
    grad_ref[...] = (cot * sig * (1.0 + preact * (1.0 - sig))).astype(jnp.bfloat16)


def activate(mid, low, high, cot):
    shape = jax.ShapeDtypeStruct(mid.shape, jnp.bfloat16)
    return pl.pallas_call(
        act_kernel,
        out_shape=[shape, shape],
        compiler_params=pltpu.CompilerParams(vmem_limit_bytes=VMEM_LIMIT),
        name="activate",
    )(mid, low, high, cot)


def total_kernel(terms_ref, out_ref, *, scale):
    total = jnp.sum(terms_ref[...].astype(jnp.float32), axis=0) * scale
    out_ref[...] = jnp.broadcast_to(total.astype(jnp.bfloat16)[None], out_ref.shape)


def total_spread(terms, scale, copies):
    return pl.pallas_call(
        functools.partial(total_kernel, scale=scale),
        out_shape=jax.ShapeDtypeStruct((copies,) + terms.shape[1:], jnp.bfloat16),
        compiler_params=pltpu.CompilerParams(vmem_limit_bytes=VMEM_LIMIT),
        name="total",
    )(terms)


def unpack_kernel(units_ref, out_ref):
    per = units_ref.shape[1]
    columns = out_ref.shape[2] // LANES
    for tap in range(TAPS):
        for column in range(columns):
            unit = tap * columns + column
            block = units_ref[unit // per, unit % per].astype(jnp.float32)
            out_ref[tap, :, column * LANES : (column + 1) * LANES] = block


def unpack(units, chans):
    return pl.pallas_call(
        unpack_kernel,
        out_shape=jax.ShapeDtypeStruct((TAPS, units.shape[2], chans), jnp.float32),
        compiler_params=pltpu.CompilerParams(vmem_limit_bytes=VMEM_LIMIT),
        name="unpack",
    )(units)


def swap_cores(blocks):
    return lax.ppermute(blocks, "core", [(0, 1), (1, 0)])


def body(volume, kernel, cotangent):
    rows = volume.shape[2]
    cells = volume.shape[3]
    chips = lax.axis_size(CHIPS)
    depths = lax.axis_size(DEP)
    ring = [(i, (i + 1) % depths) for i in range(depths)]
    back = [(b, a) for a, b in ring]
    place = jnp.stack([lax.axis_index(name) for name in ("core", "x", "zl")]).astype(jnp.int32)
    own = volume.reshape(rows, cells)
    cot = cotangent.reshape(rows, cells)

    def copies(block):
        return jnp.broadcast_to(block[None], (chips, rows, cells))

    mine = lax.all_to_all(copies(own), CHIPS, 0, 0)
    k_rows = jnp.transpose(kernel.reshape(rows, TAPS, -1), (1, 0, 2)).reshape(TAPS * rows, -1)
    mine, k_rows, cot, place = lax.optimization_barrier((mine, k_rows, cot, place))
    other = swap_cores(mine)

    up, mid, down = conv(place, k_rows, mine, other, 1)
    low = lax.ppermute(up, DEP, ring)
    high = lax.ppermute(down, DEP, back)
    activated, grad_pre = activate(mid, low, high, cot)

    grad_above = lax.ppermute(grad_pre, DEP, back)
    grad_below = lax.ppermute(grad_pre, DEP, ring)
    ys, zs, xs = lax.axis_size("y"), lax.axis_size("zh"), lax.axis_size("x")
    wide, keep, send = grads(place, k_rows, grad_above, grad_pre, grad_below, mine, other, ys)
    scale = 1.0 / math.sqrt(UNIV * DEPTH * SIDE * SIDE)
    over_y = lax.all_to_all(wide, "y", 0, 0)

    total = keep.astype(jnp.float32) + swap_cores(send).astype(jnp.float32)
    over_y, total = lax.optimization_barrier((over_y, total))
    over_z = lax.all_to_all(total_spread(over_y, 1.0, zs), "zh", 0, 0)
    steps = [
        lax.ppermute(total[away].astype(jnp.bfloat16), "x", [(i, i ^ away) for i in range(xs)])
        for away in range(1, xs)
    ]
    total = total[0] + sum(step.astype(jnp.float32) for step in steps)
    over_z, total = lax.optimization_barrier((over_z, total))
    units = lax.all_to_all(total_spread(over_z, scale, ys), "y", 0, 0)
    after = lax.ppermute(total[1], "zl", [(i, (i + 1) % 3) for i in range(3)])
    before = lax.ppermute(total[2], "zl", [(i, (i + 2) % 3) for i in range(3)])
    grad_volume = (total[0] + after + before).astype(jnp.bfloat16)
    all_taps = unpack(units, kernel.shape[-1])
    grad_kernel = jnp.transpose(all_taps, (1, 0, 2)).reshape(kernel.shape)
    return (activated.reshape(volume.shape), grad_volume.reshape(volume.shape), grad_kernel)


def solution(mesh):
    fine = Mesh(mesh.devices.reshape(8, 4, 4, 3, 2), ("y", "zh", "x", "zl", "core"))
    field = P(None, DEP, CHAN, None)
    weight = P(CHAN, None, None, None, None)
    return jax.shard_map(
        body,
        mesh=fine,
        in_specs=(field, weight, field),
        out_specs=(field, field, weight),
        check_vma=False,
    )
```

```python
import functools
import math

import jax
import jax.numpy as jnp
from jax import lax
from jax.experimental import pallas as pl
from jax.experimental.pallas import tpu as pltpu
from jax.sharding import Mesh
from jax.sharding import PartitionSpec as P

DEPTH = 32
SIDE = 32
UNIV = 1
TAPS = 27
LANES = 128
VMEM_LIMIT = 48 * 1024 * 1024
DEP = ("y", "zh")
CHIPS = ("x", "zl")
CHAN = ("x", "zl", "core")


def shift_cells(plane, row_step, col_step):
    cells = plane.shape[-1]
    if col_step:
        columns = lax.broadcasted_iota(jnp.int32, plane.shape, 1) % SIDE
        edge = 0 if col_step > 0 else SIDE - 1
        plain = pltpu.roll(plane, col_step % cells, 1)
        wrapped = pltpu.roll(plane, (col_step - col_step * SIDE) % cells, 1)
        plane = jnp.where(columns == edge, wrapped, plain)
    if row_step:
        plane = pltpu.roll(plane, (row_step * SIDE) % cells, 1)
    return plane


def merge_cores(core_ref, mine_ref, other_ref, x_ref):
    first = core_ref[0] == 0
    mine, other = mine_ref[...], other_ref[...]
    x_ref[:, 0] = jnp.where(first, mine, other)
    x_ref[:, 1] = jnp.where(first, other, mine)
    return x_ref[...].reshape(-1, x_ref.shape[-1])


def conv_kernel(core_ref, w_ref, mine_ref, other_ref, *refs, sign):
    outs, x_ref = refs[:3], refs[3]
    rows = outs[0].shape[0]
    x = merge_cores(core_ref, mine_ref, other_ref, x_ref)
    for depth_tap in range(3):
        w = w_ref[depth_tap * 9 * rows : (depth_tap + 1) * 9 * rows, :]
        product = jnp.dot(w, x, preferred_element_type=jnp.float32)
        total = None
        for col_tap in range(3):
            part = None
            for row_tap in range(3):
                at = (row_tap * 3 + col_tap) * rows
                term = shift_cells(product[at : at + rows], sign * (1 - row_tap), 0)
                part = term if part is None else part + term
            part = shift_cells(part, 0, sign * (1 - col_tap))
            total = part if total is None else total + part
        outs[depth_tap][...] = total


def merged_specs(count):
    smem = pl.BlockSpec(memory_space=pltpu.SMEM)
    return [smem] + [pl.BlockSpec(memory_space=pltpu.VMEM)] * count


def merged_scratch(mine):
    return [pltpu.VMEM((mine.shape[0], 2) + mine.shape[1:], mine.dtype)]


def conv(core, weights, mine, other, sign):
    rows = weights.shape[0] // TAPS
    cells = mine.shape[-1]
    return pl.pallas_call(
        functools.partial(conv_kernel, sign=sign),
        out_shape=[jax.ShapeDtypeStruct((rows, cells), jnp.float32)] * 3,
        in_specs=merged_specs(3),
        scratch_shapes=merged_scratch(mine),
        compiler_params=pltpu.CompilerParams(vmem_limit_bytes=VMEM_LIMIT),
        name="conv",
    )(core, weights, mine, other)


def wgrad_kernel(
    place_ref, above_ref, own_ref, below_ref, mine_ref, other_ref, wide_ref, stack_ref, x_ref
):
    rows = own_ref.shape[0]
    slots, per = wide_ref.shape[:2]
    columns = x_ref.shape[0] * x_ref.shape[1] * x_ref.shape[2] // LANES
    x = merge_cores(place_ref, mine_ref, other_ref, x_ref)
    for depth_tap, ref in enumerate((above_ref, own_ref, below_ref)):
        plane = ref[...].astype(jnp.float32)
        moved = [shift_cells(plane, 0, col_tap - 1) for col_tap in range(3)]
        for row_tap in range(3):
            for col_tap in range(3):
                at = ((depth_tap * 3 + row_tap) * 3 + col_tap) * rows
                stack_ref[at : at + rows, :] = shift_cells(moved[col_tap], row_tap - 1, 0).astype(
                    jnp.bfloat16
                )
        at = depth_tap * 9 * rows
        grad = lax.dot_general(
            stack_ref[at : at + 9 * rows, :],
            x,
            (((1,), (1,)), ((), ())),
            preferred_element_type=jnp.float32,
        ).astype(jnp.bfloat16)
        for tap in range(9):
            for column in range(columns):
                unit = (depth_tap * 9 + tap) * columns + column
                wide_ref[unit // per, unit % per] = grad[
                    tap * rows : (tap + 1) * rows, column * LANES : (column + 1) * LANES
                ]
    for unit in range(TAPS * columns, slots * per):
        wide_ref[unit // per, unit % per] = jnp.zeros((rows, LANES), jnp.bfloat16)


def wgrad(place, above, own, below, mine, other, slots):
    rows, cells = own.shape
    chans = 2 * mine.shape[0] * mine.shape[1]
    per = -(-TAPS * chans // (LANES * slots))
    return pl.pallas_call(
        wgrad_kernel,
        out_shape=[
            jax.ShapeDtypeStruct((slots, per, rows, LANES), jnp.bfloat16),
            jax.ShapeDtypeStruct((TAPS * rows, cells), jnp.bfloat16),
        ],
        in_specs=merged_specs(5),
        scratch_shapes=merged_scratch(mine),
        compiler_params=pltpu.CompilerParams(vmem_limit_bytes=VMEM_LIMIT),
        name="wgrad",
    )(place, above, own, below, mine, other)


def dgrad_kernel(place_ref, k_ref, stack_ref, keep_ref, send_ref):
    rows = keep_ref.shape[2]
    partial = lax.dot_general(
        k_ref[...], stack_ref[...], (((0,), (0,)), ((), ())), preferred_element_type=jnp.float32
    )
    first = place_ref[0] == 0
    for x_at in range(4):
        for z_at in range(3):
            x_slot = x_at ^ place_ref[1]
            z_slot = lax.rem(z_at - place_ref[2] + 3, 3)
            at = (x_at * 3 + z_at) * 2 * rows
            even, odd = partial[at : at + rows], partial[at + rows : at + 2 * rows]
            keep_ref[x_slot, z_slot] = jnp.where(first, even, odd)
            send_ref[x_slot, z_slot] = jnp.where(first, odd, even).astype(jnp.bfloat16)


def dgrad(place, k_rows, stack):
    shape = (4, 3, k_rows.shape[0] // TAPS, stack.shape[1])
    return pl.pallas_call(
        dgrad_kernel,
        out_shape=[
            jax.ShapeDtypeStruct(shape, jnp.float32),
            jax.ShapeDtypeStruct(shape, jnp.bfloat16),
        ],
        in_specs=merged_specs(2),
        compiler_params=pltpu.CompilerParams(vmem_limit_bytes=VMEM_LIMIT),
        name="dgrad",
    )(place, k_rows, stack)


def act_kernel(mid_ref, low_ref, high_ref, cot_ref, act_ref, grad_ref):
    preact = mid_ref[...] + low_ref[...] + high_ref[...]
    sig = jax.nn.sigmoid(preact)
    act_ref[...] = (preact * sig).astype(jnp.bfloat16)
    cot = cot_ref[...].astype(jnp.float32)
    grad_ref[...] = (cot * sig * (1.0 + preact * (1.0 - sig))).astype(jnp.bfloat16)


def activate(mid, low, high, cot):
    shape = jax.ShapeDtypeStruct(mid.shape, jnp.bfloat16)
    return pl.pallas_call(
        act_kernel,
        out_shape=[shape, shape],
        compiler_params=pltpu.CompilerParams(vmem_limit_bytes=VMEM_LIMIT),
        name="activate",
    )(mid, low, high, cot)


def total_kernel(terms_ref, out_ref, *, scale):
    total = jnp.sum(terms_ref[...].astype(jnp.float32), axis=0) * scale
    out_ref[...] = jnp.broadcast_to(total.astype(jnp.bfloat16)[None], out_ref.shape)


def total_spread(terms, scale, copies):
    return pl.pallas_call(
        functools.partial(total_kernel, scale=scale),
        out_shape=jax.ShapeDtypeStruct((copies,) + terms.shape[1:], jnp.bfloat16),
        compiler_params=pltpu.CompilerParams(vmem_limit_bytes=VMEM_LIMIT),
        name="total",
    )(terms)


def halve_kernel(kept_ref, came_ref, keep_ref, send_ref):
    for at in range(keep_ref.shape[0]):
        keep_ref[at] = kept_ref[2 * at] + came_ref[2 * at].astype(jnp.float32)
        total = kept_ref[2 * at + 1] + came_ref[2 * at + 1].astype(jnp.float32)
        send_ref[at] = total.astype(jnp.bfloat16)


def halve(kept, came):
    shape = (kept.shape[0] // 2,) + kept.shape[1:]
    return pl.pallas_call(
        halve_kernel,
        out_shape=[
            jax.ShapeDtypeStruct(shape, jnp.float32),
            jax.ShapeDtypeStruct(shape, jnp.bfloat16),
        ],
        compiler_params=pltpu.CompilerParams(vmem_limit_bytes=VMEM_LIMIT),
        name="halve",
    )(kept, came)


def unpack_kernel(units_ref, out_ref):
    per = units_ref.shape[1]
    columns = out_ref.shape[2] // LANES
    for tap in range(TAPS):
        for column in range(columns):
            unit = tap * columns + column
            block = units_ref[unit // per, unit % per].astype(jnp.float32)
            out_ref[tap, :, column * LANES : (column + 1) * LANES] = block


def unpack(units, chans):
    return pl.pallas_call(
        unpack_kernel,
        out_shape=jax.ShapeDtypeStruct((TAPS, units.shape[2], chans), jnp.float32),
        compiler_params=pltpu.CompilerParams(vmem_limit_bytes=VMEM_LIMIT),
        name="unpack",
    )(units)


def swap_cores(blocks):
    return lax.ppermute(blocks, "core", [(0, 1), (1, 0)])


def body(volume, kernel, cotangent):
    rows = volume.shape[2]
    cells = volume.shape[3]
    chips = lax.axis_size(CHIPS)
    depths = lax.axis_size(DEP)
    ring = [(i, (i + 1) % depths) for i in range(depths)]
    back = [(b, a) for a, b in ring]
    place = jnp.stack([lax.axis_index(name) for name in ("core", "x", "zl")]).astype(jnp.int32)
    own = volume.reshape(rows, cells)
    cot = cotangent.reshape(rows, cells)

    def copies(block):
        return jnp.broadcast_to(block[None], (chips, rows, cells))

    mine = lax.all_to_all(copies(own), CHIPS, 0, 0)
    k_rows = jnp.transpose(kernel.reshape(rows, TAPS, -1), (1, 0, 2)).reshape(TAPS * rows, -1)
    mine, k_rows, cot, place = lax.optimization_barrier((mine, k_rows, cot, place))
    other = swap_cores(mine)

    up, mid, down = conv(place, k_rows, mine, other, 1)
    low = lax.ppermute(up, DEP, ring)
    high = lax.ppermute(down, DEP, back)
    activated, grad_pre = activate(mid, low, high, cot)

    grad_above = lax.ppermute(grad_pre, DEP, back)
    grad_below = lax.ppermute(grad_pre, DEP, ring)
    ys, zs = lax.axis_size("y"), lax.axis_size("zh")
    wide, stack = wgrad(place, grad_above, grad_pre, grad_below, mine, other, ys)
    scale = 1.0 / math.sqrt(UNIV * DEPTH * SIDE * SIDE)
    over_y = lax.all_to_all(wide, "y", 0, 0)

    keep, send = dgrad(place, k_rows, stack)
    keep, send = halve(keep, swap_cores(send))
    over_y, keep = lax.optimization_barrier((over_y, keep))
    over_z = lax.all_to_all(total_spread(over_y, 1.0, zs), "zh", 0, 0)
    total = keep + lax.ppermute(send, "x", [(i, i ^ 1) for i in range(4)]).astype(jnp.float32)
    over_z, _ = lax.optimization_barrier((over_z, total))
    units = lax.all_to_all(total_spread(over_z, scale, ys), "y", 0, 0)
    step = lax.ppermute(total[1].astype(jnp.bfloat16), "x", [(i, i ^ 2) for i in range(4)])
    total = total[0] + step.astype(jnp.float32)
    after = lax.ppermute(total[1], "zl", [(i, (i + 1) % 3) for i in range(3)])
    before = lax.ppermute(total[2], "zl", [(i, (i + 2) % 3) for i in range(3)])
    grad_volume = (total[0] + after + before).astype(jnp.bfloat16)
    all_taps = unpack(units, kernel.shape[-1])
    grad_kernel = jnp.transpose(all_taps, (1, 0, 2)).reshape(kernel.shape)
    return (activated.reshape(volume.shape), grad_volume.reshape(volume.shape), grad_kernel)


def solution(mesh):
    fine = Mesh(mesh.devices.reshape(8, 4, 4, 3, 2), ("y", "zh", "x", "zl", "core"))
    field = P(None, DEP, CHAN, None)
    weight = P(CHAN, None, None, None, None)
    return jax.shard_map(
        body,
        mesh=fine,
        in_specs=(field, weight, field),
        out_specs=(field, field, weight),
        check_vma=False,
    )
```

```python
import functools
import math

import jax
import jax.numpy as jnp
from jax import lax
from jax.experimental import pallas as pl
from jax.experimental.pallas import tpu as pltpu
from jax.sharding import Mesh
from jax.sharding import PartitionSpec as P

DEPTH = 32
SIDE = 32
UNIV = 1
TAPS = 27
LANES = 128
VMEM_LIMIT = 48 * 1024 * 1024
DEP = ("y", "zh")
CHIPS = ("x", "zl")
CHAN = ("x", "zl", "core")


def shift_cells(plane, row_step, col_step):
    cells = plane.shape[-1]
    if col_step:
        columns = lax.broadcasted_iota(jnp.int32, plane.shape, 1) % SIDE
        edge = 0 if col_step > 0 else SIDE - 1
        plain = pltpu.roll(plane, col_step % cells, 1)
        wrapped = pltpu.roll(plane, (col_step - col_step * SIDE) % cells, 1)
        plane = jnp.where(columns == edge, wrapped, plain)
    if row_step:
        plane = pltpu.roll(plane, (row_step * SIDE) % cells, 1)
    return plane


def merge_cores(core_ref, mine_ref, other_ref, x_ref):
    first = core_ref[0] == 0
    mine, other = mine_ref[...], other_ref[...]
    x_ref[:, 0] = jnp.where(first, mine, other)
    x_ref[:, 1] = jnp.where(first, other, mine)
    return x_ref[...].reshape(-1, x_ref.shape[-1])


def conv_kernel(core_ref, odd_ref, w_ref, mine_ref, other_ref, near_ref, mid_ref, far_ref, x_ref):
    rows = mid_ref.shape[0]
    x = merge_cores(core_ref, mine_ref, other_ref, x_ref)
    sums = []
    for depth_tap in range(3):
        w = w_ref[depth_tap * 9 * rows : (depth_tap + 1) * 9 * rows, :]
        product = jnp.dot(w, x, preferred_element_type=jnp.float32)
        total = None
        for col_tap in range(3):
            part = None
            for row_tap in range(3):
                at = (row_tap * 3 + col_tap) * rows
                term = shift_cells(product[at : at + rows], 1 - row_tap, 0)
                part = term if part is None else part + term
            part = shift_cells(part, 0, 1 - col_tap)
            total = part if total is None else total + part
        sums.append(total)
    up, mid, down = sums
    odd = odd_ref[0] == 1
    near_ref[...] = jnp.where(odd, down, up)
    mid_ref[...] = mid
    far_ref[...] = jnp.where(odd, up, down)


def specs(scalars, arrays):
    smem = pl.BlockSpec(memory_space=pltpu.SMEM)
    return [smem] * scalars + [pl.BlockSpec(memory_space=pltpu.VMEM)] * arrays


def merged_scratch(mine):
    return [pltpu.VMEM((mine.shape[0], 2) + mine.shape[1:], mine.dtype)]


def conv(core, odd, weights, mine, other):
    rows = weights.shape[0] // TAPS
    cells = mine.shape[-1]
    return pl.pallas_call(
        conv_kernel,
        out_shape=[jax.ShapeDtypeStruct((rows, cells), jnp.float32)] * 3,
        in_specs=specs(2, 3),
        scratch_shapes=merged_scratch(mine),
        compiler_params=pltpu.CompilerParams(vmem_limit_bytes=VMEM_LIMIT),
        name="conv",
    )(core, odd, weights, mine, other)


def stack_plane(plane, stack_ref, at):
    rows = plane.shape[0]
    plane = plane.astype(jnp.float32)
    moved = [shift_cells(plane, 0, col_tap - 1) for col_tap in range(3)]
    for row_tap in range(3):
        for col_tap in range(3):
            stack_ref[at : at + rows, :] = shift_cells(moved[col_tap], row_tap - 1, 0).astype(
                jnp.bfloat16
            )
            at += rows


def cross(stack, x):
    return lax.dot_general(
        stack, x, (((1,), (1,)), ((), ())), preferred_element_type=jnp.float32
    ).astype(jnp.bfloat16)


def own_kernel(core_ref, own_ref, mine_ref, other_ref, units_ref, stack_ref, x_ref):
    rows = own_ref.shape[0]
    x = merge_cores(core_ref, mine_ref, other_ref, x_ref)
    columns = x.shape[0] // LANES
    stack_plane(own_ref[...], stack_ref, 0)
    grad = cross(stack_ref[...], x)
    for unit in range(9 * columns):
        tap, column = divmod(unit, columns)
        units_ref[unit] = grad[
            tap * rows : (tap + 1) * rows, column * LANES : (column + 1) * LANES
        ]


def wgrad_own(core, own, mine, other):
    rows, cells = own.shape
    chans = 2 * mine.shape[0] * mine.shape[1]
    return pl.pallas_call(
        own_kernel,
        out_shape=[
            jax.ShapeDtypeStruct((9 * chans // LANES, rows, LANES), jnp.bfloat16),
            jax.ShapeDtypeStruct((9 * rows, cells), jnp.bfloat16),
            jax.ShapeDtypeStruct((mine.shape[0], 2) + mine.shape[1:], mine.dtype),
        ],
        in_specs=specs(1, 3),
        compiler_params=pltpu.CompilerParams(vmem_limit_bytes=VMEM_LIMIT),
        name="wgrad_own",
    )(core, own, mine, other)


def halo_kernel(odd_ref, near_ref, far_ref, x_ref, units_ref, wide_ref, stack_ref):
    rows = near_ref.shape[0]
    slots, per = wide_ref.shape[:2]
    x = x_ref[...].reshape(-1, x_ref.shape[-1])
    columns = x.shape[0] // LANES
    odd = odd_ref[0] == 1
    near, far = near_ref[...].astype(jnp.float32), far_ref[...].astype(jnp.float32)
    for half, plane in enumerate((jnp.where(odd, far, near), jnp.where(odd, near, far))):
        stack_plane(plane, stack_ref, half * 9 * rows)
        grad = cross(stack_ref[half * 9 * rows : (half + 1) * 9 * rows, :], x)
        for at in range(9 * columns):
            tap, column = divmod(at, columns)
            unit = 18 * half * columns + at
            wide_ref[unit // per, unit % per] = grad[
                tap * rows : (tap + 1) * rows, column * LANES : (column + 1) * LANES
            ]
    for at in range(9 * columns):
        unit = 9 * columns + at
        wide_ref[unit // per, unit % per] = units_ref[at]
    for unit in range(TAPS * columns, slots * per):
        wide_ref[unit // per, unit % per] = jnp.zeros((rows, LANES), jnp.bfloat16)


def wgrad_halo(odd, near, far, x, units, slots):
    rows, cells = near.shape
    per = -(-3 * units.shape[0] // slots)
    return pl.pallas_call(
        halo_kernel,
        out_shape=[
            jax.ShapeDtypeStruct((slots, per, rows, LANES), jnp.bfloat16),
            jax.ShapeDtypeStruct((18 * rows, cells), jnp.bfloat16),
        ],
        in_specs=specs(1, 4),
        compiler_params=pltpu.CompilerParams(vmem_limit_bytes=VMEM_LIMIT),
        name="wgrad_halo",
    )(odd, near, far, x, units)


def dgrad_kernel(core_ref, x_at_ref, z_at_ref, k_ref, own_ref, halo_ref, keep_ref, send_ref):
    rows = keep_ref.shape[2]
    n = 9 * rows
    partial = None
    for at, stack in ((0, halo_ref[:n, :]), (n, own_ref[...]), (2 * n, halo_ref[n:, :])):
        term = lax.dot_general(
            k_ref[at : at + n, :],
            stack,
            (((0,), (0,)), ((), ())),
            preferred_element_type=jnp.float32,
        )
        partial = term if partial is None else partial + term
    first = core_ref[0] == 0
    for x_at in range(4):
        for z_at in range(3):
            x_slot = x_at ^ x_at_ref[0]
            z_slot = lax.rem(z_at - z_at_ref[0] + 3, 3)
            at = (x_at * 3 + z_at) * 2 * rows
            even, odd = partial[at : at + rows], partial[at + rows : at + 2 * rows]
            keep_ref[z_slot, x_slot] = jnp.where(first, even, odd)
            send_ref[z_slot, x_slot] = jnp.where(first, odd, even).astype(jnp.bfloat16)


def dgrad(core, x_at, z_at, k_rows, own, halo):
    shape = (3, 4, k_rows.shape[0] // TAPS, own.shape[1])
    return pl.pallas_call(
        dgrad_kernel,
        out_shape=[
            jax.ShapeDtypeStruct(shape, jnp.float32),
            jax.ShapeDtypeStruct(shape, jnp.bfloat16),
        ],
        in_specs=specs(3, 3),
        compiler_params=pltpu.CompilerParams(vmem_limit_bytes=VMEM_LIMIT),
        name="dgrad",
    )(core, x_at, z_at, k_rows, own, halo)


def act_kernel(mid_ref, low_ref, high_ref, cot_ref, act_ref, grad_ref):
    preact = mid_ref[...] + low_ref[...] + high_ref[...]
    sig = jax.nn.sigmoid(preact)
    act_ref[...] = (preact * sig).astype(jnp.bfloat16)
    cot = cot_ref[...].astype(jnp.float32)
    grad_ref[...] = (cot * sig * (1.0 + preact * (1.0 - sig))).astype(jnp.bfloat16)


def activate(mid, low, high, cot):
    shape = jax.ShapeDtypeStruct(mid.shape, jnp.bfloat16)
    return pl.pallas_call(
        act_kernel,
        out_shape=[shape, shape],
        compiler_params=pltpu.CompilerParams(vmem_limit_bytes=VMEM_LIMIT),
        name="activate",
    )(mid, low, high, cot)


def total_kernel(terms_ref, out_ref, *, scale):
    total = jnp.sum(terms_ref[...].astype(jnp.float32), axis=0) * scale
    out_ref[...] = jnp.broadcast_to(total.astype(jnp.bfloat16)[None], out_ref.shape)


def total_spread(terms, scale, copies):
    return pl.pallas_call(
        functools.partial(total_kernel, scale=scale),
        out_shape=jax.ShapeDtypeStruct((copies,) + terms.shape[1:], jnp.bfloat16),
        compiler_params=pltpu.CompilerParams(vmem_limit_bytes=VMEM_LIMIT),
        name="total",
    )(terms)


def part_kernel(kept_ref, came_ref, here_ref, after_ref, before_ref):
    here_ref[...] = kept_ref[0] + came_ref[0].astype(jnp.float32)
    after_ref[...] = (kept_ref[1] + came_ref[1].astype(jnp.float32)).astype(jnp.bfloat16)
    before_ref[...] = (kept_ref[2] + came_ref[2].astype(jnp.float32)).astype(jnp.bfloat16)


def part(kept, came):
    return pl.pallas_call(
        part_kernel,
        out_shape=[
            jax.ShapeDtypeStruct(kept.shape[1:], kind)
            for kind in (jnp.float32, jnp.bfloat16, jnp.bfloat16)
        ],
        compiler_params=pltpu.CompilerParams(vmem_limit_bytes=VMEM_LIMIT),
        name="part",
    )(kept, came)


def unpack_kernel(units_ref, out_ref):
    per = units_ref.shape[1]
    columns = out_ref.shape[2] // LANES
    for tap in range(TAPS):
        for column in range(columns):
            unit = tap * columns + column
            block = units_ref[unit // per, unit % per].astype(jnp.float32)
            out_ref[tap, :, column * LANES : (column + 1) * LANES] = block


def unpack(units, chans):
    return pl.pallas_call(
        unpack_kernel,
        out_shape=jax.ShapeDtypeStruct((TAPS, units.shape[2], chans), jnp.float32),
        compiler_params=pltpu.CompilerParams(vmem_limit_bytes=VMEM_LIMIT),
        name="unpack",
    )(units)


def swap_cores(blocks):
    return lax.ppermute(blocks, "core", [(0, 1), (1, 0)])


def body(volume, kernel, cotangent):
    rows = volume.shape[2]
    cells = volume.shape[3]
    chips = lax.axis_size(CHIPS)
    depths = lax.axis_size(DEP)
    near_pairs = [(i, i ^ 1) for i in range(depths)]
    far_pairs = [(i, (i + 1 if i % 2 else i - 1) % depths) for i in range(depths)]

    def index(name):
        return lax.axis_index(name).astype(jnp.int32).reshape(1)

    core, x_at, z_at, odd = index("core"), index("x"), index("zl"), index("zh") % 2
    own = volume.reshape(rows, cells)
    cot = cotangent.reshape(rows, cells)

    def copies(block):
        return jnp.broadcast_to(block[None], (chips, rows, cells))

    mine = lax.all_to_all(copies(own), CHIPS, 0, 0)
    k_rows = jnp.transpose(kernel.reshape(rows, TAPS, -1), (1, 0, 2)).reshape(TAPS * rows, -1)
    mine, k_rows, cot, core, odd, x_at, z_at = lax.optimization_barrier(
        (mine, k_rows, cot, core, odd, x_at, z_at)
    )
    other = swap_cores(mine)

    near, mid, far = conv(core, odd, k_rows, mine, other)
    near = lax.ppermute(near, DEP, near_pairs)
    far = lax.ppermute(far, DEP, far_pairs)
    activated, grad_pre = activate(mid, near, far, cot)

    near_grad = lax.ppermute(grad_pre, DEP, near_pairs)
    far_grad = lax.ppermute(grad_pre, DEP, far_pairs)
    own_units, own_stack, x = wgrad_own(core, grad_pre, mine, other)
    ys, zs = lax.axis_size("y"), lax.axis_size("zh")
    wide, halo_stack = wgrad_halo(odd, near_grad, far_grad, x, own_units, ys)
    scale = 1.0 / math.sqrt(UNIV * DEPTH * SIDE * SIDE)
    over_y = lax.all_to_all(wide, "y", 0, 0)

    keep, send = dgrad(core, x_at, z_at, k_rows, own_stack, halo_stack)
    here, after, before = part(keep, swap_cores(send))
    over_y, here = lax.optimization_barrier((over_y, here))
    over_z = lax.all_to_all(total_spread(over_y, 1.0, zs), "zh", 0, 0)
    after = lax.ppermute(after, "zl", [(i, (i + 1) % 3) for i in range(3)])
    before = lax.ppermute(before, "zl", [(i, (i + 2) % 3) for i in range(3)])
    total = here + after.astype(jnp.float32) + before.astype(jnp.float32)
    total = total.reshape(2, 2, rows, cells)
    over_z, _ = lax.optimization_barrier((over_z, total))
    units = lax.all_to_all(total_spread(over_z, scale, ys), "y", 0, 0)
    step = lax.ppermute(total[:, 1].astype(jnp.bfloat16), "x", [(i, i ^ 1) for i in range(4)])
    total = total[:, 0] + step.astype(jnp.float32)
    step = lax.ppermute(total[1].astype(jnp.bfloat16), "x", [(i, i ^ 2) for i in range(4)])
    grad_volume = (total[0] + step.astype(jnp.float32)).astype(jnp.bfloat16)
    all_taps = unpack(units, kernel.shape[-1])
    grad_kernel = jnp.transpose(all_taps, (1, 0, 2)).reshape(kernel.shape)
    return (activated.reshape(volume.shape), grad_volume.reshape(volume.shape), grad_kernel)


def solution(mesh):
    fine = Mesh(mesh.devices.reshape(8, 4, 4, 3, 2), ("y", "zh", "x", "zl", "core"))
    field = P(None, DEP, CHAN, None)
    weight = P(CHAN, None, None, None, None)
    return jax.shard_map(
        body,
        mesh=fine,
        in_specs=(field, weight, field),
        out_specs=(field, field, weight),
        check_vma=False,
    )
```

```python
import functools
import math

import jax
import jax.numpy as jnp
from jax import lax
from jax.experimental import pallas as pl
from jax.experimental.pallas import tpu as pltpu
from jax.sharding import Mesh
from jax.sharding import PartitionSpec as P

DEPTH = 32
SIDE = 32
UNIV = 1
TAPS = 27
LANES = 128
VMEM_LIMIT = 48 * 1024 * 1024
DEP = ("y", "zh")
CHIPS = ("x", "zl")
CHAN = ("x", "zl", "core")


def shift_cells(plane, row_step, col_step):
    cells = plane.shape[-1]
    if col_step:
        columns = lax.broadcasted_iota(jnp.int32, plane.shape, 1) % SIDE
        edge = 0 if col_step > 0 else SIDE - 1
        plain = pltpu.roll(plane, col_step % cells, 1)
        wrapped = pltpu.roll(plane, (col_step - col_step * SIDE) % cells, 1)
        plane = jnp.where(columns == edge, wrapped, plain)
    if row_step:
        plane = pltpu.roll(plane, (row_step * SIDE) % cells, 1)
    return plane


def merge_cores(core_ref, mine_ref, other_ref, x_ref):
    first = core_ref[0] == 0
    mine, other = mine_ref[...], other_ref[...]
    x_ref[:, 0] = jnp.where(first, mine, other)
    x_ref[:, 1] = jnp.where(first, other, mine)
    return x_ref[...].reshape(-1, x_ref.shape[-1])


def conv_kernel(
    core_ref, w_ref, mine_ref, other_ref, own_ref, next_ref, prev_ref, next2_ref, prev2_ref, x_ref
):
    rows = next2_ref.shape[0]
    x = merge_cores(core_ref, mine_ref, other_ref, x_ref)
    for depth_tap in range(3):
        w = w_ref[depth_tap * 9 * rows : (depth_tap + 1) * 9 * rows, :]
        product = jnp.dot(w, x, preferred_element_type=jnp.float32)
        total = None
        for col_tap in range(3):
            part = None
            for row_tap in range(3):
                at = (row_tap * 3 + col_tap) * rows
                term = shift_cells(product[at : at + rows], 1 - row_tap, 0)
                part = term if part is None else part + term
            part = shift_cells(part, 0, 1 - col_tap)
            total = part if total is None else total + part
        own_ref[depth_tap] = total
        narrow = total.astype(jnp.bfloat16)
        if depth_tap < 2:
            next_ref[depth_tap] = narrow
        if depth_tap > 0:
            prev_ref[depth_tap - 1] = narrow
        if depth_tap == 0:
            next2_ref[...] = narrow
        if depth_tap == 2:
            prev2_ref[...] = narrow


def specs(scalars, arrays):
    smem = pl.BlockSpec(memory_space=pltpu.SMEM)
    return [smem] * scalars + [pl.BlockSpec(memory_space=pltpu.VMEM)] * arrays


def conv(core, weights, mine, other):
    rows = weights.shape[0] // TAPS
    cells = mine.shape[-1]
    one, two = (rows, cells), (2, rows, cells)
    return pl.pallas_call(
        conv_kernel,
        out_shape=[
            jax.ShapeDtypeStruct((3, rows, cells), jnp.float32),
            jax.ShapeDtypeStruct(two, jnp.bfloat16),
            jax.ShapeDtypeStruct(two, jnp.bfloat16),
            jax.ShapeDtypeStruct(one, jnp.bfloat16),
            jax.ShapeDtypeStruct(one, jnp.bfloat16),
            jax.ShapeDtypeStruct((mine.shape[0], 2) + mine.shape[1:], mine.dtype),
        ],
        in_specs=specs(1, 3),
        compiler_params=pltpu.CompilerParams(vmem_limit_bytes=VMEM_LIMIT),
        name="conv",
    )(core, weights, mine, other)


def stack_plane(plane, stack_ref, at):
    rows = plane.shape[0]
    plane = plane.astype(jnp.float32)
    moved = [shift_cells(plane, 0, col_tap - 1) for col_tap in range(3)]
    for row_tap in range(3):
        for col_tap in range(3):
            stack_ref[at : at + rows, :] = shift_cells(moved[col_tap], row_tap - 1, 0).astype(
                jnp.bfloat16
            )
            at += rows


def cross(stack, x):
    return lax.dot_general(
        stack, x, (((1,), (1,)), ((), ())), preferred_element_type=jnp.float32
    ).astype(jnp.bfloat16)


def grads_kernel(
    own_ref, prev_ref, next_ref, prev2_ref, next2_ref, cot_ref, cot_prev_ref, cot_next_ref, x_ref,
    act_ref, wide_ref, stack_ref,
):
    rows = act_ref.shape[0]
    slots, per = wide_ref.shape[:2]
    x = x_ref[...].reshape(-1, x_ref.shape[-1])
    columns = x.shape[0] // LANES
    f32 = jnp.float32
    above = own_ref[0] + next_ref[0].astype(f32) + next2_ref[...].astype(f32)
    here = own_ref[1] + prev_ref[0].astype(f32) + next_ref[1].astype(f32)
    below = own_ref[2] + prev_ref[1].astype(f32) + prev2_ref[...].astype(f32)
    planes = ((above, cot_next_ref), (here, cot_ref), (below, cot_prev_ref))
    for depth_tap, (preact, cotangent_ref) in enumerate(planes):
        sig = jax.nn.sigmoid(preact)
        if depth_tap == 1:
            act_ref[...] = (preact * sig).astype(jnp.bfloat16)
        cot = cotangent_ref[...].astype(f32)
        grad_pre = (cot * sig * (1.0 + preact * (1.0 - sig))).astype(jnp.bfloat16)
        at = depth_tap * 9 * rows
        stack_plane(grad_pre, stack_ref, at)
        grad = cross(stack_ref[at : at + 9 * rows, :], x)
        for index in range(9 * columns):
            tap, column = divmod(index, columns)
            unit = depth_tap * 9 * columns + index
            wide_ref[unit // per, unit % per] = grad[
                tap * rows : (tap + 1) * rows, column * LANES : (column + 1) * LANES
            ]
    for unit in range(TAPS * columns, slots * per):
        wide_ref[unit // per, unit % per] = jnp.zeros((rows, LANES), jnp.bfloat16)


def grads(sums, cots, x, slots):
    rows, cells = cots[0].shape
    per = -(-TAPS * 2 * x.shape[0] * rows // (LANES * slots))
    return pl.pallas_call(
        grads_kernel,
        out_shape=[
            jax.ShapeDtypeStruct((rows, cells), jnp.bfloat16),
            jax.ShapeDtypeStruct((slots, per, rows, LANES), jnp.bfloat16),
            jax.ShapeDtypeStruct((TAPS * rows, cells), jnp.bfloat16),
        ],
        compiler_params=pltpu.CompilerParams(vmem_limit_bytes=VMEM_LIMIT),
        name="grads",
    )(*sums, *cots, x)


def dgrad_kernel(core_ref, x_at_ref, z_at_ref, k_ref, stack_ref, keep_ref, send_ref):
    rows = keep_ref.shape[2]
    partial = lax.dot_general(
        k_ref[...], stack_ref[...], (((0,), (0,)), ((), ())), preferred_element_type=jnp.float32
    )
    first = core_ref[0] == 0
    for x_at in range(4):
        for z_at in range(3):
            x_slot = x_at ^ x_at_ref[0]
            z_slot = lax.rem(z_at - z_at_ref[0] + 3, 3)
            at = (x_at * 3 + z_at) * 2 * rows
            even, odd = partial[at : at + rows], partial[at + rows : at + 2 * rows]
            keep_ref[z_slot, x_slot] = jnp.where(first, even, odd)
            send_ref[z_slot, x_slot] = jnp.where(first, odd, even).astype(jnp.bfloat16)


def dgrad(core, x_at, z_at, k_rows, stack):
    shape = (3, 4, k_rows.shape[0] // TAPS, stack.shape[1])
    return pl.pallas_call(
        dgrad_kernel,
        out_shape=[
            jax.ShapeDtypeStruct(shape, jnp.float32),
            jax.ShapeDtypeStruct(shape, jnp.bfloat16),
        ],
        in_specs=specs(3, 2),
        compiler_params=pltpu.CompilerParams(vmem_limit_bytes=VMEM_LIMIT),
        name="dgrad",
    )(core, x_at, z_at, k_rows, stack)


def total_kernel(terms_ref, out_ref, *, scale):
    total = jnp.sum(terms_ref[...].astype(jnp.float32), axis=0) * scale
    out_ref[...] = jnp.broadcast_to(total.astype(jnp.bfloat16)[None], out_ref.shape)


def total_spread(terms, scale, copies):
    return pl.pallas_call(
        functools.partial(total_kernel, scale=scale),
        out_shape=jax.ShapeDtypeStruct((copies,) + terms.shape[1:], jnp.bfloat16),
        compiler_params=pltpu.CompilerParams(vmem_limit_bytes=VMEM_LIMIT),
        name="total",
    )(terms)


def part_kernel(kept_ref, came_ref, here_ref, after_ref, before_ref):
    here_ref[...] = kept_ref[0] + came_ref[0].astype(jnp.float32)
    after_ref[...] = (kept_ref[1] + came_ref[1].astype(jnp.float32)).astype(jnp.bfloat16)
    before_ref[...] = (kept_ref[2] + came_ref[2].astype(jnp.float32)).astype(jnp.bfloat16)


def part(kept, came):
    return pl.pallas_call(
        part_kernel,
        out_shape=[
            jax.ShapeDtypeStruct(kept.shape[1:], kind)
            for kind in (jnp.float32, jnp.bfloat16, jnp.bfloat16)
        ],
        compiler_params=pltpu.CompilerParams(vmem_limit_bytes=VMEM_LIMIT),
        name="part",
    )(kept, came)


def unpack_kernel(units_ref, out_ref):
    per = units_ref.shape[1]
    columns = out_ref.shape[2] // LANES
    for tap in range(TAPS):
        for column in range(columns):
            unit = tap * columns + column
            block = units_ref[unit // per, unit % per].astype(jnp.float32)
            out_ref[tap, :, column * LANES : (column + 1) * LANES] = block


def unpack(units, chans):
    return pl.pallas_call(
        unpack_kernel,
        out_shape=jax.ShapeDtypeStruct((TAPS, units.shape[2], chans), jnp.float32),
        compiler_params=pltpu.CompilerParams(vmem_limit_bytes=VMEM_LIMIT),
        name="unpack",
    )(units)


def swap_cores(blocks):
    return lax.ppermute(blocks, "core", [(0, 1), (1, 0)])


def body(volume, kernel, cotangent):
    rows = volume.shape[2]
    cells = volume.shape[3]
    chips = lax.axis_size(CHIPS)
    depths = lax.axis_size(DEP)

    def shift(block, step):
        return lax.ppermute(block, DEP, [(i, (i + step) % depths) for i in range(depths)])

    def index(name):
        return lax.axis_index(name).astype(jnp.int32).reshape(1)

    core, x_at, z_at = index("core"), index("x"), index("zl")
    own = volume.reshape(rows, cells)
    cot = cotangent.reshape(rows, cells)

    def copies(block):
        return jnp.broadcast_to(block[None], (chips, rows, cells))

    mine = lax.all_to_all(copies(own), CHIPS, 0, 0)
    k_rows = jnp.transpose(kernel.reshape(rows, TAPS, -1), (1, 0, 2)).reshape(TAPS * rows, -1)
    cot_next, cot_prev = shift(cot, -1), shift(cot, 1)
    mine, k_rows, cot, cot_next, cot_prev, core, x_at, z_at = lax.optimization_barrier(
        (mine, k_rows, cot, cot_next, cot_prev, core, x_at, z_at)
    )
    other = swap_cores(mine)

    sums, to_next, to_prev, to_next2, to_prev2, x = conv(core, k_rows, mine, other)
    sums = (sums, shift(to_next, 1), shift(to_prev, -1), shift(to_next2, 2), shift(to_prev2, -2))
    ys, zs = lax.axis_size("y"), lax.axis_size("zh")
    activated, wide, stack = grads(sums, (cot, cot_prev, cot_next), x, ys)
    scale = 1.0 / math.sqrt(UNIV * DEPTH * SIDE * SIDE)
    over_y = lax.all_to_all(wide, "y", 0, 0)

    keep, send = dgrad(core, x_at, z_at, k_rows, stack)
    here, after, before = part(keep, swap_cores(send))
    over_y, here = lax.optimization_barrier((over_y, here))
    over_z = lax.all_to_all(total_spread(over_y, 1.0, zs), "zh", 0, 0)
    after = lax.ppermute(after, "zl", [(i, (i + 1) % 3) for i in range(3)])
    before = lax.ppermute(before, "zl", [(i, (i + 2) % 3) for i in range(3)])
    total = here + after.astype(jnp.float32) + before.astype(jnp.float32)
    total = total.reshape(2, 2, rows, cells)
    over_z, _ = lax.optimization_barrier((over_z, total))
    units = lax.all_to_all(total_spread(over_z, scale, ys), "y", 0, 0)
    step = lax.ppermute(total[:, 1].astype(jnp.bfloat16), "x", [(i, i ^ 1) for i in range(4)])
    total = total[:, 0] + step.astype(jnp.float32)
    step = lax.ppermute(total[1].astype(jnp.bfloat16), "x", [(i, i ^ 2) for i in range(4)])
    grad_volume = (total[0] + step.astype(jnp.float32)).astype(jnp.bfloat16)
    all_taps = unpack(units, kernel.shape[-1])
    grad_kernel = jnp.transpose(all_taps, (1, 0, 2)).reshape(kernel.shape)
    return (activated.reshape(volume.shape), grad_volume.reshape(volume.shape), grad_kernel)


def solution(mesh):
    fine = Mesh(mesh.devices.reshape(8, 4, 4, 3, 2), ("y", "zh", "x", "zl", "core"))
    field = P(None, DEP, CHAN, None)
    weight = P(CHAN, None, None, None, None)
    return jax.shard_map(
        body,
        mesh=fine,
        in_specs=(field, weight, field),
        out_specs=(field, field, weight),
        check_vma=False,
    )
```

```python
import functools
import math

import jax
import jax.numpy as jnp
from jax import lax
from jax.experimental import pallas as pl
from jax.experimental.pallas import tpu as pltpu
from jax.sharding import Mesh
from jax.sharding import PartitionSpec as P

DEPTH = 32
SIDE = 32
UNIV = 1
TAPS = 27
LANES = 128
VMEM_LIMIT = 48 * 1024 * 1024
DEP = ("y", "zh")
CHIPS = ("x", "zl")
CHAN = ("x", "zl", "core")


def shift_cells(plane, row_step, col_step):
    cells = plane.shape[-1]
    if col_step:
        columns = lax.broadcasted_iota(jnp.int32, plane.shape, 1) % SIDE
        edge = 0 if col_step > 0 else SIDE - 1
        plain = pltpu.roll(plane, col_step % cells, 1)
        wrapped = pltpu.roll(plane, (col_step - col_step * SIDE) % cells, 1)
        plane = jnp.where(columns == edge, wrapped, plain)
    if row_step:
        plane = pltpu.roll(plane, (row_step * SIDE) % cells, 1)
    return plane


def merge_cores(core_ref, mine_ref, other_ref, x_ref):
    first = core_ref[0] == 0
    mine, other = mine_ref[...], other_ref[...]
    x_ref[:, 0] = jnp.where(first, mine, other)
    x_ref[:, 1] = jnp.where(first, other, mine)
    return x_ref[...].reshape(-1, x_ref.shape[-1])


def conv_kernel(core_ref, w_ref, mine_ref, other_ref, *refs):
    outs, x_ref = refs[:3], refs[3]
    rows = outs[0].shape[0]
    x = merge_cores(core_ref, mine_ref, other_ref, x_ref)
    for depth_tap in range(3):
        w = w_ref[depth_tap * 9 * rows : (depth_tap + 1) * 9 * rows, :]
        product = jnp.dot(w, x, preferred_element_type=jnp.float32)
        total = None
        for col_tap in range(3):
            part = None
            for row_tap in range(3):
                at = (row_tap * 3 + col_tap) * rows
                term = shift_cells(product[at : at + rows], 1 - row_tap, 0)
                part = term if part is None else part + term
            part = shift_cells(part, 0, 1 - col_tap)
            total = part if total is None else total + part
        outs[depth_tap][...] = total.astype(outs[depth_tap].dtype)


def specs(scalars, arrays):
    smem = pl.BlockSpec(memory_space=pltpu.SMEM)
    return [smem] * scalars + [pl.BlockSpec(memory_space=pltpu.VMEM)] * arrays


def merged_scratch(mine):
    return [pltpu.VMEM((mine.shape[0], 2) + mine.shape[1:], mine.dtype)]


def conv(core, weights, mine, other):
    rows = weights.shape[0] // TAPS
    cells = mine.shape[-1]
    return pl.pallas_call(
        conv_kernel,
        out_shape=[
            jax.ShapeDtypeStruct((rows, cells), kind)
            for kind in (jnp.bfloat16, jnp.float32, jnp.bfloat16)
        ],
        in_specs=specs(1, 3),
        scratch_shapes=merged_scratch(mine),
        compiler_params=pltpu.CompilerParams(vmem_limit_bytes=VMEM_LIMIT),
        name="conv",
    )(core, weights, mine, other)


def stack_plane(plane, stack_ref, at):
    rows = plane.shape[0]
    plane = plane.astype(jnp.float32)
    moved = [shift_cells(plane, 0, col_tap - 1) for col_tap in range(3)]
    for row_tap in range(3):
        for col_tap in range(3):
            stack_ref[at : at + rows, :] = shift_cells(moved[col_tap], row_tap - 1, 0).astype(
                jnp.bfloat16
            )
            at += rows


def cross(stack, x):
    return lax.dot_general(
        stack, x, (((1,), (1,)), ((), ())), preferred_element_type=jnp.float32
    ).astype(jnp.bfloat16)


def own_kernel(core_ref, own_ref, mine_ref, other_ref, units_ref, stack_ref, x_ref):
    rows = own_ref.shape[0]
    x = merge_cores(core_ref, mine_ref, other_ref, x_ref)
    columns = x.shape[0] // LANES
    stack_plane(own_ref[...], stack_ref, 0)
    grad = cross(stack_ref[...], x)
    for unit in range(9 * columns):
        tap, column = divmod(unit, columns)
        units_ref[unit] = grad[
            tap * rows : (tap + 1) * rows, column * LANES : (column + 1) * LANES
        ]


def wgrad_own(core, own, mine, other):
    rows, cells = own.shape
    chans = 2 * mine.shape[0] * mine.shape[1]
    return pl.pallas_call(
        own_kernel,
        out_shape=[
            jax.ShapeDtypeStruct((9 * chans // LANES, rows, LANES), jnp.bfloat16),
            jax.ShapeDtypeStruct((9 * rows, cells), jnp.bfloat16),
            jax.ShapeDtypeStruct((mine.shape[0], 2) + mine.shape[1:], mine.dtype),
        ],
        in_specs=specs(1, 3),
        compiler_params=pltpu.CompilerParams(vmem_limit_bytes=VMEM_LIMIT),
        name="wgrad_own",
    )(core, own, mine, other)


def halo_kernel(above_ref, below_ref, x_ref, units_ref, wide_ref, stack_ref):
    rows = above_ref.shape[0]
    slots, per = wide_ref.shape[:2]
    x = x_ref[...].reshape(-1, x_ref.shape[-1])
    columns = x.shape[0] // LANES
    for half, ref in enumerate((above_ref, below_ref)):
        stack_plane(ref[...], stack_ref, half * 9 * rows)
        grad = cross(stack_ref[half * 9 * rows : (half + 1) * 9 * rows, :], x)
        for at in range(9 * columns):
            tap, column = divmod(at, columns)
            unit = 18 * half * columns + at
            wide_ref[unit // per, unit % per] = grad[
                tap * rows : (tap + 1) * rows, column * LANES : (column + 1) * LANES
            ]
    for at in range(9 * columns):
        unit = 9 * columns + at
        wide_ref[unit // per, unit % per] = units_ref[at]
    for unit in range(TAPS * columns, slots * per):
        wide_ref[unit // per, unit % per] = jnp.zeros((rows, LANES), jnp.bfloat16)


def wgrad_halo(above, below, x, units, slots):
    rows, cells = above.shape
    per = -(-3 * units.shape[0] // slots)
    return pl.pallas_call(
        halo_kernel,
        out_shape=[
            jax.ShapeDtypeStruct((slots, per, rows, LANES), jnp.bfloat16),
            jax.ShapeDtypeStruct((18 * rows, cells), jnp.bfloat16),
        ],
        compiler_params=pltpu.CompilerParams(vmem_limit_bytes=VMEM_LIMIT),
        name="wgrad_halo",
    )(above, below, x, units)


def dgrad_kernel(core_ref, x_at_ref, z_at_ref, k_ref, own_ref, halo_ref, keep_ref, send_ref):
    rows = keep_ref.shape[2]
    n = 9 * rows
    partial = None
    for at, stack in ((0, halo_ref[:n, :]), (n, own_ref[...]), (2 * n, halo_ref[n:, :])):
        term = lax.dot_general(
            k_ref[at : at + n, :],
            stack,
            (((0,), (0,)), ((), ())),
            preferred_element_type=jnp.float32,
        )
        partial = term if partial is None else partial + term
    first = core_ref[0] == 0
    for x_at in range(4):
        for z_at in range(3):
            x_slot = x_at ^ x_at_ref[0]
            z_slot = lax.rem(z_at - z_at_ref[0] + 3, 3)
            at = (x_at * 3 + z_at) * 2 * rows
            even, odd = partial[at : at + rows], partial[at + rows : at + 2 * rows]
            keep_ref[x_slot, z_slot] = jnp.where(first, even, odd)
            send_ref[x_slot, z_slot] = jnp.where(first, odd, even).astype(jnp.bfloat16)


def dgrad(core, x_at, z_at, k_rows, own, halo):
    shape = (4, 3, k_rows.shape[0] // TAPS, own.shape[1])
    return pl.pallas_call(
        dgrad_kernel,
        out_shape=[
            jax.ShapeDtypeStruct(shape, jnp.float32),
            jax.ShapeDtypeStruct(shape, jnp.bfloat16),
        ],
        in_specs=specs(3, 3),
        compiler_params=pltpu.CompilerParams(vmem_limit_bytes=VMEM_LIMIT),
        name="dgrad",
    )(core, x_at, z_at, k_rows, own, halo)


def act_kernel(mid_ref, low_ref, high_ref, cot_ref, act_ref, grad_ref):
    preact = mid_ref[...] + low_ref[...].astype(jnp.float32) + high_ref[...].astype(jnp.float32)
    sig = jax.nn.sigmoid(preact)
    act_ref[...] = (preact * sig).astype(jnp.bfloat16)
    cot = cot_ref[...].astype(jnp.float32)
    grad_ref[...] = (cot * sig * (1.0 + preact * (1.0 - sig))).astype(jnp.bfloat16)


def activate(mid, low, high, cot):
    shape = jax.ShapeDtypeStruct(mid.shape, jnp.bfloat16)
    return pl.pallas_call(
        act_kernel,
        out_shape=[shape, shape],
        compiler_params=pltpu.CompilerParams(vmem_limit_bytes=VMEM_LIMIT),
        name="activate",
    )(mid, low, high, cot)


def total_kernel(terms_ref, out_ref, *, scale):
    total = jnp.sum(terms_ref[...].astype(jnp.float32), axis=0) * scale
    out_ref[...] = jnp.broadcast_to(total.astype(jnp.bfloat16)[None], out_ref.shape)


def total_spread(terms, scale, copies):
    return pl.pallas_call(
        functools.partial(total_kernel, scale=scale),
        out_shape=jax.ShapeDtypeStruct((copies,) + terms.shape[1:], jnp.bfloat16),
        compiler_params=pltpu.CompilerParams(vmem_limit_bytes=VMEM_LIMIT),
        name="total",
    )(terms)


def halve_kernel(kept_ref, came_ref, keep_ref, send_ref):
    for at in range(keep_ref.shape[0]):
        keep_ref[at] = kept_ref[2 * at] + came_ref[2 * at].astype(jnp.float32)
        total = kept_ref[2 * at + 1] + came_ref[2 * at + 1].astype(jnp.float32)
        send_ref[at] = total.astype(jnp.bfloat16)


def halve(kept, came):
    shape = (kept.shape[0] // 2,) + kept.shape[1:]
    return pl.pallas_call(
        halve_kernel,
        out_shape=[
            jax.ShapeDtypeStruct(shape, jnp.float32),
            jax.ShapeDtypeStruct(shape, jnp.bfloat16),
        ],
        compiler_params=pltpu.CompilerParams(vmem_limit_bytes=VMEM_LIMIT),
        name="halve",
    )(kept, came)


def unpack_kernel(units_ref, out_ref):
    per = units_ref.shape[1]
    columns = out_ref.shape[2] // LANES
    for tap in range(TAPS):
        for column in range(columns):
            unit = tap * columns + column
            block = units_ref[unit // per, unit % per].astype(jnp.float32)
            out_ref[tap, :, column * LANES : (column + 1) * LANES] = block


def unpack(units, chans):
    return pl.pallas_call(
        unpack_kernel,
        out_shape=jax.ShapeDtypeStruct((TAPS, units.shape[2], chans), jnp.float32),
        compiler_params=pltpu.CompilerParams(vmem_limit_bytes=VMEM_LIMIT),
        name="unpack",
    )(units)


def swap_cores(blocks):
    return lax.ppermute(blocks, "core", [(0, 1), (1, 0)])


def body(volume, kernel, cotangent):
    rows = volume.shape[2]
    cells = volume.shape[3]
    chips = lax.axis_size(CHIPS)
    depths = lax.axis_size(DEP)

    def shift(block, step):
        return lax.ppermute(block, DEP, [(i, (i + step) % depths) for i in range(depths)])

    def index(name):
        return lax.axis_index(name).astype(jnp.int32).reshape(1)

    core, x_at, z_at = index("core"), index("x"), index("zl")
    own = volume.reshape(rows, cells)
    cot = cotangent.reshape(rows, cells)

    def copies(block):
        return jnp.broadcast_to(block[None], (chips, rows, cells))

    mine = lax.all_to_all(copies(own), CHIPS, 0, 0)
    k_rows = jnp.transpose(kernel.reshape(rows, TAPS, -1), (1, 0, 2)).reshape(TAPS * rows, -1)
    mine, k_rows, cot, core, x_at, z_at = lax.optimization_barrier(
        (mine, k_rows, cot, core, x_at, z_at)
    )
    other = swap_cores(mine)

    up, mid, down = conv(core, k_rows, mine, other)
    activated, grad_pre = activate(mid, shift(up, 1), shift(down, -1), cot)

    above, below = shift(grad_pre, -1), shift(grad_pre, 1)
    own_units, own_stack, x = wgrad_own(core, grad_pre, mine, other)
    ys, zs = lax.axis_size("y"), lax.axis_size("zh")
    wide, halo_stack = wgrad_halo(above, below, x, own_units, ys)
    scale = 1.0 / math.sqrt(UNIV * DEPTH * SIDE * SIDE)
    over_y = lax.all_to_all(wide, "y", 0, 0)

    keep, send = dgrad(core, x_at, z_at, k_rows, own_stack, halo_stack)
    keep, send = halve(keep, swap_cores(send))
    over_y, keep = lax.optimization_barrier((over_y, keep))
    over_z = lax.all_to_all(total_spread(over_y, 1.0, zs), "zh", 0, 0)
    total = keep + lax.ppermute(send, "x", [(i, i ^ 1) for i in range(4)]).astype(jnp.float32)
    after, before = total[:, 1].astype(jnp.bfloat16), total[:, 2].astype(jnp.bfloat16)
    over_z, _ = lax.optimization_barrier((over_z, (after, before)))
    after = lax.ppermute(after, "zl", [(i, (i + 1) % 3) for i in range(3)])
    before = lax.ppermute(before, "zl", [(i, (i + 2) % 3) for i in range(3)])
    units = lax.all_to_all(total_spread(over_z, scale, ys), "y", 0, 0)
    total = total[:, 0] + after.astype(jnp.float32) + before.astype(jnp.float32)
    step = lax.ppermute(total[1].astype(jnp.bfloat16), "x", [(i, i ^ 2) for i in range(4)])
    grad_volume = (total[0] + step.astype(jnp.float32)).astype(jnp.bfloat16)
    all_taps = unpack(units, kernel.shape[-1])
    grad_kernel = jnp.transpose(all_taps, (1, 0, 2)).reshape(kernel.shape)
    return (activated.reshape(volume.shape), grad_volume.reshape(volume.shape), grad_kernel)


def solution(mesh):
    fine = Mesh(mesh.devices.reshape(8, 4, 4, 3, 2), ("y", "zh", "x", "zl", "core"))
    field = P(None, DEP, CHAN, None)
    weight = P(CHAN, None, None, None, None)
    return jax.shard_map(
        body,
        mesh=fine,
        in_specs=(field, weight, field),
        out_specs=(field, field, weight),
        check_vma=False,
    )
```

```python
import functools
import math

import jax
import jax.numpy as jnp
from jax import lax
from jax.experimental import pallas as pl
from jax.experimental.pallas import tpu as pltpu
from jax.sharding import Mesh
from jax.sharding import PartitionSpec as P

DEPTH = 32
SIDE = 32
UNIV = 1
TAPS = 27
LANES = 128
VMEM_LIMIT = 48 * 1024 * 1024
DEP = ("y", "zh")
CHIPS = ("x", "zl")
CHAN = ("x", "zl", "core")


def shift_cells(plane, row_step, col_step):
    cells = plane.shape[-1]
    if col_step:
        columns = lax.broadcasted_iota(jnp.int32, plane.shape, 1) % SIDE
        edge = 0 if col_step > 0 else SIDE - 1
        plain = pltpu.roll(plane, col_step % cells, 1)
        wrapped = pltpu.roll(plane, (col_step - col_step * SIDE) % cells, 1)
        plane = jnp.where(columns == edge, wrapped, plain)
    if row_step:
        plane = pltpu.roll(plane, (row_step * SIDE) % cells, 1)
    return plane


def merge_cores(core_ref, mine_ref, other_ref, x_ref):
    first = core_ref[0] == 0
    mine, other = mine_ref[...], other_ref[...]
    x_ref[:, 0] = jnp.where(first, mine, other)
    x_ref[:, 1] = jnp.where(first, other, mine)
    return x_ref[...].reshape(-1, x_ref.shape[-1])


def conv_kernel(core_ref, w_ref, mine_ref, other_ref, *refs):
    outs, x_ref = refs[:3], refs[3]
    rows = outs[0].shape[0]
    x = merge_cores(core_ref, mine_ref, other_ref, x_ref)
    for depth_tap in range(3):
        w = w_ref[depth_tap * 9 * rows : (depth_tap + 1) * 9 * rows, :]
        product = jnp.dot(w, x, preferred_element_type=jnp.float32)
        total = None
        for col_tap in range(3):
            part = None
            for row_tap in range(3):
                at = (row_tap * 3 + col_tap) * rows
                term = shift_cells(product[at : at + rows], 1 - row_tap, 0)
                part = term if part is None else part + term
            part = shift_cells(part, 0, 1 - col_tap)
            total = part if total is None else total + part
        outs[depth_tap][...] = total.astype(outs[depth_tap].dtype)


def specs(scalars, arrays):
    smem = pl.BlockSpec(memory_space=pltpu.SMEM)
    return [smem] * scalars + [pl.BlockSpec(memory_space=pltpu.VMEM)] * arrays


def merged_scratch(mine):
    return [pltpu.VMEM((mine.shape[0], 2) + mine.shape[1:], mine.dtype)]


def conv(core, weights, mine, other):
    rows = weights.shape[0] // TAPS
    cells = mine.shape[-1]
    return pl.pallas_call(
        conv_kernel,
        out_shape=[
            jax.ShapeDtypeStruct((rows, cells), kind)
            for kind in (jnp.bfloat16, jnp.float32, jnp.bfloat16)
        ],
        in_specs=specs(1, 3),
        scratch_shapes=merged_scratch(mine),
        compiler_params=pltpu.CompilerParams(vmem_limit_bytes=VMEM_LIMIT),
        name="conv",
    )(core, weights, mine, other)


def stack_plane(plane, stack_ref, at):
    rows = plane.shape[0]
    plane = plane.astype(jnp.float32)
    moved = [shift_cells(plane, 0, col_tap - 1) for col_tap in range(3)]
    for row_tap in range(3):
        for col_tap in range(3):
            stack_ref[at : at + rows, :] = shift_cells(moved[col_tap], row_tap - 1, 0).astype(
                jnp.bfloat16
            )
            at += rows


def cross(stack, x):
    return lax.dot_general(
        stack, x, (((1,), (1,)), ((), ())), preferred_element_type=jnp.float32
    ).astype(jnp.bfloat16)


def own_kernel(core_ref, own_ref, mine_ref, other_ref, units_ref, stack_ref, x_ref):
    rows = own_ref.shape[0]
    x = merge_cores(core_ref, mine_ref, other_ref, x_ref)
    columns = x.shape[0] // LANES
    stack_plane(own_ref[...], stack_ref, 0)
    grad = cross(stack_ref[...], x)
    for unit in range(9 * columns):
        tap, column = divmod(unit, columns)
        units_ref[unit] = grad[
            tap * rows : (tap + 1) * rows, column * LANES : (column + 1) * LANES
        ]


def wgrad_own(core, own, mine, other):
    rows, cells = own.shape
    chans = 2 * mine.shape[0] * mine.shape[1]
    return pl.pallas_call(
        own_kernel,
        out_shape=[
            jax.ShapeDtypeStruct((9 * chans // LANES, rows, LANES), jnp.bfloat16),
            jax.ShapeDtypeStruct((9 * rows, cells), jnp.bfloat16),
            jax.ShapeDtypeStruct((mine.shape[0], 2) + mine.shape[1:], mine.dtype),
        ],
        in_specs=specs(1, 3),
        compiler_params=pltpu.CompilerParams(vmem_limit_bytes=VMEM_LIMIT),
        name="wgrad_own",
    )(core, own, mine, other)


def halo_kernel(above_ref, below_ref, x_ref, units_ref, wide_ref, stack_ref):
    rows = above_ref.shape[0]
    slots, per = wide_ref.shape[:2]
    x = x_ref[...].reshape(-1, x_ref.shape[-1])
    columns = x.shape[0] // LANES
    for half, ref in enumerate((above_ref, below_ref)):
        stack_plane(ref[...], stack_ref, half * 9 * rows)
        grad = cross(stack_ref[half * 9 * rows : (half + 1) * 9 * rows, :], x)
        for at in range(9 * columns):
            tap, column = divmod(at, columns)
            unit = 18 * half * columns + at
            wide_ref[unit // per, unit % per] = grad[
                tap * rows : (tap + 1) * rows, column * LANES : (column + 1) * LANES
            ]
    for at in range(9 * columns):
        unit = 9 * columns + at
        wide_ref[unit // per, unit % per] = units_ref[at]
    for unit in range(TAPS * columns, slots * per):
        wide_ref[unit // per, unit % per] = jnp.zeros((rows, LANES), jnp.bfloat16)


def wgrad_halo(above, below, x, units, slots):
    rows, cells = above.shape
    per = -(-3 * units.shape[0] // slots)
    return pl.pallas_call(
        halo_kernel,
        out_shape=[
            jax.ShapeDtypeStruct((slots, per, rows, LANES), jnp.bfloat16),
            jax.ShapeDtypeStruct((18 * rows, cells), jnp.bfloat16),
        ],
        compiler_params=pltpu.CompilerParams(vmem_limit_bytes=VMEM_LIMIT),
        name="wgrad_halo",
    )(above, below, x, units)


def dgrad_kernel(core_ref, x_at_ref, z_at_ref, k_ref, own_ref, halo_ref, keep_ref, send_ref):
    rows = keep_ref.shape[2]
    n = 9 * rows
    partial = None
    for at, stack in ((0, halo_ref[:n, :]), (n, own_ref[...]), (2 * n, halo_ref[n:, :])):
        term = lax.dot_general(
            k_ref[at : at + n, :],
            stack,
            (((0,), (0,)), ((), ())),
            preferred_element_type=jnp.float32,
        )
        partial = term if partial is None else partial + term
    first = core_ref[0] == 0
    for x_at in range(4):
        for z_at in range(3):
            x_slot = x_at ^ x_at_ref[0]
            z_slot = lax.rem(z_at - z_at_ref[0] + 3, 3)
            at = (x_at * 3 + z_at) * 2 * rows
            even, odd = partial[at : at + rows], partial[at + rows : at + 2 * rows]
            keep_ref[z_slot, x_slot] = jnp.where(first, even, odd)
            send_ref[z_slot, x_slot] = jnp.where(first, odd, even).astype(jnp.bfloat16)


def dgrad(core, x_at, z_at, k_rows, own, halo):
    shape = (3, 4, k_rows.shape[0] // TAPS, own.shape[1])
    return pl.pallas_call(
        dgrad_kernel,
        out_shape=[
            jax.ShapeDtypeStruct(shape, jnp.float32),
            jax.ShapeDtypeStruct(shape, jnp.bfloat16),
        ],
        in_specs=specs(3, 3),
        compiler_params=pltpu.CompilerParams(vmem_limit_bytes=VMEM_LIMIT),
        name="dgrad",
    )(core, x_at, z_at, k_rows, own, halo)


def act_kernel(mid_ref, low_ref, high_ref, cot_ref, act_ref, grad_ref):
    preact = mid_ref[...] + low_ref[...].astype(jnp.float32) + high_ref[...].astype(jnp.float32)
    sig = jax.nn.sigmoid(preact)
    act_ref[...] = (preact * sig).astype(jnp.bfloat16)
    cot = cot_ref[...].astype(jnp.float32)
    grad_ref[...] = (cot * sig * (1.0 + preact * (1.0 - sig))).astype(jnp.bfloat16)


def activate(mid, low, high, cot):
    shape = jax.ShapeDtypeStruct(mid.shape, jnp.bfloat16)
    return pl.pallas_call(
        act_kernel,
        out_shape=[shape, shape],
        compiler_params=pltpu.CompilerParams(vmem_limit_bytes=VMEM_LIMIT),
        name="activate",
    )(mid, low, high, cot)


def total_kernel(terms_ref, out_ref, *, scale):
    total = jnp.sum(terms_ref[...].astype(jnp.float32), axis=0) * scale
    out_ref[...] = jnp.broadcast_to(total.astype(jnp.bfloat16)[None], out_ref.shape)


def total_spread(terms, scale, copies):
    return pl.pallas_call(
        functools.partial(total_kernel, scale=scale),
        out_shape=jax.ShapeDtypeStruct((copies,) + terms.shape[1:], jnp.bfloat16),
        compiler_params=pltpu.CompilerParams(vmem_limit_bytes=VMEM_LIMIT),
        name="total",
    )(terms)


def part_kernel(kept_ref, came_ref, here_ref, after_ref, before_ref):
    here_ref[...] = kept_ref[0] + came_ref[0].astype(jnp.float32)
    after_ref[...] = (kept_ref[1] + came_ref[1].astype(jnp.float32)).astype(jnp.bfloat16)
    before_ref[...] = (kept_ref[2] + came_ref[2].astype(jnp.float32)).astype(jnp.bfloat16)


def part(kept, came):
    return pl.pallas_call(
        part_kernel,
        out_shape=[
            jax.ShapeDtypeStruct(kept.shape[1:], kind)
            for kind in (jnp.float32, jnp.bfloat16, jnp.bfloat16)
        ],
        compiler_params=pltpu.CompilerParams(vmem_limit_bytes=VMEM_LIMIT),
        name="part",
    )(kept, came)


def unpack_kernel(units_ref, out_ref):
    per = units_ref.shape[1]
    columns = out_ref.shape[2] // LANES
    for tap in range(TAPS):
        for column in range(columns):
            unit = tap * columns + column
            block = units_ref[unit // per, unit % per].astype(jnp.float32)
            out_ref[tap, :, column * LANES : (column + 1) * LANES] = block


def unpack(units, chans):
    return pl.pallas_call(
        unpack_kernel,
        out_shape=jax.ShapeDtypeStruct((TAPS, units.shape[2], chans), jnp.float32),
        compiler_params=pltpu.CompilerParams(vmem_limit_bytes=VMEM_LIMIT),
        name="unpack",
    )(units)


def swap_cores(blocks):
    return lax.ppermute(blocks, "core", [(0, 1), (1, 0)])


def body(volume, kernel, cotangent):
    rows = volume.shape[2]
    cells = volume.shape[3]
    chips = lax.axis_size(CHIPS)
    depths = lax.axis_size(DEP)

    def shift(block, step):
        return lax.ppermute(block, DEP, [(i, (i + step) % depths) for i in range(depths)])

    def index(name):
        return lax.axis_index(name).astype(jnp.int32).reshape(1)

    core, x_at, z_at = index("core"), index("x"), index("zl")
    own = volume.reshape(rows, cells)
    cot = cotangent.reshape(rows, cells)

    def copies(block):
        return jnp.broadcast_to(block[None], (chips, rows, cells))

    mine = lax.all_to_all(copies(own), CHIPS, 0, 0)
    k_rows = jnp.transpose(kernel.reshape(rows, TAPS, -1), (1, 0, 2)).reshape(TAPS * rows, -1)
    mine, k_rows, cot, core, x_at, z_at = lax.optimization_barrier(
        (mine, k_rows, cot, core, x_at, z_at)
    )
    other = swap_cores(mine)

    up, mid, down = conv(core, k_rows, mine, other)
    activated, grad_pre = activate(mid, shift(up, 1), shift(down, -1), cot)

    above, below = shift(grad_pre, -1), shift(grad_pre, 1)
    own_units, own_stack, x = wgrad_own(core, grad_pre, mine, other)
    wide, halo_stack = wgrad_halo(above, below, x, own_units, depths)
    scale = 1.0 / math.sqrt(UNIV * DEPTH * SIDE * SIDE)
    terms = lax.all_to_all(wide, DEP, 0, 0)

    keep, send = dgrad(core, x_at, z_at, k_rows, own_stack, halo_stack)
    here, after, before = part(keep, swap_cores(send))
    after = lax.ppermute(after, "zl", [(i, (i + 1) % 3) for i in range(3)])
    before = lax.ppermute(before, "zl", [(i, (i + 2) % 3) for i in range(3)])
    total = here + after.astype(jnp.float32) + before.astype(jnp.float32)
    total = total.reshape(2, 2, rows, cells)
    step = total[:, 1].astype(jnp.bfloat16)
    terms, _ = lax.optimization_barrier((terms, step))
    units = lax.all_to_all(total_spread(terms, scale, depths), DEP, 0, 0)
    step = lax.ppermute(step, "x", [(i, i ^ 1) for i in range(4)])
    total = total[:, 0] + step.astype(jnp.float32)
    step = lax.ppermute(total[1].astype(jnp.bfloat16), "x", [(i, i ^ 2) for i in range(4)])
    grad_volume = (total[0] + step.astype(jnp.float32)).astype(jnp.bfloat16)
    all_taps = unpack(units, kernel.shape[-1])
    grad_kernel = jnp.transpose(all_taps, (1, 0, 2)).reshape(kernel.shape)
    return (activated.reshape(volume.shape), grad_volume.reshape(volume.shape), grad_kernel)


def solution(mesh):
    fine = Mesh(mesh.devices.reshape(8, 4, 4, 3, 2), ("y", "zh", "x", "zl", "core"))
    field = P(None, DEP, CHAN, None)
    weight = P(CHAN, None, None, None, None)
    return jax.shard_map(
        body,
        mesh=fine,
        in_specs=(field, weight, field),
        out_specs=(field, field, weight),
        check_vma=False,
    )
```

```python
import functools
import math

import jax
import jax.numpy as jnp
from jax import lax
from jax.experimental import pallas as pl
from jax.experimental.pallas import tpu as pltpu
from jax.sharding import Mesh
from jax.sharding import PartitionSpec as P

DEPTH = 32
SIDE = 32
UNIV = 1
TAPS = 27
LANES = 128
VMEM_LIMIT = 48 * 1024 * 1024
DEP = ("y", "zh")
CHIPS = ("x", "zl")
CHAN = ("x", "zl", "core")


def shift_cells(plane, row_step, col_step):
    cells = plane.shape[-1]
    if col_step:
        columns = lax.broadcasted_iota(jnp.int32, plane.shape, 1) % SIDE
        edge = 0 if col_step > 0 else SIDE - 1
        plain = pltpu.roll(plane, col_step % cells, 1)
        wrapped = pltpu.roll(plane, (col_step - col_step * SIDE) % cells, 1)
        plane = jnp.where(columns == edge, wrapped, plain)
    if row_step:
        plane = pltpu.roll(plane, (row_step * SIDE) % cells, 1)
    return plane


def merge_cores(core_ref, mine_ref, other_ref, x_ref):
    first = core_ref[0] == 0
    mine, other = mine_ref[...], other_ref[...]
    x_ref[:, 0] = jnp.where(first, mine, other)
    x_ref[:, 1] = jnp.where(first, other, mine)
    return x_ref[...].reshape(-1, x_ref.shape[-1])


def conv_kernel(core_ref, w_ref, mine_ref, other_ref, *refs):
    outs, x_ref = refs[:3], refs[3]
    rows = outs[0].shape[0]
    x = merge_cores(core_ref, mine_ref, other_ref, x_ref)
    for depth_tap in range(3):
        w = w_ref[depth_tap * 9 * rows : (depth_tap + 1) * 9 * rows, :]
        product = jnp.dot(w, x, preferred_element_type=jnp.float32)
        total = None
        for col_tap in range(3):
            part = None
            for row_tap in range(3):
                at = (row_tap * 3 + col_tap) * rows
                term = shift_cells(product[at : at + rows], 1 - row_tap, 0)
                part = term if part is None else part + term
            part = shift_cells(part, 0, 1 - col_tap)
            total = part if total is None else total + part
        outs[depth_tap][...] = total.astype(outs[depth_tap].dtype)


def specs(scalars, arrays):
    smem = pl.BlockSpec(memory_space=pltpu.SMEM)
    return [smem] * scalars + [pl.BlockSpec(memory_space=pltpu.VMEM)] * arrays


def merged_scratch(mine):
    return [pltpu.VMEM((mine.shape[0], 2) + mine.shape[1:], mine.dtype)]


def conv(core, weights, mine, other):
    rows = weights.shape[0] // TAPS
    cells = mine.shape[-1]
    return pl.pallas_call(
        conv_kernel,
        out_shape=[
            jax.ShapeDtypeStruct((rows, cells), kind)
            for kind in (jnp.bfloat16, jnp.float32, jnp.bfloat16)
        ],
        in_specs=specs(1, 3),
        scratch_shapes=merged_scratch(mine),
        compiler_params=pltpu.CompilerParams(vmem_limit_bytes=VMEM_LIMIT),
        name="conv",
    )(core, weights, mine, other)


def stack_plane(plane, stack_ref, at):
    rows = plane.shape[0]
    plane = plane.astype(jnp.float32)
    moved = [shift_cells(plane, 0, col_tap - 1) for col_tap in range(3)]
    for row_tap in range(3):
        for col_tap in range(3):
            stack_ref[at : at + rows, :] = shift_cells(moved[col_tap], row_tap - 1, 0).astype(
                jnp.bfloat16
            )
            at += rows


def cross(stack, x):
    return lax.dot_general(
        stack, x, (((1,), (1,)), ((), ())), preferred_element_type=jnp.float32
    ).astype(jnp.bfloat16)


def own_kernel(core_ref, own_ref, mine_ref, other_ref, units_ref, stack_ref, x_ref):
    rows = own_ref.shape[0]
    x = merge_cores(core_ref, mine_ref, other_ref, x_ref)
    columns = x.shape[0] // LANES
    stack_plane(own_ref[...], stack_ref, 0)
    grad = cross(stack_ref[...], x)
    for unit in range(9 * columns):
        tap, column = divmod(unit, columns)
        units_ref[unit] = grad[
            tap * rows : (tap + 1) * rows, column * LANES : (column + 1) * LANES
        ]


def wgrad_own(core, own, mine, other):
    rows, cells = own.shape
    chans = 2 * mine.shape[0] * mine.shape[1]
    return pl.pallas_call(
        own_kernel,
        out_shape=[
            jax.ShapeDtypeStruct((9 * chans // LANES, rows, LANES), jnp.bfloat16),
            jax.ShapeDtypeStruct((9 * rows, cells), jnp.bfloat16),
            jax.ShapeDtypeStruct((mine.shape[0], 2) + mine.shape[1:], mine.dtype),
        ],
        in_specs=specs(1, 3),
        compiler_params=pltpu.CompilerParams(vmem_limit_bytes=VMEM_LIMIT),
        name="wgrad_own",
    )(core, own, mine, other)


def halo_kernel(above_ref, below_ref, x_ref, units_ref, wide_ref, stack_ref):
    rows = above_ref.shape[0]
    slots, per = wide_ref.shape[:2]
    x = x_ref[...].reshape(-1, x_ref.shape[-1])
    columns = x.shape[0] // LANES
    for half, ref in enumerate((above_ref, below_ref)):
        stack_plane(ref[...], stack_ref, half * 9 * rows)
        grad = cross(stack_ref[half * 9 * rows : (half + 1) * 9 * rows, :], x)
        for at in range(9 * columns):
            tap, column = divmod(at, columns)
            unit = 18 * half * columns + at
            wide_ref[unit // per, unit % per] = grad[
                tap * rows : (tap + 1) * rows, column * LANES : (column + 1) * LANES
            ]
    for at in range(9 * columns):
        unit = 9 * columns + at
        wide_ref[unit // per, unit % per] = units_ref[at]
    for unit in range(TAPS * columns, slots * per):
        wide_ref[unit // per, unit % per] = jnp.zeros((rows, LANES), jnp.bfloat16)


def wgrad_halo(above, below, x, units, slots):
    rows, cells = above.shape
    per = -(-3 * units.shape[0] // slots)
    return pl.pallas_call(
        halo_kernel,
        out_shape=[
            jax.ShapeDtypeStruct((slots, per, rows, LANES), jnp.bfloat16),
            jax.ShapeDtypeStruct((18 * rows, cells), jnp.bfloat16),
        ],
        compiler_params=pltpu.CompilerParams(vmem_limit_bytes=VMEM_LIMIT),
        name="wgrad_halo",
    )(above, below, x, units)


def dgrad_kernel(core_ref, x_at_ref, z_at_ref, k_ref, own_ref, halo_ref, keep_ref, send_ref):
    rows = keep_ref.shape[2]
    n = 9 * rows
    partial = None
    for at, stack in ((0, halo_ref[:n, :]), (n, own_ref[...]), (2 * n, halo_ref[n:, :])):
        term = lax.dot_general(
            k_ref[at : at + n, :],
            stack,
            (((0,), (0,)), ((), ())),
            preferred_element_type=jnp.float32,
        )
        partial = term if partial is None else partial + term
    first = core_ref[0] == 0
    for x_at in range(4):
        for z_at in range(3):
            x_slot = x_at ^ x_at_ref[0]
            z_slot = lax.rem(z_at - z_at_ref[0] + 3, 3)
            at = (x_at * 3 + z_at) * 2 * rows
            even, odd = partial[at : at + rows], partial[at + rows : at + 2 * rows]
            keep_ref[x_slot, z_slot] = jnp.where(first, even, odd)
            send_ref[x_slot, z_slot] = jnp.where(first, odd, even).astype(jnp.bfloat16)


def dgrad(core, x_at, z_at, k_rows, own, halo):
    shape = (4, 3, k_rows.shape[0] // TAPS, own.shape[1])
    return pl.pallas_call(
        dgrad_kernel,
        out_shape=[
            jax.ShapeDtypeStruct(shape, jnp.float32),
            jax.ShapeDtypeStruct(shape, jnp.bfloat16),
        ],
        in_specs=specs(3, 3),
        compiler_params=pltpu.CompilerParams(vmem_limit_bytes=VMEM_LIMIT),
        name="dgrad",
    )(core, x_at, z_at, k_rows, own, halo)


def act_kernel(mid_ref, low_ref, high_ref, cot_ref, act_ref, grad_ref):
    preact = mid_ref[...] + low_ref[...].astype(jnp.float32) + high_ref[...].astype(jnp.float32)
    sig = jax.nn.sigmoid(preact)
    act_ref[...] = (preact * sig).astype(jnp.bfloat16)
    cot = cot_ref[...].astype(jnp.float32)
    grad_ref[...] = (cot * sig * (1.0 + preact * (1.0 - sig))).astype(jnp.bfloat16)


def activate(mid, low, high, cot):
    shape = jax.ShapeDtypeStruct(mid.shape, jnp.bfloat16)
    return pl.pallas_call(
        act_kernel,
        out_shape=[shape, shape],
        compiler_params=pltpu.CompilerParams(vmem_limit_bytes=VMEM_LIMIT),
        name="activate",
    )(mid, low, high, cot)


def total_kernel(terms_ref, out_ref, *, scale):
    total = jnp.sum(terms_ref[...].astype(jnp.float32), axis=0) * scale
    out_ref[...] = jnp.broadcast_to(total.astype(jnp.bfloat16)[None], out_ref.shape)


def total_spread(terms, scale, copies):
    return pl.pallas_call(
        functools.partial(total_kernel, scale=scale),
        out_shape=jax.ShapeDtypeStruct((copies,) + terms.shape[1:], jnp.bfloat16),
        compiler_params=pltpu.CompilerParams(vmem_limit_bytes=VMEM_LIMIT),
        name="total",
    )(terms)


def unpack_kernel(units_ref, out_ref):
    per = units_ref.shape[1]
    columns = out_ref.shape[2] // LANES
    for tap in range(TAPS):
        for column in range(columns):
            unit = tap * columns + column
            block = units_ref[unit // per, unit % per].astype(jnp.float32)
            out_ref[tap, :, column * LANES : (column + 1) * LANES] = block


def unpack(units, chans):
    return pl.pallas_call(
        unpack_kernel,
        out_shape=jax.ShapeDtypeStruct((TAPS, units.shape[2], chans), jnp.float32),
        compiler_params=pltpu.CompilerParams(vmem_limit_bytes=VMEM_LIMIT),
        name="unpack",
    )(units)


def swap_cores(blocks):
    return lax.ppermute(blocks, "core", [(0, 1), (1, 0)])


def body(volume, kernel, cotangent):
    rows = volume.shape[2]
    cells = volume.shape[3]
    chips = lax.axis_size(CHIPS)
    depths = lax.axis_size(DEP)

    def shift(block, step):
        return lax.ppermute(block, DEP, [(i, (i + step) % depths) for i in range(depths)])

    def index(name):
        return lax.axis_index(name).astype(jnp.int32).reshape(1)

    core, x_at, z_at = index("core"), index("x"), index("zl")
    own = volume.reshape(rows, cells)
    cot = cotangent.reshape(rows, cells)

    def copies(block):
        return jnp.broadcast_to(block[None], (chips, rows, cells))

    mine = lax.all_to_all(copies(own), CHIPS, 0, 0)
    k_rows = jnp.transpose(kernel.reshape(rows, TAPS, -1), (1, 0, 2)).reshape(TAPS * rows, -1)
    mine, k_rows, cot, core, x_at, z_at = lax.optimization_barrier(
        (mine, k_rows, cot, core, x_at, z_at)
    )
    other = swap_cores(mine)

    up, mid, down = conv(core, k_rows, mine, other)
    activated, grad_pre = activate(mid, shift(up, 1), shift(down, -1), cot)

    above, below = shift(grad_pre, -1), shift(grad_pre, 1)
    own_units, own_stack, x = wgrad_own(core, grad_pre, mine, other)
    ys, zs = lax.axis_size("y"), lax.axis_size("zh")
    wide, halo_stack = wgrad_halo(above, below, x, own_units, ys)
    scale = 1.0 / math.sqrt(UNIV * DEPTH * SIDE * SIDE)
    over_y = lax.all_to_all(wide, "y", 0, 0)

    keep, send = dgrad(core, x_at, z_at, k_rows, own_stack, halo_stack)
    total = keep + swap_cores(send).astype(jnp.float32)
    total = total.reshape(2, 2, 3, rows, cells)
    keep, send = total[:, 0], total[:, 1].astype(jnp.bfloat16)
    over_y, _ = lax.optimization_barrier((over_y, send))
    over_z = lax.all_to_all(total_spread(over_y, 1.0, zs), "zh", 0, 0)
    total = keep + lax.ppermute(send, "x", [(i, i ^ 1) for i in range(4)]).astype(jnp.float32)
    after, before = total[:, 1].astype(jnp.bfloat16), total[:, 2].astype(jnp.bfloat16)
    over_z, _ = lax.optimization_barrier((over_z, (after, before)))
    after = lax.ppermute(after, "zl", [(i, (i + 1) % 3) for i in range(3)])
    before = lax.ppermute(before, "zl", [(i, (i + 2) % 3) for i in range(3)])
    units = lax.all_to_all(total_spread(over_z, scale, ys), "y", 0, 0)
    total = total[:, 0] + after.astype(jnp.float32) + before.astype(jnp.float32)
    step = lax.ppermute(total[1].astype(jnp.bfloat16), "x", [(i, i ^ 2) for i in range(4)])
    grad_volume = (total[0] + step.astype(jnp.float32)).astype(jnp.bfloat16)
    all_taps = unpack(units, kernel.shape[-1])
    grad_kernel = jnp.transpose(all_taps, (1, 0, 2)).reshape(kernel.shape)
    return (activated.reshape(volume.shape), grad_volume.reshape(volume.shape), grad_kernel)


def solution(mesh):
    fine = Mesh(mesh.devices.reshape(8, 4, 4, 3, 2), ("y", "zh", "x", "zl", "core"))
    field = P(None, DEP, CHAN, None)
    weight = P(CHAN, None, None, None, None)
    return jax.shard_map(
        body,
        mesh=fine,
        in_specs=(field, weight, field),
        out_specs=(field, field, weight),
        check_vma=False,
    )
```

```python
import functools
import math

import jax
import jax.numpy as jnp
from jax import lax
from jax.experimental import pallas as pl
from jax.experimental.pallas import tpu as pltpu
from jax.sharding import Mesh
from jax.sharding import PartitionSpec as P

DEPTH = 32
SIDE = 32
UNIV = 1
TAPS = 27
LANES = 128
HALF = 8
VMEM_LIMIT = 48 * 1024 * 1024
DEP = ("y", "zh")
CHIPS = ("x", "zl")
CHAN = ("x", "zl", "core")


def shift_cells(plane, row_step, col_step):
    cells = plane.shape[-1]
    if col_step:
        columns = lax.broadcasted_iota(jnp.int32, plane.shape, 1) % SIDE
        edge = 0 if col_step > 0 else SIDE - 1
        plain = pltpu.roll(plane, col_step % cells, 1)
        wrapped = pltpu.roll(plane, (col_step - col_step * SIDE) % cells, 1)
        plane = jnp.where(columns == edge, wrapped, plain)
    if row_step:
        plane = pltpu.roll(plane, (row_step * SIDE) % cells, 1)
    return plane


def merge_cores(core_ref, mine_ref, other_ref, x_ref):
    first = core_ref[0] == 0
    mine, other = mine_ref[...], other_ref[...]
    x_ref[:, 0] = jnp.where(first, mine, other)
    x_ref[:, 1] = jnp.where(first, other, mine)
    return x_ref[...].reshape(-1, x_ref.shape[-1])


def conv_kernel(core_ref, w_ref, mine_ref, other_ref, *refs):
    outs, x_ref = refs[:3], refs[3]
    rows = outs[0].shape[0]
    x = merge_cores(core_ref, mine_ref, other_ref, x_ref)
    for depth_tap in range(3):
        w = w_ref[depth_tap * 9 * rows : (depth_tap + 1) * 9 * rows, :]
        product = jnp.dot(w, x, preferred_element_type=jnp.float32)
        total = None
        for col_tap in range(3):
            part = None
            for row_tap in range(3):
                at = (row_tap * 3 + col_tap) * rows
                term = shift_cells(product[at : at + rows], 1 - row_tap, 0)
                part = term if part is None else part + term
            part = shift_cells(part, 0, 1 - col_tap)
            total = part if total is None else total + part
        outs[depth_tap][...] = total.astype(outs[depth_tap].dtype)


def specs(scalars, arrays):
    smem = pl.BlockSpec(memory_space=pltpu.SMEM)
    return [smem] * scalars + [pl.BlockSpec(memory_space=pltpu.VMEM)] * arrays


def merged_scratch(mine):
    return [pltpu.VMEM((mine.shape[0], 2) + mine.shape[1:], mine.dtype)]


def conv(core, weights, mine, other):
    rows = weights.shape[0] // TAPS
    cells = mine.shape[-1]
    return pl.pallas_call(
        conv_kernel,
        out_shape=[
            jax.ShapeDtypeStruct((rows, cells), kind)
            for kind in (jnp.bfloat16, jnp.float32, jnp.bfloat16)
        ],
        in_specs=specs(1, 3),
        scratch_shapes=merged_scratch(mine),
        compiler_params=pltpu.CompilerParams(vmem_limit_bytes=VMEM_LIMIT),
        name="conv",
    )(core, weights, mine, other)


def stack_plane(plane, stack_ref, at):
    rows = plane.shape[0]
    plane = plane.astype(jnp.float32)
    moved = [shift_cells(plane, 0, col_tap - 1) for col_tap in range(3)]
    for row_tap in range(3):
        for col_tap in range(3):
            stack_ref[at : at + rows, :] = shift_cells(moved[col_tap], row_tap - 1, 0).astype(
                jnp.bfloat16
            )
            at += rows


def cross(stack, x):
    return lax.dot_general(
        stack, x, (((1,), (1,)), ((), ())), preferred_element_type=jnp.float32
    )


def units_of(grad):
    columns = grad.shape[1] // LANES
    for at in range(grad.shape[0] // HALF * columns):
        row, column = divmod(at, columns)
        yield grad[row * HALF : (row + 1) * HALF, column * LANES : (column + 1) * LANES]


def own_kernel(core_ref, own_ref, mine_ref, other_ref, units_ref, stack_ref, x_ref):
    x = merge_cores(core_ref, mine_ref, other_ref, x_ref)
    stack_plane(own_ref[...], stack_ref, 0)
    for at, unit in enumerate(units_of(cross(stack_ref[...], x))):
        units_ref[at] = unit.astype(jnp.bfloat16)


def plane_shapes(own, chans):
    rows, cells = own.shape
    return [
        jax.ShapeDtypeStruct((9 * rows * chans // (HALF * LANES), HALF, LANES), jnp.bfloat16),
        jax.ShapeDtypeStruct((9 * rows, cells), jnp.bfloat16),
    ]


def wgrad_own(core, own, mine, other):
    chans = 2 * mine.shape[0] * mine.shape[1]
    x = jax.ShapeDtypeStruct((mine.shape[0], 2) + mine.shape[1:], mine.dtype)
    return pl.pallas_call(
        own_kernel,
        out_shape=plane_shapes(own, chans) + [x],
        in_specs=specs(1, 3),
        compiler_params=pltpu.CompilerParams(vmem_limit_bytes=VMEM_LIMIT),
        name="wgrad_own",
    )(core, own, mine, other)


def below_kernel(below_ref, x_ref, units_ref, stack_ref):
    stack_plane(below_ref[...], stack_ref, 0)
    grad = cross(stack_ref[...], x_ref[...].reshape(-1, x_ref.shape[-1]))
    for at, unit in enumerate(units_of(grad)):
        units_ref[at] = unit.astype(jnp.bfloat16)


def wgrad_below(below, x):
    return pl.pallas_call(
        below_kernel,
        out_shape=plane_shapes(below, x.shape[0] * x.shape[1] * x.shape[2]),
        compiler_params=pltpu.CompilerParams(vmem_limit_bytes=VMEM_LIMIT),
        name="wgrad_below",
    )(below, x)


def above_kernel(above_ref, x_ref, own_ref, below_ref, wide_ref, stack_ref):
    slots, per = wide_ref.shape[:2]
    count = own_ref.shape[0]
    for at in range(count):
        for unit, ref in ((count + at, own_ref), (2 * count + at, below_ref)):
            wide_ref[unit // per, unit % per] = ref[at]
    for unit in range(3 * count, slots * per):
        wide_ref[unit // per, unit % per] = jnp.zeros((HALF, LANES), jnp.bfloat16)
    stack_plane(above_ref[...], stack_ref, 0)
    grad = cross(stack_ref[...], x_ref[...].reshape(-1, x_ref.shape[-1]))
    for at, unit in enumerate(units_of(grad)):
        wide_ref[at // per, at % per] = unit.astype(jnp.bfloat16)


def wgrad_above(above, x, own_units, below_units, slots):
    per = -(-3 * own_units.shape[0] // slots)
    stack = plane_shapes(above, x.shape[0] * x.shape[1] * x.shape[2])[1]
    return pl.pallas_call(
        above_kernel,
        out_shape=[jax.ShapeDtypeStruct((slots, per, HALF, LANES), jnp.bfloat16), stack],
        compiler_params=pltpu.CompilerParams(vmem_limit_bytes=VMEM_LIMIT),
        name="wgrad_above",
    )(above, x, own_units, below_units)


def dgrad_kernel(
    core_ref, x_at_ref, z_at_ref, k_ref, above_ref, own_ref, below_ref, keep_ref, send_ref
):
    rows = keep_ref.shape[2]
    n = 9 * rows
    partial = None
    for at, stack_ref in ((0, above_ref), (n, own_ref), (2 * n, below_ref)):
        term = lax.dot_general(
            k_ref[at : at + n, :],
            stack_ref[...],
            (((0,), (0,)), ((), ())),
            preferred_element_type=jnp.float32,
        )
        partial = term if partial is None else partial + term
    first = core_ref[0] == 0
    for x_at in range(4):
        for z_at in range(3):
            x_slot = x_at ^ x_at_ref[0]
            z_slot = lax.rem(z_at - z_at_ref[0] + 3, 3)
            at = (x_at * 3 + z_at) * 2 * rows
            even, odd = partial[at : at + rows], partial[at + rows : at + 2 * rows]
            keep_ref[x_slot, z_slot] = jnp.where(first, even, odd)
            send_ref[x_slot, z_slot] = jnp.where(first, odd, even).astype(jnp.bfloat16)


def dgrad(core, x_at, z_at, k_rows, above, own, below):
    shape = (4, 3, k_rows.shape[0] // TAPS, own.shape[1])
    return pl.pallas_call(
        dgrad_kernel,
        out_shape=[
            jax.ShapeDtypeStruct(shape, jnp.float32),
            jax.ShapeDtypeStruct(shape, jnp.bfloat16),
        ],
        in_specs=specs(3, 4),
        compiler_params=pltpu.CompilerParams(vmem_limit_bytes=VMEM_LIMIT),
        name="dgrad",
    )(core, x_at, z_at, k_rows, above, own, below)


def act_kernel(mid_ref, low_ref, high_ref, cot_ref, act_ref, grad_ref):
    preact = mid_ref[...] + low_ref[...].astype(jnp.float32) + high_ref[...].astype(jnp.float32)
    sig = jax.nn.sigmoid(preact)
    act_ref[...] = (preact * sig).astype(jnp.bfloat16)
    cot = cot_ref[...].astype(jnp.float32)
    grad_ref[...] = (cot * sig * (1.0 + preact * (1.0 - sig))).astype(jnp.bfloat16)


def activate(mid, low, high, cot):
    shape = jax.ShapeDtypeStruct(mid.shape, jnp.bfloat16)
    return pl.pallas_call(
        act_kernel,
        out_shape=[shape, shape],
        compiler_params=pltpu.CompilerParams(vmem_limit_bytes=VMEM_LIMIT),
        name="activate",
    )(mid, low, high, cot)


def total_kernel(terms_ref, out_ref, *, scale):
    total = jnp.sum(terms_ref[...].astype(jnp.float32), axis=0) * scale
    out_ref[...] = jnp.broadcast_to(total.astype(jnp.bfloat16)[None], out_ref.shape)


def total_spread(terms, scale, copies):
    return pl.pallas_call(
        functools.partial(total_kernel, scale=scale),
        out_shape=jax.ShapeDtypeStruct((copies,) + terms.shape[1:], jnp.bfloat16),
        compiler_params=pltpu.CompilerParams(vmem_limit_bytes=VMEM_LIMIT),
        name="total",
    )(terms)


def halve_kernel(kept_ref, came_ref, keep_ref, send_ref):
    for at in range(keep_ref.shape[0]):
        keep_ref[at] = kept_ref[2 * at] + came_ref[2 * at].astype(jnp.float32)
        total = kept_ref[2 * at + 1] + came_ref[2 * at + 1].astype(jnp.float32)
        send_ref[at] = total.astype(jnp.bfloat16)


def halve(kept, came):
    shape = (kept.shape[0] // 2,) + kept.shape[1:]
    return pl.pallas_call(
        halve_kernel,
        out_shape=[
            jax.ShapeDtypeStruct(shape, jnp.float32),
            jax.ShapeDtypeStruct(shape, jnp.bfloat16),
        ],
        compiler_params=pltpu.CompilerParams(vmem_limit_bytes=VMEM_LIMIT),
        name="halve",
    )(kept, came)


def unpack_kernel(units_ref, out_ref):
    taps, rows, chans = out_ref.shape
    per = units_ref.shape[1]
    columns = chans // LANES
    for at in range(taps * rows // HALF * columns):
        row, column = divmod(at, columns)
        tap, half = divmod(row, rows // HALF)
        block = units_ref[at // per, at % per].astype(jnp.float32)
        out_ref[
            tap, half * HALF : (half + 1) * HALF, column * LANES : (column + 1) * LANES
        ] = block


def unpack(units, rows, chans):
    return pl.pallas_call(
        unpack_kernel,
        out_shape=jax.ShapeDtypeStruct((TAPS, rows, chans), jnp.float32),
        compiler_params=pltpu.CompilerParams(vmem_limit_bytes=VMEM_LIMIT),
        name="unpack",
    )(units)


def swap_cores(blocks):
    return lax.ppermute(blocks, "core", [(0, 1), (1, 0)])


def body(volume, kernel, cotangent):
    rows = volume.shape[2]
    cells = volume.shape[3]
    chips = lax.axis_size(CHIPS)
    depths = lax.axis_size(DEP)

    def shift(block, step):
        return lax.ppermute(block, DEP, [(i, (i + step) % depths) for i in range(depths)])

    def index(name):
        return lax.axis_index(name).astype(jnp.int32).reshape(1)

    core, x_at, z_at = index("core"), index("x"), index("zl")
    own = volume.reshape(rows, cells)
    cot = cotangent.reshape(rows, cells)

    def copies(block):
        return jnp.broadcast_to(block[None], (chips, rows, cells))

    mine = lax.all_to_all(copies(own), CHIPS, 0, 0)
    k_rows = jnp.transpose(kernel.reshape(rows, TAPS, -1), (1, 0, 2)).reshape(TAPS * rows, -1)
    mine, k_rows, cot, core, x_at, z_at = lax.optimization_barrier(
        (mine, k_rows, cot, core, x_at, z_at)
    )
    other = swap_cores(mine)

    up, mid, down = conv(core, k_rows, mine, other)
    activated, grad_pre = activate(mid, shift(up, 1), shift(down, -1), cot)

    above, below = shift(grad_pre, -1), shift(grad_pre, 1)
    own_units, own_stack, x = wgrad_own(core, grad_pre, mine, other)
    ys, zs = lax.axis_size("y"), lax.axis_size("zh")
    below_units, below_stack = wgrad_below(below, x)
    wide, above_stack = wgrad_above(above, x, own_units, below_units, ys)
    scale = 1.0 / math.sqrt(UNIV * DEPTH * SIDE * SIDE)
    over_y = lax.all_to_all(wide, "y", 0, 0)

    keep, send = dgrad(core, x_at, z_at, k_rows, above_stack, own_stack, below_stack)
    keep, send = halve(keep, swap_cores(send))
    over_y, keep = lax.optimization_barrier((over_y, keep))
    over_z = lax.all_to_all(total_spread(over_y, 1.0, zs), "zh", 0, 0)
    total = keep + lax.ppermute(send, "x", [(i, i ^ 1) for i in range(4)]).astype(jnp.float32)
    after, before = total[:, 1].astype(jnp.bfloat16), total[:, 2].astype(jnp.bfloat16)
    over_z, _ = lax.optimization_barrier((over_z, (after, before)))
    after = lax.ppermute(after, "zl", [(i, (i + 1) % 3) for i in range(3)])
    before = lax.ppermute(before, "zl", [(i, (i + 2) % 3) for i in range(3)])
    units = lax.all_to_all(total_spread(over_z, scale, ys), "y", 0, 0)
    total = total[:, 0] + after.astype(jnp.float32) + before.astype(jnp.float32)
    step = lax.ppermute(total[1].astype(jnp.bfloat16), "x", [(i, i ^ 2) for i in range(4)])
    grad_volume = (total[0] + step.astype(jnp.float32)).astype(jnp.bfloat16)
    all_taps = unpack(units, rows, kernel.shape[-1])
    grad_kernel = jnp.transpose(all_taps, (1, 0, 2)).reshape(kernel.shape)
    return (activated.reshape(volume.shape), grad_volume.reshape(volume.shape), grad_kernel)


def solution(mesh):
    fine = Mesh(mesh.devices.reshape(8, 4, 4, 3, 2), ("y", "zh", "x", "zl", "core"))
    field = P(None, DEP, CHAN, None)
    weight = P(CHAN, None, None, None, None)
    return jax.shard_map(
        body,
        mesh=fine,
        in_specs=(field, weight, field),
        out_specs=(field, field, weight),
        check_vma=False,
    )
```

```python
import functools
import math

import jax
import jax.numpy as jnp
from jax import lax
from jax.experimental import pallas as pl
from jax.experimental.pallas import tpu as pltpu
from jax.sharding import Mesh
from jax.sharding import PartitionSpec as P

DEPTH = 32
SIDE = 32
UNIV = 1
TAPS = 27
LANES = 128
HALF = 8
VMEM_LIMIT = 48 * 1024 * 1024
DEP = ("y", "zh")
CHIPS = ("x", "zl")
CHAN = ("x", "zl", "core")


def shift_cells(plane, row_step, col_step):
    cells = plane.shape[-1]
    if col_step:
        columns = lax.broadcasted_iota(jnp.int32, plane.shape, 1) % SIDE
        edge = 0 if col_step > 0 else SIDE - 1
        plain = pltpu.roll(plane, col_step % cells, 1)
        wrapped = pltpu.roll(plane, (col_step - col_step * SIDE) % cells, 1)
        plane = jnp.where(columns == edge, wrapped, plain)
    if row_step:
        plane = pltpu.roll(plane, (row_step * SIDE) % cells, 1)
    return plane


def merge_cores(core_ref, mine_ref, other_ref, x_ref):
    first = core_ref[0] == 0
    mine, other = mine_ref[...], other_ref[...]
    x_ref[:, 0] = jnp.where(first, mine, other)
    x_ref[:, 1] = jnp.where(first, other, mine)
    return x_ref[...].reshape(-1, x_ref.shape[-1])


def conv_kernel(core_ref, w_ref, mine_ref, other_ref, *refs):
    outs, x_ref = refs[:3], refs[3]
    rows = outs[0].shape[0]
    x = merge_cores(core_ref, mine_ref, other_ref, x_ref)
    for depth_tap in range(3):
        w = w_ref[depth_tap * 9 * rows : (depth_tap + 1) * 9 * rows, :]
        product = jnp.dot(w, x, preferred_element_type=jnp.float32)
        total = None
        for col_tap in range(3):
            part = None
            for row_tap in range(3):
                at = (row_tap * 3 + col_tap) * rows
                term = shift_cells(product[at : at + rows], 1 - row_tap, 0)
                part = term if part is None else part + term
            part = shift_cells(part, 0, 1 - col_tap)
            total = part if total is None else total + part
        outs[depth_tap][...] = total.astype(outs[depth_tap].dtype)


def specs(scalars, arrays):
    smem = pl.BlockSpec(memory_space=pltpu.SMEM)
    return [smem] * scalars + [pl.BlockSpec(memory_space=pltpu.VMEM)] * arrays


def merged_scratch(mine):
    return [pltpu.VMEM((mine.shape[0], 2) + mine.shape[1:], mine.dtype)]


def conv(core, weights, mine, other):
    rows = weights.shape[0] // TAPS
    cells = mine.shape[-1]
    return pl.pallas_call(
        conv_kernel,
        out_shape=[
            jax.ShapeDtypeStruct((rows, cells), kind)
            for kind in (jnp.bfloat16, jnp.float32, jnp.bfloat16)
        ],
        in_specs=specs(1, 3),
        scratch_shapes=merged_scratch(mine),
        compiler_params=pltpu.CompilerParams(vmem_limit_bytes=VMEM_LIMIT),
        name="conv",
    )(core, weights, mine, other)


def stack_plane(plane, stack_ref, at):
    rows = plane.shape[0]
    plane = plane.astype(jnp.float32)
    moved = [shift_cells(plane, 0, col_tap - 1) for col_tap in range(3)]
    for row_tap in range(3):
        for col_tap in range(3):
            stack_ref[at : at + rows, :] = shift_cells(moved[col_tap], row_tap - 1, 0).astype(
                jnp.bfloat16
            )
            at += rows


def cross(stack, x):
    return lax.dot_general(
        stack, x, (((1,), (1,)), ((), ())), preferred_element_type=jnp.float32
    )


def units_of(grad):
    columns = grad.shape[1] // LANES
    for at in range(grad.shape[0] // HALF * columns):
        row, column = divmod(at, columns)
        yield grad[row * HALF : (row + 1) * HALF, column * LANES : (column + 1) * LANES]


def put(units_ref, wide_ref, first, sem):
    count = units_ref.shape[0]
    copy = pltpu.make_async_copy(units_ref, wide_ref.at[pl.ds(first, count)], sem)
    copy.start()
    return copy


def own_kernel(
    core_ref, own_ref, mine_ref, other_ref, wide_ref, stack_ref, x_ref, units_ref, pad_ref, sems
):
    count = units_ref.shape[0]
    pad_ref[...] = jnp.zeros_like(pad_ref)
    pad = put(pad_ref, wide_ref, 3 * count, sems.at[0])
    x = merge_cores(core_ref, mine_ref, other_ref, x_ref)
    stack_plane(own_ref[...], stack_ref, 0)
    for at, unit in enumerate(units_of(cross(stack_ref[...], x))):
        units_ref[at] = unit.astype(jnp.bfloat16)
    put(units_ref, wide_ref, count, sems.at[1]).wait()
    pad.wait()


def unit_shape(count):
    return (count, HALF, LANES)


def wgrad_own(core, own, mine, other, slots):
    rows, cells = own.shape
    chans = 2 * mine.shape[0] * mine.shape[1]
    count = 9 * rows * chans // (HALF * LANES)
    full = -(-3 * count // slots) * slots
    return pl.pallas_call(
        own_kernel,
        out_shape=[
            jax.ShapeDtypeStruct(unit_shape(full), jnp.bfloat16),
            jax.ShapeDtypeStruct((9 * rows, cells), jnp.bfloat16),
            jax.ShapeDtypeStruct((mine.shape[0], 2) + mine.shape[1:], mine.dtype),
        ],
        in_specs=specs(1, 3),
        out_specs=[pl.BlockSpec(memory_space=pl.ANY)] + specs(0, 2),
        scratch_shapes=[
            pltpu.VMEM(unit_shape(count), jnp.bfloat16),
            pltpu.VMEM(unit_shape(full - 3 * count), jnp.bfloat16),
            pltpu.SemaphoreType.DMA((2,)),
        ],
        compiler_params=pltpu.CompilerParams(vmem_limit_bytes=VMEM_LIMIT),
        name="wgrad_own",
    )(core, own, mine, other)


def halo_kernel(plane_ref, x_ref, before_ref, wide_ref, stack_ref, units_ref, sem, *, run):
    del before_ref
    count = units_ref.shape[0]
    stack_plane(plane_ref[...], stack_ref, 0)
    grad = cross(stack_ref[...], x_ref[...].reshape(-1, x_ref.shape[-1]))
    for at, unit in enumerate(units_of(grad)):
        units_ref[at] = unit.astype(jnp.bfloat16)
    put(units_ref, wide_ref, run * count, sem).wait()


def wgrad_halo(plane, x, wide, run):
    rows, cells = plane.shape
    chans = x.shape[0] * x.shape[1] * x.shape[2]
    return pl.pallas_call(
        functools.partial(halo_kernel, run=run),
        out_shape=[
            jax.ShapeDtypeStruct(wide.shape, wide.dtype),
            jax.ShapeDtypeStruct((9 * rows, cells), jnp.bfloat16),
        ],
        in_specs=specs(0, 2) + [pl.BlockSpec(memory_space=pl.ANY)],
        out_specs=[pl.BlockSpec(memory_space=pl.ANY)] + specs(0, 1),
        scratch_shapes=[
            pltpu.VMEM(unit_shape(9 * rows * chans // (HALF * LANES)), jnp.bfloat16),
            pltpu.SemaphoreType.DMA,
        ],
        input_output_aliases={2: 0},
        compiler_params=pltpu.CompilerParams(vmem_limit_bytes=VMEM_LIMIT),
        name="wgrad_halo",
    )(plane, x, wide)


def copies_kernel(block_ref, out_ref):
    out_ref[...] = jnp.broadcast_to(block_ref[...][None], out_ref.shape)


def copies(block, count):
    return pl.pallas_call(
        copies_kernel,
        out_shape=jax.ShapeDtypeStruct((count,) + block.shape, block.dtype),
        compiler_params=pltpu.CompilerParams(vmem_limit_bytes=VMEM_LIMIT),
        name="copies",
    )(block)


def dgrad_kernel(
    core_ref, x_at_ref, z_at_ref, k_ref, above_ref, own_ref, below_ref, keep_ref, send_ref
):
    rows = keep_ref.shape[2]
    n = 9 * rows
    partial = None
    for at, stack_ref in ((0, above_ref), (n, own_ref), (2 * n, below_ref)):
        term = lax.dot_general(
            k_ref[at : at + n, :],
            stack_ref[...],
            (((0,), (0,)), ((), ())),
            preferred_element_type=jnp.float32,
        )
        partial = term if partial is None else partial + term
    first = core_ref[0] == 0
    for x_at in range(4):
        for z_at in range(3):
            x_slot = x_at ^ x_at_ref[0]
            z_slot = lax.rem(z_at - z_at_ref[0] + 3, 3)
            at = (x_at * 3 + z_at) * 2 * rows
            even, odd = partial[at : at + rows], partial[at + rows : at + 2 * rows]
            keep_ref[x_slot, z_slot] = jnp.where(first, even, odd)
            send_ref[x_slot, z_slot] = jnp.where(first, odd, even).astype(jnp.bfloat16)


def dgrad(core, x_at, z_at, k_rows, above, own, below):
    shape = (4, 3, k_rows.shape[0] // TAPS, own.shape[1])
    return pl.pallas_call(
        dgrad_kernel,
        out_shape=[
            jax.ShapeDtypeStruct(shape, jnp.float32),
            jax.ShapeDtypeStruct(shape, jnp.bfloat16),
        ],
        in_specs=specs(3, 4),
        compiler_params=pltpu.CompilerParams(vmem_limit_bytes=VMEM_LIMIT),
        name="dgrad",
    )(core, x_at, z_at, k_rows, above, own, below)


def act_kernel(mid_ref, low_ref, high_ref, cot_ref, act_ref, grad_ref):
    preact = mid_ref[...] + low_ref[...].astype(jnp.float32) + high_ref[...].astype(jnp.float32)
    sig = jax.nn.sigmoid(preact)
    act_ref[...] = (preact * sig).astype(jnp.bfloat16)
    cot = cot_ref[...].astype(jnp.float32)
    grad_ref[...] = (cot * sig * (1.0 + preact * (1.0 - sig))).astype(jnp.bfloat16)


def activate(mid, low, high, cot):
    shape = jax.ShapeDtypeStruct(mid.shape, jnp.bfloat16)
    return pl.pallas_call(
        act_kernel,
        out_shape=[shape, shape],
        compiler_params=pltpu.CompilerParams(vmem_limit_bytes=VMEM_LIMIT),
        name="activate",
    )(mid, low, high, cot)


def total_kernel(terms_ref, out_ref, *, scale):
    total = jnp.sum(terms_ref[...].astype(jnp.float32), axis=0) * scale
    out_ref[...] = jnp.broadcast_to(total.astype(jnp.bfloat16)[None], out_ref.shape)


def total_spread(terms, scale, copies):
    return pl.pallas_call(
        functools.partial(total_kernel, scale=scale),
        out_shape=jax.ShapeDtypeStruct((copies,) + terms.shape[1:], jnp.bfloat16),
        compiler_params=pltpu.CompilerParams(vmem_limit_bytes=VMEM_LIMIT),
        name="total",
    )(terms)


def halve_kernel(kept_ref, came_ref, keep_ref, send_ref):
    for at in range(keep_ref.shape[0]):
        keep_ref[at] = kept_ref[2 * at] + came_ref[2 * at].astype(jnp.float32)
        total = kept_ref[2 * at + 1] + came_ref[2 * at + 1].astype(jnp.float32)
        send_ref[at] = total.astype(jnp.bfloat16)


def halve(kept, came):
    shape = (kept.shape[0] // 2,) + kept.shape[1:]
    return pl.pallas_call(
        halve_kernel,
        out_shape=[
            jax.ShapeDtypeStruct(shape, jnp.float32),
            jax.ShapeDtypeStruct(shape, jnp.bfloat16),
        ],
        compiler_params=pltpu.CompilerParams(vmem_limit_bytes=VMEM_LIMIT),
        name="halve",
    )(kept, came)


def unpack_kernel(units_ref, out_ref):
    taps, rows, chans = out_ref.shape
    per = units_ref.shape[1]
    columns = chans // LANES
    for at in range(taps * rows // HALF * columns):
        row, column = divmod(at, columns)
        tap, half = divmod(row, rows // HALF)
        block = units_ref[at // per, at % per].astype(jnp.float32)
        out_ref[
            tap, half * HALF : (half + 1) * HALF, column * LANES : (column + 1) * LANES
        ] = block


def unpack(units, rows, chans):
    return pl.pallas_call(
        unpack_kernel,
        out_shape=jax.ShapeDtypeStruct((TAPS, rows, chans), jnp.float32),
        compiler_params=pltpu.CompilerParams(vmem_limit_bytes=VMEM_LIMIT),
        name="unpack",
    )(units)


def swap_cores(blocks):
    return lax.ppermute(blocks, "core", [(0, 1), (1, 0)])


def body(volume, kernel, cotangent):
    rows = volume.shape[2]
    cells = volume.shape[3]
    chips = lax.axis_size(CHIPS)
    depths = lax.axis_size(DEP)

    def shift(block, step):
        return lax.ppermute(block, DEP, [(i, (i + step) % depths) for i in range(depths)])

    def index(name):
        return lax.axis_index(name).astype(jnp.int32).reshape(1)

    core, x_at, z_at = index("core"), index("x"), index("zl")
    own = volume.reshape(rows, cells)
    cot = cotangent.reshape(rows, cells)

    mine = lax.all_to_all(copies(own, chips), CHIPS, 0, 0)
    k_rows = jnp.transpose(kernel.reshape(rows, TAPS, -1), (1, 0, 2)).reshape(TAPS * rows, -1)
    mine, k_rows, cot, core, x_at, z_at = lax.optimization_barrier(
        (mine, k_rows, cot, core, x_at, z_at)
    )
    other = swap_cores(mine)

    up, mid, down = conv(core, k_rows, mine, other)
    activated, grad_pre = activate(mid, shift(up, 1), shift(down, -1), cot)

    above, below = shift(grad_pre, -1), shift(grad_pre, 1)
    ys, zs = lax.axis_size("y"), lax.axis_size("zh")
    wide, own_stack, x = wgrad_own(core, grad_pre, mine, other, ys)
    wide, below_stack = wgrad_halo(below, x, wide, 2)
    wide, above_stack = wgrad_halo(above, x, wide, 0)
    wide = wide.reshape((ys, -1) + wide.shape[1:])
    scale = 1.0 / math.sqrt(UNIV * DEPTH * SIDE * SIDE)
    over_y = lax.all_to_all(wide, "y", 0, 0)

    keep, send = dgrad(core, x_at, z_at, k_rows, above_stack, own_stack, below_stack)
    keep, send = halve(keep, swap_cores(send))
    over_y, keep = lax.optimization_barrier((over_y, keep))
    over_z = lax.all_to_all(total_spread(over_y, 1.0, zs), "zh", 0, 0)
    total = keep + lax.ppermute(send, "x", [(i, i ^ 1) for i in range(4)]).astype(jnp.float32)
    after, before = total[:, 1].astype(jnp.bfloat16), total[:, 2].astype(jnp.bfloat16)
    over_z, _ = lax.optimization_barrier((over_z, (after, before)))
    after = lax.ppermute(after, "zl", [(i, (i + 1) % 3) for i in range(3)])
    before = lax.ppermute(before, "zl", [(i, (i + 2) % 3) for i in range(3)])
    units = lax.all_to_all(total_spread(over_z, scale, ys), "y", 0, 0)
    total = total[:, 0] + after.astype(jnp.float32) + before.astype(jnp.float32)
    step = lax.ppermute(total[1].astype(jnp.bfloat16), "x", [(i, i ^ 2) for i in range(4)])
    grad_volume = (total[0] + step.astype(jnp.float32)).astype(jnp.bfloat16)
    all_taps = unpack(units, rows, kernel.shape[-1])
    grad_kernel = jnp.transpose(all_taps, (1, 0, 2)).reshape(kernel.shape)
    return (activated.reshape(volume.shape), grad_volume.reshape(volume.shape), grad_kernel)


def solution(mesh):
    fine = Mesh(mesh.devices.reshape(8, 4, 4, 3, 2), ("y", "zh", "x", "zl", "core"))
    field = P(None, DEP, CHAN, None)
    weight = P(CHAN, None, None, None, None)
    return jax.shard_map(
        body,
        mesh=fine,
        in_specs=(field, weight, field),
        out_specs=(field, field, weight),
        check_vma=False,
    )
```

```python
import functools
import math

import jax
import jax.numpy as jnp
from jax import lax
from jax.experimental import pallas as pl
from jax.experimental.pallas import tpu as pltpu
from jax.sharding import Mesh
from jax.sharding import PartitionSpec as P

DEPTH = 32
SIDE = 32
UNIV = 1
TAPS = 27
LANES = 128
HALF = 8
VMEM_LIMIT = 48 * 1024 * 1024
DEP = ("y", "zh")
CHIPS = ("x", "zl")
CHAN = ("x", "zl", "core")


def shift_cells(plane, row_step, col_step):
    cells = plane.shape[-1]
    if col_step:
        columns = lax.broadcasted_iota(jnp.int32, plane.shape, 1) % SIDE
        edge = 0 if col_step > 0 else SIDE - 1
        plain = pltpu.roll(plane, col_step % cells, 1)
        wrapped = pltpu.roll(plane, (col_step - col_step * SIDE) % cells, 1)
        plane = jnp.where(columns == edge, wrapped, plain)
    if row_step:
        plane = pltpu.roll(plane, (row_step * SIDE) % cells, 1)
    return plane


def merge_cores(core_ref, mine_ref, other_ref, x_ref):
    first = core_ref[0] == 0
    mine, other = mine_ref[...], other_ref[...]
    x_ref[:, 0] = jnp.where(first, mine, other)
    x_ref[:, 1] = jnp.where(first, other, mine)
    return x_ref[...].reshape(-1, x_ref.shape[-1])


def conv_kernel(core_ref, w_ref, mine_ref, other_ref, *refs):
    outs, x_ref = refs[:3], refs[3]
    rows = outs[0].shape[0]
    x = merge_cores(core_ref, mine_ref, other_ref, x_ref)
    for depth_tap in range(3):
        w = w_ref[depth_tap * 9 * rows : (depth_tap + 1) * 9 * rows, :]
        product = jnp.dot(w, x, preferred_element_type=jnp.float32)
        total = None
        for col_tap in range(3):
            part = None
            for row_tap in range(3):
                at = (row_tap * 3 + col_tap) * rows
                term = shift_cells(product[at : at + rows], 1 - row_tap, 0)
                part = term if part is None else part + term
            part = shift_cells(part, 0, 1 - col_tap)
            total = part if total is None else total + part
        outs[depth_tap][...] = total.astype(outs[depth_tap].dtype)


def specs(scalars, arrays):
    smem = pl.BlockSpec(memory_space=pltpu.SMEM)
    return [smem] * scalars + [pl.BlockSpec(memory_space=pltpu.VMEM)] * arrays


def merged_scratch(mine):
    return [pltpu.VMEM((mine.shape[0], 2) + mine.shape[1:], mine.dtype)]


def conv(core, weights, mine, other):
    rows = weights.shape[0] // TAPS
    cells = mine.shape[-1]
    return pl.pallas_call(
        conv_kernel,
        out_shape=[
            jax.ShapeDtypeStruct((rows, cells), kind)
            for kind in (jnp.bfloat16, jnp.float32, jnp.bfloat16)
        ],
        in_specs=specs(1, 3),
        scratch_shapes=merged_scratch(mine),
        compiler_params=pltpu.CompilerParams(vmem_limit_bytes=VMEM_LIMIT),
        name="conv",
    )(core, weights, mine, other)


def stack_plane(plane, stack_ref, at):
    rows = plane.shape[0]
    plane = plane.astype(jnp.float32)
    moved = [shift_cells(plane, 0, col_tap - 1) for col_tap in range(3)]
    for row_tap in range(3):
        for col_tap in range(3):
            stack_ref[at : at + rows, :] = shift_cells(moved[col_tap], row_tap - 1, 0).astype(
                jnp.bfloat16
            )
            at += rows


def cross(stack, x):
    return lax.dot_general(
        stack, x, (((1,), (1,)), ((), ())), preferred_element_type=jnp.float32
    )


def units_of(grad):
    columns = grad.shape[1] // LANES
    for at in range(grad.shape[0] // HALF * columns):
        row, column = divmod(at, columns)
        yield grad[row * HALF : (row + 1) * HALF, column * LANES : (column + 1) * LANES]


def own_kernel(core_ref, own_ref, mine_ref, other_ref, units_ref, stack_ref, x_ref):
    x = merge_cores(core_ref, mine_ref, other_ref, x_ref)
    stack_plane(own_ref[...], stack_ref, 0)
    for at, unit in enumerate(units_of(cross(stack_ref[...], x))):
        units_ref[at] = unit.astype(jnp.bfloat16)


def plane_shapes(own, chans):
    rows, cells = own.shape
    return [
        jax.ShapeDtypeStruct((9 * rows * chans // (HALF * LANES), HALF, LANES), jnp.bfloat16),
        jax.ShapeDtypeStruct((9 * rows, cells), jnp.bfloat16),
    ]


def wgrad_own(core, own, mine, other):
    chans = 2 * mine.shape[0] * mine.shape[1]
    x = jax.ShapeDtypeStruct((mine.shape[0], 2) + mine.shape[1:], mine.dtype)
    return pl.pallas_call(
        own_kernel,
        out_shape=plane_shapes(own, chans) + [x],
        in_specs=specs(1, 3),
        compiler_params=pltpu.CompilerParams(vmem_limit_bytes=VMEM_LIMIT),
        name="wgrad_own",
    )(core, own, mine, other)


def first_kernel(plane_ref, x_ref, units_ref, stack_ref):
    stack_plane(plane_ref[...], stack_ref, 0)
    grad = cross(stack_ref[...], x_ref[...].reshape(-1, x_ref.shape[-1]))
    for at, unit in enumerate(units_of(grad)):
        units_ref[at] = unit.astype(jnp.bfloat16)


def wgrad_first(plane, x):
    return pl.pallas_call(
        first_kernel,
        out_shape=plane_shapes(plane, x.shape[0] * x.shape[1] * x.shape[2]),
        compiler_params=pltpu.CompilerParams(vmem_limit_bytes=VMEM_LIMIT),
        name="wgrad_first",
    )(plane, x)


def last_kernel(below_ref, x_ref, above_ref, own_ref, wide_ref, stack_ref):
    slots, per = wide_ref.shape[:2]
    count = own_ref.shape[0]
    for at in range(count):
        for unit, ref in ((at, above_ref), (count + at, own_ref)):
            wide_ref[unit // per, unit % per] = ref[at]
    for unit in range(3 * count, slots * per):
        wide_ref[unit // per, unit % per] = jnp.zeros((HALF, LANES), jnp.bfloat16)
    stack_plane(below_ref[...], stack_ref, 0)
    grad = cross(stack_ref[...], x_ref[...].reshape(-1, x_ref.shape[-1]))
    for at, unit in enumerate(units_of(grad), 2 * count):
        wide_ref[at // per, at % per] = unit.astype(jnp.bfloat16)


def wgrad_last(below, x, above_units, own_units, slots):
    per = -(-3 * own_units.shape[0] // slots)
    stack = plane_shapes(below, x.shape[0] * x.shape[1] * x.shape[2])[1]
    return pl.pallas_call(
        last_kernel,
        out_shape=[jax.ShapeDtypeStruct((slots, per, HALF, LANES), jnp.bfloat16), stack],
        compiler_params=pltpu.CompilerParams(vmem_limit_bytes=VMEM_LIMIT),
        name="wgrad_last",
    )(below, x, above_units, own_units)


def dgrad_kernel(
    core_ref, x_at_ref, z_at_ref, k_ref, above_ref, own_ref, below_ref, keep_ref, send_ref
):
    rows = keep_ref.shape[2]
    n = 9 * rows
    partial = None
    for at, stack_ref in ((0, above_ref), (n, own_ref), (2 * n, below_ref)):
        term = lax.dot_general(
            k_ref[at : at + n, :],
            stack_ref[...],
            (((0,), (0,)), ((), ())),
            preferred_element_type=jnp.float32,
        )
        partial = term if partial is None else partial + term
    first = core_ref[0] == 0
    for x_at in range(4):
        for z_at in range(3):
            x_slot = x_at ^ x_at_ref[0]
            z_slot = lax.rem(z_at - z_at_ref[0] + 3, 3)
            at = (x_at * 3 + z_at) * 2 * rows
            even, odd = partial[at : at + rows], partial[at + rows : at + 2 * rows]
            keep_ref[x_slot, z_slot] = jnp.where(first, even, odd)
            send_ref[x_slot, z_slot] = jnp.where(first, odd, even).astype(jnp.bfloat16)


def dgrad(core, x_at, z_at, k_rows, above, own, below):
    shape = (4, 3, k_rows.shape[0] // TAPS, own.shape[1])
    return pl.pallas_call(
        dgrad_kernel,
        out_shape=[
            jax.ShapeDtypeStruct(shape, jnp.float32),
            jax.ShapeDtypeStruct(shape, jnp.bfloat16),
        ],
        in_specs=specs(3, 4),
        compiler_params=pltpu.CompilerParams(vmem_limit_bytes=VMEM_LIMIT),
        name="dgrad",
    )(core, x_at, z_at, k_rows, above, own, below)


def act_kernel(mid_ref, low_ref, high_ref, cot_ref, act_ref, grad_ref):
    preact = mid_ref[...] + low_ref[...].astype(jnp.float32) + high_ref[...].astype(jnp.float32)
    sig = jax.nn.sigmoid(preact)
    act_ref[...] = (preact * sig).astype(jnp.bfloat16)
    cot = cot_ref[...].astype(jnp.float32)
    grad_ref[...] = (cot * sig * (1.0 + preact * (1.0 - sig))).astype(jnp.bfloat16)


def activate(mid, low, high, cot):
    shape = jax.ShapeDtypeStruct(mid.shape, jnp.bfloat16)
    return pl.pallas_call(
        act_kernel,
        out_shape=[shape, shape],
        compiler_params=pltpu.CompilerParams(vmem_limit_bytes=VMEM_LIMIT),
        name="activate",
    )(mid, low, high, cot)


def total_kernel(terms_ref, out_ref, *, scale):
    total = jnp.sum(terms_ref[...].astype(jnp.float32), axis=0) * scale
    out_ref[...] = jnp.broadcast_to(total.astype(jnp.bfloat16)[None], out_ref.shape)


def total_spread(terms, scale, copies):
    return pl.pallas_call(
        functools.partial(total_kernel, scale=scale),
        out_shape=jax.ShapeDtypeStruct((copies,) + terms.shape[1:], jnp.bfloat16),
        compiler_params=pltpu.CompilerParams(vmem_limit_bytes=VMEM_LIMIT),
        name="total",
    )(terms)


def halve_kernel(kept_ref, came_ref, keep_ref, send_ref):
    for at in range(keep_ref.shape[0]):
        keep_ref[at] = kept_ref[2 * at] + came_ref[2 * at].astype(jnp.float32)
        total = kept_ref[2 * at + 1] + came_ref[2 * at + 1].astype(jnp.float32)
        send_ref[at] = total.astype(jnp.bfloat16)


def halve(kept, came):
    shape = (kept.shape[0] // 2,) + kept.shape[1:]
    return pl.pallas_call(
        halve_kernel,
        out_shape=[
            jax.ShapeDtypeStruct(shape, jnp.float32),
            jax.ShapeDtypeStruct(shape, jnp.bfloat16),
        ],
        compiler_params=pltpu.CompilerParams(vmem_limit_bytes=VMEM_LIMIT),
        name="halve",
    )(kept, came)


def unpack_kernel(units_ref, out_ref):
    taps, rows, chans = out_ref.shape
    columns = chans // LANES
    for at in range(units_ref.shape[0]):
        row, column = divmod(at, columns)
        tap, half = divmod(row, rows // HALF)
        block = units_ref[at].astype(jnp.float32)
        out_ref[
            tap, half * HALF : (half + 1) * HALF, column * LANES : (column + 1) * LANES
        ] = block


def unpack(units, rows, chans):
    count = 9 * rows * chans // (HALF * LANES)
    return pl.pallas_call(
        unpack_kernel,
        grid=(3,),
        in_specs=[pl.BlockSpec((count, HALF, LANES), lambda i: (i, 0, 0))],
        out_specs=pl.BlockSpec((9, rows, chans), lambda i: (i, 0, 0)),
        out_shape=jax.ShapeDtypeStruct((TAPS, rows, chans), jnp.float32),
        compiler_params=pltpu.CompilerParams(vmem_limit_bytes=VMEM_LIMIT),
        name="unpack",
    )(units.reshape(-1, HALF, LANES))


def swap_cores(blocks):
    return lax.ppermute(blocks, "core", [(0, 1), (1, 0)])


def body(volume, kernel, cotangent):
    rows = volume.shape[2]
    cells = volume.shape[3]
    chips = lax.axis_size(CHIPS)
    depths = lax.axis_size(DEP)

    def shift(block, step):
        return lax.ppermute(block, DEP, [(i, (i + step) % depths) for i in range(depths)])

    def index(name):
        return lax.axis_index(name).astype(jnp.int32).reshape(1)

    core, x_at, z_at = index("core"), index("x"), index("zl")
    own = volume.reshape(rows, cells)
    cot = cotangent.reshape(rows, cells)

    def copies(block):
        return jnp.broadcast_to(block[None], (chips, rows, cells))

    mine = lax.all_to_all(copies(own), CHIPS, 0, 0)
    k_rows = jnp.transpose(kernel.reshape(rows, TAPS, -1), (1, 0, 2)).reshape(TAPS * rows, -1)
    mine, k_rows, cot, core, x_at, z_at = lax.optimization_barrier(
        (mine, k_rows, cot, core, x_at, z_at)
    )
    other = swap_cores(mine)

    up, mid, down = conv(core, k_rows, mine, other)
    activated, grad_pre = activate(mid, shift(up, 1), shift(down, -1), cot)

    above, below = shift(grad_pre, -1), shift(grad_pre, 1)
    own_units, own_stack, x = wgrad_own(core, grad_pre, mine, other)
    ys, zs = lax.axis_size("y"), lax.axis_size("zh")
    above_units, above_stack = wgrad_first(above, x)
    wide, below_stack = wgrad_last(below, x, above_units, own_units, ys)
    scale = 1.0 / math.sqrt(UNIV * DEPTH * SIDE * SIDE)
    over_y = lax.all_to_all(wide, "y", 0, 0)

    keep, send = dgrad(core, x_at, z_at, k_rows, above_stack, own_stack, below_stack)
    keep, send = halve(keep, swap_cores(send))
    over_y, keep = lax.optimization_barrier((over_y, keep))
    over_z = lax.all_to_all(total_spread(over_y, 1.0, zs), "zh", 0, 0)
    total = keep + lax.ppermute(send, "x", [(i, i ^ 1) for i in range(4)]).astype(jnp.float32)
    after, before = total[:, 1].astype(jnp.bfloat16), total[:, 2].astype(jnp.bfloat16)
    over_z, _ = lax.optimization_barrier((over_z, (after, before)))
    after = lax.ppermute(after, "zl", [(i, (i + 1) % 3) for i in range(3)])
    before = lax.ppermute(before, "zl", [(i, (i + 2) % 3) for i in range(3)])
    units = lax.all_to_all(total_spread(over_z, scale, ys), "y", 0, 0)
    total = total[:, 0] + after.astype(jnp.float32) + before.astype(jnp.float32)
    step = lax.ppermute(total[1].astype(jnp.bfloat16), "x", [(i, i ^ 2) for i in range(4)])
    grad_volume = (total[0] + step.astype(jnp.float32)).astype(jnp.bfloat16)
    all_taps = unpack(units, rows, kernel.shape[-1])
    grad_kernel = jnp.transpose(all_taps, (1, 0, 2)).reshape(kernel.shape)
    return (activated.reshape(volume.shape), grad_volume.reshape(volume.shape), grad_kernel)


def solution(mesh):
    fine = Mesh(mesh.devices.reshape(8, 4, 4, 3, 2), ("y", "zh", "x", "zl", "core"))
    field = P(None, DEP, CHAN, None)
    weight = P(CHAN, None, None, None, None)
    return jax.shard_map(
        body,
        mesh=fine,
        in_specs=(field, weight, field),
        out_specs=(field, field, weight),
        check_vma=False,
    )
```

```python
import functools
import math

import jax
import jax.numpy as jnp
from jax import lax
from jax.experimental import pallas as pl
from jax.experimental.pallas import tpu as pltpu
from jax.sharding import Mesh
from jax.sharding import PartitionSpec as P

DEPTH = 32
SIDE = 32
UNIV = 1
TAPS = 27
LANES = 128
HALF = 8
VMEM_LIMIT = 48 * 1024 * 1024
DEP = ("y", "zh")
CHIPS = ("x", "zl")
CHAN = ("x", "zl", "core")


def shift_cells(plane, row_step, col_step):
    cells = plane.shape[-1]
    if col_step:
        columns = lax.broadcasted_iota(jnp.int32, plane.shape, 1) % SIDE
        edge = 0 if col_step > 0 else SIDE - 1
        plain = pltpu.roll(plane, col_step % cells, 1)
        wrapped = pltpu.roll(plane, (col_step - col_step * SIDE) % cells, 1)
        plane = jnp.where(columns == edge, wrapped, plain)
    if row_step:
        plane = pltpu.roll(plane, (row_step * SIDE) % cells, 1)
    return plane


def merge_cores(core_ref, mine_ref, other_ref, x_ref):
    first = core_ref[0] == 0
    mine, other = mine_ref[...], other_ref[...]
    x_ref[:, 0] = jnp.where(first, mine, other)
    x_ref[:, 1] = jnp.where(first, other, mine)
    return x_ref[...].reshape(-1, x_ref.shape[-1])


def conv_kernel(core_ref, w_ref, mine_ref, other_ref, *refs):
    outs, x_ref = refs[:3], refs[3]
    rows = outs[0].shape[0]
    x = merge_cores(core_ref, mine_ref, other_ref, x_ref)
    for depth_tap in range(3):
        w = w_ref[depth_tap * 9 * rows : (depth_tap + 1) * 9 * rows, :]
        product = jnp.dot(w, x, preferred_element_type=jnp.float32)
        total = None
        for col_tap in range(3):
            part = None
            for row_tap in range(3):
                at = (row_tap * 3 + col_tap) * rows
                term = shift_cells(product[at : at + rows], 1 - row_tap, 0)
                part = term if part is None else part + term
            part = shift_cells(part, 0, 1 - col_tap)
            total = part if total is None else total + part
        outs[depth_tap][...] = total.astype(outs[depth_tap].dtype)


def specs(scalars, arrays):
    smem = pl.BlockSpec(memory_space=pltpu.SMEM)
    return [smem] * scalars + [pl.BlockSpec(memory_space=pltpu.VMEM)] * arrays


def merged_scratch(mine):
    return [pltpu.VMEM((mine.shape[0], 2) + mine.shape[1:], mine.dtype)]


def conv(core, weights, mine, other):
    rows = weights.shape[0] // TAPS
    cells = mine.shape[-1]
    return pl.pallas_call(
        conv_kernel,
        out_shape=[
            jax.ShapeDtypeStruct((rows, cells), kind)
            for kind in (jnp.bfloat16, jnp.float32, jnp.bfloat16)
        ],
        in_specs=specs(1, 3),
        scratch_shapes=merged_scratch(mine),
        compiler_params=pltpu.CompilerParams(vmem_limit_bytes=VMEM_LIMIT),
        name="conv",
    )(core, weights, mine, other)


def stack_plane(plane, stack_ref, at):
    rows = plane.shape[0]
    plane = plane.astype(jnp.float32)
    moved = [shift_cells(plane, 0, col_tap - 1) for col_tap in range(3)]
    for row_tap in range(3):
        for col_tap in range(3):
            stack_ref[at : at + rows, :] = shift_cells(moved[col_tap], row_tap - 1, 0).astype(
                jnp.bfloat16
            )
            at += rows


def cross(stack, x):
    return lax.dot_general(
        stack, x, (((1,), (1,)), ((), ())), preferred_element_type=jnp.float32
    )


def units_of(grad):
    columns = grad.shape[1] // LANES
    for at in range(grad.shape[0] // HALF * columns):
        row, column = divmod(at, columns)
        yield grad[row * HALF : (row + 1) * HALF, column * LANES : (column + 1) * LANES]


def own_kernel(core_ref, own_ref, mine_ref, other_ref, units_ref, stack_ref, x_ref):
    x = merge_cores(core_ref, mine_ref, other_ref, x_ref)
    stack_plane(own_ref[...], stack_ref, 0)
    for at, unit in enumerate(units_of(cross(stack_ref[...], x))):
        units_ref[at] = unit.astype(jnp.bfloat16)


def plane_shapes(own, chans):
    rows, cells = own.shape
    return [
        jax.ShapeDtypeStruct((9 * rows * chans // (HALF * LANES), HALF, LANES), jnp.bfloat16),
        jax.ShapeDtypeStruct((9 * rows, cells), jnp.bfloat16),
    ]


def wgrad_own(core, own, mine, other):
    chans = 2 * mine.shape[0] * mine.shape[1]
    x = jax.ShapeDtypeStruct((mine.shape[0], 2) + mine.shape[1:], mine.dtype)
    return pl.pallas_call(
        own_kernel,
        out_shape=plane_shapes(own, chans) + [x],
        in_specs=specs(1, 3),
        compiler_params=pltpu.CompilerParams(vmem_limit_bytes=VMEM_LIMIT),
        name="wgrad_own",
    )(core, own, mine, other)


def below_kernel(below_ref, x_ref, units_ref, stack_ref):
    stack_plane(below_ref[...], stack_ref, 0)
    grad = cross(stack_ref[...], x_ref[...].reshape(-1, x_ref.shape[-1]))
    for at, unit in enumerate(units_of(grad)):
        units_ref[at] = unit.astype(jnp.bfloat16)


def wgrad_below(below, x):
    return pl.pallas_call(
        below_kernel,
        out_shape=plane_shapes(below, x.shape[0] * x.shape[1] * x.shape[2]),
        compiler_params=pltpu.CompilerParams(vmem_limit_bytes=VMEM_LIMIT),
        name="wgrad_below",
    )(below, x)


def above_kernel(above_ref, x_ref, own_ref, below_ref, wide_ref, stack_ref):
    slots, per = wide_ref.shape[:2]
    count = own_ref.shape[0]
    for at in range(count):
        for unit, ref in ((count + at, own_ref), (2 * count + at, below_ref)):
            wide_ref[unit // per, unit % per] = ref[at]
    for unit in range(3 * count, slots * per):
        wide_ref[unit // per, unit % per] = jnp.zeros((HALF, LANES), jnp.bfloat16)
    stack_plane(above_ref[...], stack_ref, 0)
    grad = cross(stack_ref[...], x_ref[...].reshape(-1, x_ref.shape[-1]))
    for at, unit in enumerate(units_of(grad)):
        wide_ref[at // per, at % per] = unit.astype(jnp.bfloat16)


def wgrad_above(above, x, own_units, below_units, slots):
    per = -(-3 * own_units.shape[0] // slots)
    stack = plane_shapes(above, x.shape[0] * x.shape[1] * x.shape[2])[1]
    return pl.pallas_call(
        above_kernel,
        out_shape=[jax.ShapeDtypeStruct((slots, per, HALF, LANES), jnp.bfloat16), stack],
        compiler_params=pltpu.CompilerParams(vmem_limit_bytes=VMEM_LIMIT),
        name="wgrad_above",
    )(above, x, own_units, below_units)


def dgrad_kernel(
    core_ref, x_at_ref, z_at_ref, k_ref, above_ref, own_ref, below_ref, keep_ref, send_ref
):
    rows = keep_ref.shape[2]
    n = 9 * rows
    partial = None
    for at, stack_ref in ((0, above_ref), (n, own_ref), (2 * n, below_ref)):
        term = lax.dot_general(
            k_ref[at : at + n, :],
            stack_ref[...],
            (((0,), (0,)), ((), ())),
            preferred_element_type=jnp.float32,
        )
        partial = term if partial is None else partial + term
    first = core_ref[0] == 0
    for x_at in range(4):
        for z_at in range(3):
            x_slot = x_at ^ x_at_ref[0]
            z_slot = lax.rem(z_at - z_at_ref[0] + 3, 3)
            at = (x_at * 3 + z_at) * 2 * rows
            even, odd = partial[at : at + rows], partial[at + rows : at + 2 * rows]
            keep_ref[x_slot, z_slot] = jnp.where(first, even, odd)
            send_ref[x_slot, z_slot] = jnp.where(first, odd, even).astype(jnp.bfloat16)


def dgrad(core, x_at, z_at, k_rows, above, own, below):
    shape = (4, 3, k_rows.shape[0] // TAPS, own.shape[1])
    return pl.pallas_call(
        dgrad_kernel,
        out_shape=[
            jax.ShapeDtypeStruct(shape, jnp.float32),
            jax.ShapeDtypeStruct(shape, jnp.bfloat16),
        ],
        in_specs=specs(3, 4),
        compiler_params=pltpu.CompilerParams(vmem_limit_bytes=VMEM_LIMIT),
        name="dgrad",
    )(core, x_at, z_at, k_rows, above, own, below)


def act_kernel(mid_ref, low_ref, high_ref, cot_ref, act_ref, grad_ref):
    preact = mid_ref[...] + low_ref[...].astype(jnp.float32) + high_ref[...].astype(jnp.float32)
    sig = jax.nn.sigmoid(preact)
    act_ref[...] = (preact * sig).astype(jnp.bfloat16)
    cot = cot_ref[...].astype(jnp.float32)
    grad_ref[...] = (cot * sig * (1.0 + preact * (1.0 - sig))).astype(jnp.bfloat16)


def activate(mid, low, high, cot):
    shape = jax.ShapeDtypeStruct(mid.shape, jnp.bfloat16)
    return pl.pallas_call(
        act_kernel,
        out_shape=[shape, shape],
        compiler_params=pltpu.CompilerParams(vmem_limit_bytes=VMEM_LIMIT),
        name="activate",
    )(mid, low, high, cot)


def total_kernel(terms_ref, out_ref, *, scale):
    total = jnp.sum(terms_ref[...].astype(jnp.float32), axis=0) * scale
    out_ref[...] = jnp.broadcast_to(total.astype(jnp.bfloat16)[None], out_ref.shape)


def total_spread(terms, scale, copies):
    return pl.pallas_call(
        functools.partial(total_kernel, scale=scale),
        out_shape=jax.ShapeDtypeStruct((copies,) + terms.shape[1:], jnp.bfloat16),
        compiler_params=pltpu.CompilerParams(vmem_limit_bytes=VMEM_LIMIT),
        name="total",
    )(terms)


def halve_kernel(kept_ref, came_ref, keep_ref, send_ref):
    for at in range(keep_ref.shape[0]):
        keep_ref[at] = kept_ref[2 * at] + came_ref[2 * at].astype(jnp.float32)
        total = kept_ref[2 * at + 1] + came_ref[2 * at + 1].astype(jnp.float32)
        send_ref[at] = total.astype(jnp.bfloat16)


def halve(kept, came):
    shape = (kept.shape[0] // 2,) + kept.shape[1:]
    return pl.pallas_call(
        halve_kernel,
        out_shape=[
            jax.ShapeDtypeStruct(shape, jnp.float32),
            jax.ShapeDtypeStruct(shape, jnp.bfloat16),
        ],
        compiler_params=pltpu.CompilerParams(vmem_limit_bytes=VMEM_LIMIT),
        name="halve",
    )(kept, came)


def unpack_kernel(units_ref, out_ref):
    taps, rows, chans = out_ref.shape
    per = units_ref.shape[1]
    columns = chans // LANES
    for at in range(taps * rows // HALF * columns):
        row, column = divmod(at, columns)
        tap, half = divmod(row, rows // HALF)
        block = units_ref[at // per, at % per].astype(jnp.float32)
        out_ref[
            tap, half * HALF : (half + 1) * HALF, column * LANES : (column + 1) * LANES
        ] = block


def unpack(units, rows, chans):
    return pl.pallas_call(
        unpack_kernel,
        out_shape=jax.ShapeDtypeStruct((TAPS, rows, chans), jnp.float32),
        compiler_params=pltpu.CompilerParams(vmem_limit_bytes=VMEM_LIMIT),
        name="unpack",
    )(units)


def swap_cores(blocks):
    return lax.ppermute(blocks, "core", [(0, 1), (1, 0)])


def body(volume, kernel, cotangent):
    rows = volume.shape[2]
    cells = volume.shape[3]
    chips = lax.axis_size(CHIPS)
    depths = lax.axis_size(DEP)

    def shift(block, step):
        return lax.ppermute(block, DEP, [(i, (i + step) % depths) for i in range(depths)])

    def index(name):
        return lax.axis_index(name).astype(jnp.int32).reshape(1)

    core, x_at, z_at = index("core"), index("x"), index("zl")
    own = volume.reshape(rows, cells)
    cot = cotangent.reshape(rows, cells)

    def copies(block):
        return jnp.broadcast_to(block[None], (chips, rows, cells))

    mine = lax.all_to_all(copies(own), CHIPS, 0, 0)
    k_rows = jnp.transpose(kernel.reshape(rows, TAPS, -1), (1, 0, 2)).reshape(TAPS * rows, -1)
    mine, k_rows, cot, core, x_at, z_at = lax.optimization_barrier(
        (mine, k_rows, cot, core, x_at, z_at)
    )
    other = swap_cores(mine)

    up, mid, down = conv(core, k_rows, mine, other)
    activated, grad_pre = activate(mid, shift(up, 1), shift(down, -1), cot)

    above, below = shift(grad_pre, -1), shift(grad_pre, 1)
    own_units, own_stack, x = wgrad_own(core, grad_pre, mine, other)
    ys, zs = lax.axis_size("y"), lax.axis_size("zh")
    below_units, below_stack = wgrad_below(below, x)
    wide, above_stack = wgrad_above(above, x, own_units, below_units, ys)
    scale = 1.0 / math.sqrt(UNIV * DEPTH * SIDE * SIDE)
    over_y = lax.all_to_all(wide, "y", 0, 0)

    keep, send = dgrad(core, x_at, z_at, k_rows, above_stack, own_stack, below_stack)
    keep, send = halve(keep, swap_cores(send))
    over_y, keep = lax.optimization_barrier((over_y, keep))
    over_z = lax.all_to_all(total_spread(over_y, 1.0, zs), "zh", 0, 0)
    total = keep + lax.ppermute(send, "x", [(i, i ^ 1) for i in range(4)]).astype(jnp.float32)
    over_z, _ = lax.optimization_barrier((over_z, total))
    units = lax.all_to_all(total_spread(over_z, scale, ys), "y", 0, 0)
    step = lax.ppermute(total[1].astype(jnp.bfloat16), "x", [(i, i ^ 2) for i in range(4)])
    total = total[0] + step.astype(jnp.float32)
    after, before = total[1].astype(jnp.bfloat16), total[2].astype(jnp.bfloat16)
    after = lax.ppermute(after, "zl", [(i, (i + 1) % 3) for i in range(3)])
    before = lax.ppermute(before, "zl", [(i, (i + 2) % 3) for i in range(3)])
    grad_volume = total[0] + after.astype(jnp.float32) + before.astype(jnp.float32)
    grad_volume = grad_volume.astype(jnp.bfloat16)
    all_taps = unpack(units, rows, kernel.shape[-1])
    grad_kernel = jnp.transpose(all_taps, (1, 0, 2)).reshape(kernel.shape)
    return (activated.reshape(volume.shape), grad_volume.reshape(volume.shape), grad_kernel)


def solution(mesh):
    fine = Mesh(mesh.devices.reshape(8, 4, 4, 3, 2), ("y", "zh", "x", "zl", "core"))
    field = P(None, DEP, CHAN, None)
    weight = P(CHAN, None, None, None, None)
    return jax.shard_map(
        body,
        mesh=fine,
        in_specs=(field, weight, field),
        out_specs=(field, field, weight),
        check_vma=False,
    )
```

```python
import functools
import math

import jax
import jax.numpy as jnp
from jax import lax
from jax.experimental import pallas as pl
from jax.experimental.pallas import tpu as pltpu
from jax.sharding import Mesh
from jax.sharding import PartitionSpec as P

DEPTH = 32
SIDE = 32
UNIV = 1
TAPS = 27
LANES = 128
HALF = 8
VMEM_LIMIT = 48 * 1024 * 1024
DEP = ("y", "zh")
CHIPS = ("x", "zl")
CHAN = ("x", "zl", "core")


def shift_cells(plane, row_step, col_step):
    cells = plane.shape[-1]
    if col_step:
        columns = lax.broadcasted_iota(jnp.int32, plane.shape, 1) % SIDE
        edge = 0 if col_step > 0 else SIDE - 1
        plain = pltpu.roll(plane, col_step % cells, 1)
        wrapped = pltpu.roll(plane, (col_step - col_step * SIDE) % cells, 1)
        plane = jnp.where(columns == edge, wrapped, plain)
    if row_step:
        plane = pltpu.roll(plane, (row_step * SIDE) % cells, 1)
    return plane


def merge_cores(core_ref, mine_ref, other_ref, x_ref):
    first = core_ref[0] == 0
    mine, other = mine_ref[...], other_ref[...]
    x_ref[:, 0] = jnp.where(first, mine, other)
    x_ref[:, 1] = jnp.where(first, other, mine)
    return x_ref[...].reshape(-1, x_ref.shape[-1])


def conv_kernel(core_ref, w_ref, mine_ref, other_ref, *refs):
    outs, x_ref = refs[:3], refs[3]
    rows = outs[0].shape[0]
    x = merge_cores(core_ref, mine_ref, other_ref, x_ref)
    for depth_tap in range(3):
        w = w_ref[depth_tap * 9 * rows : (depth_tap + 1) * 9 * rows, :]
        product = jnp.dot(w, x, preferred_element_type=jnp.float32)
        total = None
        for col_tap in range(3):
            part = None
            for row_tap in range(3):
                at = (row_tap * 3 + col_tap) * rows
                term = shift_cells(product[at : at + rows], 1 - row_tap, 0)
                part = term if part is None else part + term
            part = shift_cells(part, 0, 1 - col_tap)
            total = part if total is None else total + part
        outs[depth_tap][...] = total.astype(outs[depth_tap].dtype)


def specs(scalars, arrays):
    smem = pl.BlockSpec(memory_space=pltpu.SMEM)
    return [smem] * scalars + [pl.BlockSpec(memory_space=pltpu.VMEM)] * arrays


def merged_scratch(mine):
    return [pltpu.VMEM((mine.shape[0], 2) + mine.shape[1:], mine.dtype)]


def conv(core, weights, mine, other):
    rows = weights.shape[0] // TAPS
    cells = mine.shape[-1]
    return pl.pallas_call(
        conv_kernel,
        out_shape=[
            jax.ShapeDtypeStruct((rows, cells), kind)
            for kind in (jnp.bfloat16, jnp.float32, jnp.bfloat16)
        ],
        in_specs=specs(1, 3),
        scratch_shapes=merged_scratch(mine),
        compiler_params=pltpu.CompilerParams(vmem_limit_bytes=VMEM_LIMIT),
        name="conv",
    )(core, weights, mine, other)


def stack_plane(plane, stack_ref, at):
    rows = plane.shape[0]
    plane = plane.astype(jnp.float32)
    moved = [shift_cells(plane, 0, col_tap - 1) for col_tap in range(3)]
    for row_tap in range(3):
        for col_tap in range(3):
            stack_ref[at : at + rows, :] = shift_cells(moved[col_tap], row_tap - 1, 0).astype(
                jnp.bfloat16
            )
            at += rows


def cross(stack, x):
    return lax.dot_general(
        stack, x, (((1,), (1,)), ((), ())), preferred_element_type=jnp.float32
    )


def units_of(grad):
    columns = grad.shape[1] // LANES
    for at in range(grad.shape[0] // HALF * columns):
        row, column = divmod(at, columns)
        yield grad[row * HALF : (row + 1) * HALF, column * LANES : (column + 1) * LANES]


def own_kernel(core_ref, own_ref, mine_ref, other_ref, units_ref, stack_ref, x_ref):
    x = merge_cores(core_ref, mine_ref, other_ref, x_ref)
    stack_plane(own_ref[...], stack_ref, 0)
    for at, unit in enumerate(units_of(cross(stack_ref[...], x))):
        units_ref[at] = unit.astype(jnp.bfloat16)


def plane_shapes(own, chans):
    rows, cells = own.shape
    return [
        jax.ShapeDtypeStruct((9 * rows * chans // (HALF * LANES), HALF, LANES), jnp.bfloat16),
        jax.ShapeDtypeStruct((9 * rows, cells), jnp.bfloat16),
    ]


def wgrad_own(core, own, mine, other):
    chans = 2 * mine.shape[0] * mine.shape[1]
    x = jax.ShapeDtypeStruct((mine.shape[0], 2) + mine.shape[1:], mine.dtype)
    return pl.pallas_call(
        own_kernel,
        out_shape=plane_shapes(own, chans) + [x],
        in_specs=specs(1, 3),
        compiler_params=pltpu.CompilerParams(vmem_limit_bytes=VMEM_LIMIT),
        name="wgrad_own",
    )(core, own, mine, other)


def below_kernel(below_ref, x_ref, units_ref, stack_ref):
    stack_plane(below_ref[...], stack_ref, 0)
    grad = cross(stack_ref[...], x_ref[...].reshape(-1, x_ref.shape[-1]))
    for at, unit in enumerate(units_of(grad)):
        units_ref[at] = unit.astype(jnp.bfloat16)


def wgrad_below(below, x):
    return pl.pallas_call(
        below_kernel,
        out_shape=plane_shapes(below, x.shape[0] * x.shape[1] * x.shape[2]),
        compiler_params=pltpu.CompilerParams(vmem_limit_bytes=VMEM_LIMIT),
        name="wgrad_below",
    )(below, x)


def above_kernel(
    above_ref, x_ref, own_ref, below_ref, wide_ref, stack_ref, units_ref, pad_ref, sems
):
    count = own_ref.shape[0]
    pad_ref[...] = jnp.zeros_like(pad_ref)
    moves = [
        pltpu.make_async_copy(ref, wide_ref.at[pl.ds(run * count, ref.shape[0])], sems.at[run])
        for run, ref in enumerate((units_ref, own_ref, below_ref, pad_ref))
    ]
    for move in moves[1:]:
        move.start()
    stack_plane(above_ref[...], stack_ref, 0)
    grad = cross(stack_ref[...], x_ref[...].reshape(-1, x_ref.shape[-1]))
    for at, unit in enumerate(units_of(grad)):
        units_ref[at] = unit.astype(jnp.bfloat16)
    moves[0].start()
    for move in moves:
        move.wait()


def wgrad_above(above, x, own_units, below_units, slots):
    count = own_units.shape[0]
    full = -(-3 * count // slots) * slots
    stack = plane_shapes(above, x.shape[0] * x.shape[1] * x.shape[2])[1]
    return pl.pallas_call(
        above_kernel,
        out_shape=[jax.ShapeDtypeStruct((full, HALF, LANES), jnp.bfloat16), stack],
        out_specs=[pl.BlockSpec(memory_space=pl.ANY), pl.BlockSpec(memory_space=pltpu.VMEM)],
        scratch_shapes=[
            pltpu.VMEM((count, HALF, LANES), jnp.bfloat16),
            pltpu.VMEM((full - 3 * count, HALF, LANES), jnp.bfloat16),
            pltpu.SemaphoreType.DMA((4,)),
        ],
        compiler_params=pltpu.CompilerParams(vmem_limit_bytes=VMEM_LIMIT),
        name="wgrad_above",
    )(above, x, own_units, below_units)


def dgrad_kernel(
    core_ref, x_at_ref, z_at_ref, k_ref, above_ref, own_ref, below_ref, keep_ref, send_ref
):
    rows = keep_ref.shape[2]
    n = 9 * rows
    partial = None
    for at, stack_ref in ((0, above_ref), (n, own_ref), (2 * n, below_ref)):
        term = lax.dot_general(
            k_ref[at : at + n, :],
            stack_ref[...],
            (((0,), (0,)), ((), ())),
            preferred_element_type=jnp.float32,
        )
        partial = term if partial is None else partial + term
    first = core_ref[0] == 0
    for x_at in range(4):
        for z_at in range(3):
            x_slot = x_at ^ x_at_ref[0]
            z_slot = lax.rem(z_at - z_at_ref[0] + 3, 3)
            at = (x_at * 3 + z_at) * 2 * rows
            even, odd = partial[at : at + rows], partial[at + rows : at + 2 * rows]
            keep_ref[x_slot, z_slot] = jnp.where(first, even, odd)
            send_ref[x_slot, z_slot] = jnp.where(first, odd, even).astype(jnp.bfloat16)


def dgrad(core, x_at, z_at, k_rows, above, own, below):
    shape = (4, 3, k_rows.shape[0] // TAPS, own.shape[1])
    return pl.pallas_call(
        dgrad_kernel,
        out_shape=[
            jax.ShapeDtypeStruct(shape, jnp.float32),
            jax.ShapeDtypeStruct(shape, jnp.bfloat16),
        ],
        in_specs=specs(3, 4),
        compiler_params=pltpu.CompilerParams(vmem_limit_bytes=VMEM_LIMIT),
        name="dgrad",
    )(core, x_at, z_at, k_rows, above, own, below)


def act_kernel(mid_ref, low_ref, high_ref, cot_ref, act_ref, grad_ref):
    preact = mid_ref[...] + low_ref[...].astype(jnp.float32) + high_ref[...].astype(jnp.float32)
    sig = jax.nn.sigmoid(preact)
    act_ref[...] = (preact * sig).astype(jnp.bfloat16)
    cot = cot_ref[...].astype(jnp.float32)
    grad_ref[...] = (cot * sig * (1.0 + preact * (1.0 - sig))).astype(jnp.bfloat16)


def activate(mid, low, high, cot):
    shape = jax.ShapeDtypeStruct(mid.shape, jnp.bfloat16)
    return pl.pallas_call(
        act_kernel,
        out_shape=[shape, shape],
        compiler_params=pltpu.CompilerParams(vmem_limit_bytes=VMEM_LIMIT),
        name="activate",
    )(mid, low, high, cot)


def total_kernel(terms_ref, out_ref, *, scale):
    total = jnp.sum(terms_ref[...].astype(jnp.float32), axis=0) * scale
    out_ref[...] = jnp.broadcast_to(total.astype(jnp.bfloat16)[None], out_ref.shape)


def total_spread(terms, scale, copies):
    return pl.pallas_call(
        functools.partial(total_kernel, scale=scale),
        out_shape=jax.ShapeDtypeStruct((copies,) + terms.shape[1:], jnp.bfloat16),
        compiler_params=pltpu.CompilerParams(vmem_limit_bytes=VMEM_LIMIT),
        name="total",
    )(terms)


def halve_kernel(kept_ref, came_ref, keep_ref, send_ref):
    for at in range(keep_ref.shape[0]):
        keep_ref[at] = kept_ref[2 * at] + came_ref[2 * at].astype(jnp.float32)
        total = kept_ref[2 * at + 1] + came_ref[2 * at + 1].astype(jnp.float32)
        send_ref[at] = total.astype(jnp.bfloat16)


def halve(kept, came):
    shape = (kept.shape[0] // 2,) + kept.shape[1:]
    return pl.pallas_call(
        halve_kernel,
        out_shape=[
            jax.ShapeDtypeStruct(shape, jnp.float32),
            jax.ShapeDtypeStruct(shape, jnp.bfloat16),
        ],
        compiler_params=pltpu.CompilerParams(vmem_limit_bytes=VMEM_LIMIT),
        name="halve",
    )(kept, came)


def unpack_kernel(units_ref, out_ref):
    taps, rows, chans = out_ref.shape
    per = units_ref.shape[1]
    columns = chans // LANES
    for at in range(taps * rows // HALF * columns):
        row, column = divmod(at, columns)
        tap, half = divmod(row, rows // HALF)
        block = units_ref[at // per, at % per].astype(jnp.float32)
        out_ref[
            tap, half * HALF : (half + 1) * HALF, column * LANES : (column + 1) * LANES
        ] = block


def unpack(units, rows, chans):
    return pl.pallas_call(
        unpack_kernel,
        out_shape=jax.ShapeDtypeStruct((TAPS, rows, chans), jnp.float32),
        compiler_params=pltpu.CompilerParams(vmem_limit_bytes=VMEM_LIMIT),
        name="unpack",
    )(units)


def swap_cores(blocks):
    return lax.ppermute(blocks, "core", [(0, 1), (1, 0)])


def body(volume, kernel, cotangent):
    rows = volume.shape[2]
    cells = volume.shape[3]
    chips = lax.axis_size(CHIPS)
    depths = lax.axis_size(DEP)

    def shift(block, step):
        return lax.ppermute(block, DEP, [(i, (i + step) % depths) for i in range(depths)])

    def index(name):
        return lax.axis_index(name).astype(jnp.int32).reshape(1)

    core, x_at, z_at = index("core"), index("x"), index("zl")
    own = volume.reshape(rows, cells)
    cot = cotangent.reshape(rows, cells)

    def copies(block):
        return jnp.broadcast_to(block[None], (chips, rows, cells))

    mine = lax.all_to_all(copies(own), CHIPS, 0, 0)
    k_rows = jnp.transpose(kernel.reshape(rows, TAPS, -1), (1, 0, 2)).reshape(TAPS * rows, -1)
    mine, k_rows, cot, core, x_at, z_at = lax.optimization_barrier(
        (mine, k_rows, cot, core, x_at, z_at)
    )
    other = swap_cores(mine)

    up, mid, down = conv(core, k_rows, mine, other)
    activated, grad_pre = activate(mid, shift(up, 1), shift(down, -1), cot)

    above, below = shift(grad_pre, -1), shift(grad_pre, 1)
    own_units, own_stack, x = wgrad_own(core, grad_pre, mine, other)
    ys, zs = lax.axis_size("y"), lax.axis_size("zh")
    below_units, below_stack = wgrad_below(below, x)
    wide, above_stack = wgrad_above(above, x, own_units, below_units, ys)
    wide = wide.reshape((ys, -1) + wide.shape[1:])
    scale = 1.0 / math.sqrt(UNIV * DEPTH * SIDE * SIDE)
    over_y = lax.all_to_all(wide, "y", 0, 0)

    keep, send = dgrad(core, x_at, z_at, k_rows, above_stack, own_stack, below_stack)
    keep, send = halve(keep, swap_cores(send))
    over_y, keep = lax.optimization_barrier((over_y, keep))
    over_z = lax.all_to_all(total_spread(over_y, 1.0, zs), "zh", 0, 0)
    total = keep + lax.ppermute(send, "x", [(i, i ^ 1) for i in range(4)]).astype(jnp.float32)
    after, before = total[:, 1].astype(jnp.bfloat16), total[:, 2].astype(jnp.bfloat16)
    over_z, _ = lax.optimization_barrier((over_z, (after, before)))
    after = lax.ppermute(after, "zl", [(i, (i + 1) % 3) for i in range(3)])
    before = lax.ppermute(before, "zl", [(i, (i + 2) % 3) for i in range(3)])
    units = lax.all_to_all(total_spread(over_z, scale, ys), "y", 0, 0)
    total = total[:, 0] + after.astype(jnp.float32) + before.astype(jnp.float32)
    step = lax.ppermute(total[1].astype(jnp.bfloat16), "x", [(i, i ^ 2) for i in range(4)])
    grad_volume = (total[0] + step.astype(jnp.float32)).astype(jnp.bfloat16)
    all_taps = unpack(units, rows, kernel.shape[-1])
    grad_kernel = jnp.transpose(all_taps, (1, 0, 2)).reshape(kernel.shape)
    return (activated.reshape(volume.shape), grad_volume.reshape(volume.shape), grad_kernel)


def solution(mesh):
    fine = Mesh(mesh.devices.reshape(8, 4, 4, 3, 2), ("y", "zh", "x", "zl", "core"))
    field = P(None, DEP, CHAN, None)
    weight = P(CHAN, None, None, None, None)
    return jax.shard_map(
        body,
        mesh=fine,
        in_specs=(field, weight, field),
        out_specs=(field, field, weight),
        check_vma=False,
    )
```
